128 devices in a mesh: region: 4 (over y), row: 8 (over z, x_hi), col: 4 (over x_lo, core).
Axes of the slice: x: 4 (x_hi: 2, x_lo: 2; x = x_hi * 2 + x_lo), y: 4, z: 4, core: 2. Of those that a mesh axis runs over, the one named last changes fastest.
Arguments:
- noisy_field: bfloat16 [4, 1024, 512, 128], P('region', 'row', 'col'), may hold values from -40 to 40
- coarse_cells: float32 [32768, 640], P(('region', 'row', 'col')), may hold values from -6 to 6
- coarse_proj: float32 [640, 128], replicated, may hold values from -0.25 to 0.25
- kernel_first: bfloat16 [3, 3, 128, 128], replicated, may hold values from -0.1875 to 0.1875
- kernel_second: bfloat16 [3, 3, 128, 128], replicated, may hold values from -0.1875 to 0.1875
- gain_first: float32 [128], replicated, may hold values from 0.25 to 1.75
- shift_first: float32 [128], replicated, may hold values from -3 to 3
- gain_second: float32 [128], replicated, may hold values from 0.25 to 1.75
- shift_second: float32 [128], replicated, may hold values from -3 to 3
- request_ids: int32 [4, 8, 4, 128, 6], P('region', 'row', 'col'), may hold values from 0 to 32767, as said below
- patch_slots: int32 [4, 8, 4, 169], P('region', 'row', 'col'), may hold values from 0 to 767, as said below
- tile_offsets: int32 [4, 8, 4, 2], P('region', 'row', 'col'), may hold values from 0 to 127
Outputs:
- denoised: bfloat16 [4, 1024, 512, 128], P('region', 'row', 'col')
The draws below stay inside these ranges and needn't reach their ends.
Inputs may be any that keep to these rules, and one draw needn't show every extreme that they name: request_ids[r, i, j, o, m] is a cell of owner o: o * 256 <= value < (o + 1) * 256, owner o being the device of index o over region, row, col in that order. `patch_slots`: the 169 entries of one tile are distinct; in every draw one owner has all 6 of its entries used by every tile.
All inputs are finite; a program needn't handle non-finite values.
Results may differ from the reference program's by a relative error of at most 0.0051.
Values may be sent and summed in bfloat16 or wider, within the bound.
A program may use at most 64 MiB of HBM per device.

```python
import jax
import jax.numpy as jnp
from jax import lax

C = 128
GROUPS = 32
CC = 640
TILE = 128
GT_DEV = 256
MOST = 6
STEP = 9
PATCH = 13
NEED = 169
REGIONS = 4
ROW_TILES = 8
COL_TILES = 4
NY = 1024
NX = 512
GCELLS = 32768
DEVICES = 128


def slot_tables(key):
    hot_owner = jax.random.randint(jax.random.fold_in(key, 7), (), 0, DEVICES)

    def one_device(device_index):
        device_key = jax.random.fold_in(key, device_index)
        subkeys = jax.random.split(device_key, 4)
        hotness = jax.random.randint(subkeys[0], (DEVICES, 1), 1, 5)
        slot_depth = jnp.arange(MOST, dtype=jnp.int32)[None, :]
        order_noise = jax.random.permutation(subkeys[1], DEVICES * MOST).astype(jnp.int32).reshape(DEVICES, MOST)
        owner_ids = jnp.arange(DEVICES, dtype=jnp.int32)[:, None]
        scores = slot_depth * hotness * (DEVICES * MOST) + order_noise
        scores = jnp.where(owner_ids == hot_owner, slot_depth - MOST, scores)
        ranked = jnp.argsort(scores.reshape(-1), stable=True).astype(jnp.int32)
        chosen = ranked[:NEED]
        shuffled = chosen[jax.random.permutation(subkeys[2], NEED)]
        local_rows = jax.random.randint(subkeys[3], (DEVICES, MOST), 0, GT_DEV)
        requests = owner_ids * GT_DEV + local_rows
        return (requests.astype(jnp.int32), shuffled.astype(jnp.int32))
    all_requests, all_slots = jax.vmap(one_device)(jnp.arange(DEVICES, dtype=jnp.int32))
    return (all_requests.reshape(REGIONS, ROW_TILES, COL_TILES, DEVICES, MOST), all_slots.reshape(REGIONS, ROW_TILES, COL_TILES, NEED))


def draw_request_ids(key, part):
    return slot_tables(key)[0]


def draw_patch_slots(key, part):
    return slot_tables(key)[1]


def draw_noisy_field(key, part):
    subkeys = jax.random.split(jax.random.fold_in(key, 11), 4)
    row_frac = jnp.arange(NY, dtype=jnp.float32) / NY
    row_scale = 0.3 * jnp.power(3.0, row_frac)[None, :, None, None] * jnp.exp(jax.random.uniform(subkeys[0], (REGIONS, NY, 1, 1), minval=0.0, maxval=jnp.log(2.0)))
    col_scale = jnp.exp(jax.random.uniform(subkeys[1], (REGIONS, 1, NX, 1), minval=0.0, maxval=jnp.log(3.3)))
    chan_scale = jnp.exp(jax.random.uniform(subkeys[2], (REGIONS, 1, 1, C), minval=-0.4, maxval=0.4))
    base_noise = jnp.clip(jax.random.normal(subkeys[3], (REGIONS, NY, NX, C)), -4.0, 4.0)
    return (base_noise * row_scale * col_scale * chan_scale).astype(jnp.bfloat16)


def set_ends(values, stream_key, smallest, high):
    shape = values.shape
    place = [jax.random.randint(jax.random.fold_in(stream_key, axis), (), 0, shape[axis]) for axis in range(len(shape))]
    values = values.at[tuple(place)].set(smallest)
    longest = shape.index(max(shape))
    place[longest] = (place[longest] + 1) % shape[longest]
    return values.at[tuple(place)].set(high)


def shard_levels(stream_key, shape, cuts, low, largest):
    def one(axis_at, parts):
        draws = jax.random.uniform(jax.random.fold_in(jax.random.fold_in(stream_key, 6), axis_at), (parts,), jnp.float32, low / len(cuts), largest / len(cuts))
        return jnp.repeat(jnp.exp(draws), shape[axis_at] // parts).reshape((-1,) + (1,) * (len(shape) - axis_at - 1))

    factor_of = one(*cuts[0])
    for cut in cuts[1:]:
        factor_of = factor_of * one(*cut)
    return factor_of


def scatter_about(stream_key, dims, deviation, most, pieces=(), kind=jnp.bfloat16):
    level = shard_levels(stream_key, dims, pieces, -0.22, 0.18) if pieces else 1.0
    array = jax.random.normal(stream_key, dims, jnp.float32) * deviation * level
    return jnp.minimum(jnp.maximum(array, -most), most).astype(kind)


def setup_inputs(seed: int = 0) -> dict:
    key_list = jax.random.split(jax.random.key(seed), 13)
    return {
        "noisy_field": draw_noisy_field(jax.random.fold_in(key_list[12], 71), 0),
        "coarse_cells": scatter_about(key_list[1], (GCELLS, CC), 1.0, 6.0, ((0, 128),), jnp.float32),
        "coarse_proj": scatter_about(key_list[2], (CC, C), CC ** -0.5, 0.25, (), jnp.float32),
        "kernel_first": scatter_about(key_list[3], (3, 3, C, C), (9 * C) ** -0.5, 0.1875),
        "kernel_second": scatter_about(key_list[4], (3, 3, C, C), (9 * C) ** -0.5, 0.1875),
        "gain_first": jnp.clip(1.0 + 0.15 * jax.random.normal(key_list[5], (C,), jnp.float32), 0.25, 1.75),
        "shift_first": scatter_about(key_list[6], (C,), 0.5, 3.0, (), jnp.float32),
        "gain_second": jnp.clip(1.0 + 0.15 * jax.random.normal(key_list[7], (C,), jnp.float32), 0.25, 1.75),
        "shift_second": scatter_about(key_list[8], (C,), 0.5, 3.0, (), jnp.float32),
        "request_ids": draw_request_ids(jax.random.fold_in(key_list[12], 71), 0),
        "patch_slots": draw_patch_slots(jax.random.fold_in(key_list[12], 71), 0),
        "tile_offsets": set_ends(jax.random.randint(key_list[11], (REGIONS, ROW_TILES, COL_TILES, 2), 0, 128), jax.random.fold_in(key_list[11], 1), 0, 127).astype(jnp.int32),
    }


precise = lax.Precision.HIGHEST

def cubic_weights(offset, points, extent):
    position = (offset.astype(jnp.float32)[..., None] + jnp.arange(points, dtype=jnp.float32) * STEP) / 128.0 + 1.0
    centres = jnp.arange(extent, dtype=jnp.float32)
    distance = jnp.abs(position[..., :, None] - centres)
    near_part = (1.5 * distance - 2.5) * distance * distance + 1.0
    far_part = ((-0.5 * distance + 2.5) * distance - 4.0) * distance + 2.0
    return jnp.where(distance < 1.0, near_part, jnp.where(distance < 2.0, far_part, 0.0))

def convolve(source, kernel):
    return lax.conv_general_dilated(source[None].astype(jnp.float32), kernel.astype(jnp.float32), (1, 1), ((1, 1), (1, 1)), dimension_numbers=('NHWC', 'HWIO', 'NHWC'), precision=precise)[0]

def apply_norm(values, totals, squares, number, gain_vec, shift_vec):
    group_width = values.shape[-1] // GROUPS
    group_mean = totals / number
    spread = squares / number - group_mean * group_mean
    inv_scale = lax.rsqrt(spread + 1e-05)
    mean_full = jnp.repeat(group_mean, group_width)
    scale_full = jnp.repeat(inv_scale, group_width)
    return jax.nn.silu((values - mean_full) * (scale_full * gain_vec) + shift_vec)

def group_norm(values, gain_vec, shift_vec):
    grouped = values.reshape(values.shape[0], values.shape[1], GROUPS, -1)
    totals = lax.optimization_barrier(jnp.sum(grouped, axis=(0, 1, 3)))
    squares = lax.optimization_barrier(jnp.sum(grouped * grouped, axis=(0, 1, 3)))
    number = values.shape[0] * values.shape[1] * (values.shape[2] // GROUPS)
    return apply_norm(values, totals, squares, number, gain_vec, shift_vec)

def reference(noisy_field, coarse_cells, coarse_proj, kernel_first, kernel_second, gain_first, shift_first, gain_second, shift_second, request_ids, patch_slots, tile_offsets):

    def one_region(inputs):
        region_field, requests, slot_list, offsets = inputs
        listed = requests.reshape(ROW_TILES, COL_TILES, DEVICES * MOST)
        cell_ids = jnp.take_along_axis(listed, slot_list, axis=2)
        gathered = coarse_cells[cell_ids]
        projected = jnp.einsum('abkd,dc->abkc', gathered, coarse_proj, precision=precise)
        projected = projected.reshape(ROW_TILES, COL_TILES, PATCH, PATCH, C)
        row_weight = cubic_weights(offsets[:, :, 0], TILE, PATCH)
        col_weight = cubic_weights(offsets[:, :, 1], TILE, PATCH)
        partial_rows = jnp.einsum('abhi,abijc->abhjc', row_weight, projected, precision=precise)
        conditioning = jnp.einsum('abwj,abhjc->abhwc', col_weight, partial_rows, precision=precise)
        conditioning = conditioning.transpose(0, 2, 1, 3, 4).reshape(NY, NX, C)
        mixed_field = (region_field.astype(jnp.float32) + conditioning).astype(jnp.bfloat16)
        first_conv = convolve(mixed_field, kernel_first)
        hidden = group_norm(first_conv, gain_first, shift_first).astype(jnp.bfloat16)
        second = convolve(hidden, kernel_second)
        result = mixed_field.astype(jnp.float32) + group_norm(second, gain_second, shift_second)
        return result.astype(jnp.bfloat16)
    return lax.map(one_region, (noisy_field, request_ids, patch_slots, tile_offsets))
```

```python
import functools

import jax
import jax.numpy as jnp
from jax import lax
from jax.experimental import pallas as pl
from jax.experimental.pallas import tpu as pltpu
from jax.sharding import PartitionSpec as P

GROUPS = 32
STEP = 9
PATCH = 13
MOST = 6
TILE = 128
C = 128
CC = 640
HELD = 256
AXES = ("region", "row", "col")
MESH = pl.DeviceIdType.MESH
F32 = jnp.float32
BF16 = jnp.bfloat16
PAIRS = 4


def split3(x):
    hi = x.astype(BF16)
    rest = x - hi.astype(F32)
    mid = rest.astype(BF16)
    lo = (rest - mid.astype(F32)).astype(BF16)
    return hi, mid, lo


def cubic(distance):
    near_part = (1.5 * distance - 2.5) * distance * distance + 1.0
    far_part = ((-0.5 * distance + 2.5) * distance - 4.0) * distance + 2.0
    return jnp.where(distance < 1.0, near_part, jnp.where(distance < 2.0, far_part, 0.0))


def weight_terms(point, lane, offset):
    position = (offset.astype(F32) + point.astype(F32) * STEP) / 128.0 + 1.0
    cell = lane % 16
    group = lane // 16
    weight = cubic(jnp.abs(position - cell.astype(F32)))
    weight = jnp.where(cell < PATCH, weight, 0.0)
    hi, mid, lo = (t.astype(F32) for t in split3(weight))
    return jnp.where(group < 3, hi, jnp.where(group < 5, mid, jnp.where(group < 6, lo, 0.0)))


def silu(v):
    half = 0.5 * v
    return half + half * jnp.tanh(half)


def kernel(
    noisy_hbm,
    cells_hbm,
    proj_hbm,
    k1_hbm,
    k2_hbm,
    g1_ref,
    s1_ref,
    g2_ref,
    s2_ref,
    ids_ref,
    slots_ref,
    off_ref,
    out_hbm,
    noisy,
    cells,
    proj,
    k1,
    k2,
    wb1,
    wb2,
    id_buf,
    id_recv,
    pcat,
    rows_out,
    rows_in,
    slot_row,
    sel,
    patch,
    partial,
    lhs_col,
    unperm,
    x1,
    x2,
    field,
    out,
    col_f,
    col_b,
    halo_b,
    halo_f,
    corner_out,
    corner_in,
    st_out,
    st_in,
    ld_sem,
    id_sem,
    row_sem,
    st_sem,
    halo_send,
    halo_recv,
    out_sem,
):
    g, i, j = (lax.axis_index(a) for a in AXES)
    me = g * 32 + i * 4 + j

    def dev(p):
        return (p // 32, (p // 4) % 8, p % 4)

    loads = [
        pltpu.make_async_copy(a, b, ld_sem.at[n])
        for n, (a, b) in enumerate(
            [(cells_hbm, cells), (proj_hbm, proj), (k1_hbm, k1), (k2_hbm, k2), (noisy_hbm, noisy)]
        )
    ]
    for c in loads:
        c.start()
    barrier = pltpu.get_barrier_semaphore()

    def greet(k, c):
        pl.semaphore_signal(barrier, inc=1, device_id=dev((me + k) % 128), device_id_type=MESH)
        return c

    lax.fori_loop(1, 128, greet, 0)

    def put_ids(o, c):
        id_buf[o, :, 0:MOST] = ids_ref[pl.ds(o, 1), :]
        return c

    lax.fori_loop(0, 128, put_ids, 0)
    id_recv[0, :, 0:MOST] = ids_ref[pl.ds(me, 1), :]
    pl.semaphore_wait(barrier, 127)

    def send_ids(k, c):
        p = (me + k) % 128
        pltpu.make_async_remote_copy(
            id_buf.at[p], id_recv.at[k], id_sem.at[0], id_sem.at[1], device_id=dev(p), device_id_type=MESH
        ).start()
        return c

    lax.fori_loop(1, 128, send_ids, 0)

    loads[0].wait()
    loads[1].wait()
    projected = jnp.dot(
        cells[...], proj[...], precision=lax.Precision.HIGHEST, preferred_element_type=F32
    )
    for n, term in enumerate(split3(projected)):
        pcat[:, n * 128 : (n + 1) * 128] = term
    rows_out[...] = jnp.zeros_like(rows_out)
    partial[...] = jnp.zeros_like(partial)

    slot_row[...] = jnp.full_like(slot_row, -1)
    slot_row[0:1, 0 : PATCH * PATCH] = slots_ref[...]
    slot = slot_row[0:1, :]
    owner = (slot * 10923) >> 16
    place = slot - owner * MOST
    index = ((owner - me + 128) & 127) * 8 + place
    index = jnp.where(slot < 0, -1, index).astype(F32)
    index = jnp.transpose(jnp.broadcast_to(index, (128, 256)))
    lane = lax.broadcasted_iota(jnp.int32, (256, 128), 1).astype(F32)
    for n in range(8):
        sel[:, n * 128 : (n + 1) * 128] = jnp.where(index == lane + 128.0 * n, 1.0, 0.0).astype(BF16)

    r_iota = lax.broadcasted_iota(jnp.int32, (128, 128), 0)
    l_iota = lax.broadcasted_iota(jnp.int32, (128, 128), 1)
    column = (r_iota % 16) * 8 + r_iota // 16
    lhs_col[:, 0:128] = weight_terms(column, l_iota, off_ref[0, 1]).astype(BF16)
    lhs_col[:, 128:256] = jnp.where(column == l_iota, 1.0, 0.0).astype(BF16)
    unperm[...] = jnp.where((l_iota % 16) * 8 + l_iota // 16 == r_iota, 1.0, 0.0).astype(BF16)
    lhs_row = weight_terms(r_iota, l_iota, off_ref[0, 0]).astype(BF16)

    loads[2].wait()
    loads[3].wait()
    zero_block = jnp.zeros((128, 128), BF16)
    for w, wb in ((k1, wb1), (k2, wb2)):
        for a in range(4):
            for b in range(3):
                for e in range(2):
                    block = w[a - e, b] if 0 <= a - e <= 2 else zero_block
                    wb[(a * 3 + b) * 128 : (a * 3 + b + 1) * 128, e * 128 : (e + 1) * 128] = block

    def whole(ref, sem):
        return pltpu.make_async_copy(ref, ref, sem)

    whole(id_recv.at[pl.ds(1, 127)], id_sem.at[1]).wait()
    asked = id_recv[:, 0, :] - me * HELD
    row_iota = lax.broadcasted_iota(jnp.int32, (128, HELD), 1)
    for m in range(MOST):
        hot = jnp.where(asked[:, m : m + 1] == row_iota, 1.0, 0.0).astype(BF16)
        found = jnp.dot(hot, pcat[...], preferred_element_type=F32)
        found = found[:, 0:128] + found[:, 128:256] + found[:, 256:384]
        rows_out[pl.ds(m, 128, stride=8), :] = found
    rows_in[0:8, :] = rows_out[0:8, :]

    def send_rows(k, c):
        part = pl.ds(pl.multiple_of(k * 8, 8), 8)
        pltpu.make_async_remote_copy(
            rows_out.at[part],
            rows_in.at[part],
            row_sem.at[0],
            row_sem.at[1],
            device_id=dev((me - k + 128) % 128),
            device_id_type=MESH,
        ).start()
        return c

    lax.fori_loop(1, 128, send_rows, 0)
    whole(id_buf.at[pl.ds(1, 127)], id_sem.at[0]).wait()
    loads[4].wait()
    whole(rows_in.at[pl.ds(8, 1016)], row_sem.at[1]).wait()

    terms = jnp.concatenate(split3(rows_in[...]), axis=1)
    cell = jnp.dot(sel[...], terms, preferred_element_type=F32)
    patch[...] = cell[:, 0:128] + cell[:, 128:256] + cell[:, 256:384]
    zero_tile = jnp.zeros((32, 128), BF16)

    def stack_terms(x):
        hi, mid, lo = split3(x)
        return jnp.concatenate([hi, mid, lo, hi, mid, hi, zero_tile], axis=0)

    for b in range(PATCH):
        rhs = stack_terms(patch[pl.ds(b, 16, stride=PATCH), :])
        partial[pl.ds(b, 128, stride=16), :] = jnp.dot(lhs_row, rhs, preferred_element_type=F32)

    def mix_pair(p):
        rhs = []
        for e in range(2):
            h = 2 * p + e
            t = stack_terms(partial[pl.ds(pl.multiple_of(h * 16, 16), 16), :])
            rhs.append(jnp.concatenate([t, noisy[h]], axis=0))
        mixed = jnp.dot(
            lhs_col[...], jnp.concatenate(rhs, axis=1), preferred_element_type=F32
        ).astype(BF16)
        for e in range(2):
            h = 2 * p + e
            m = mixed[:, e * 128 : (e + 1) * 128]
            x1[h + 1, 1:9] = m.reshape(8, 16, 128)
            mf = m.astype(F32)
            col_f[0, pl.ds(h, 1), :] = mf[0:1]
            col_f[1, pl.ds(h, 1), :] = mf[127:128]

    def neighbour(di, dj):
        return (g, (i + di + 8) % 8, (j + dj + 4) % 4)

    def row_copies(x, base):
        cs = []
        for n, (src, dst, di) in enumerate(((1, 129, -1), (128, 0, 1))):
            cs.append(
                pltpu.make_async_remote_copy(
                    x.at[src, pl.ds(1, 8)],
                    x.at[dst, pl.ds(1, 8)],
                    halo_send.at[base + n],
                    halo_recv.at[base + n],
                    device_id=neighbour(di, 0),
                    device_id_type=MESH,
                )
            )
        return cs

    def corner_copies(base):
        cs = []
        for n, (di, dj) in enumerate(((-1, -1), (-1, 1), (1, -1), (1, 1))):
            slot_n = base // 8 * 4 + n
            cs.append(
                pltpu.make_async_remote_copy(
                    corner_out.at[slot_n],
                    corner_in.at[slot_n],
                    halo_send.at[base + 4 + n],
                    halo_recv.at[base + 4 + n],
                    device_id=neighbour(di, dj),
                    device_id_type=MESH,
                )
            )
        return cs

    def col_copies(base):
        cs = []
        for n, dj in enumerate((-1, 1)):
            slot_n = base // 8 * 2 + n
            cs.append(
                pltpu.make_async_remote_copy(
                    col_b.at[slot_n],
                    halo_b.at[slot_n],
                    halo_send.at[base + 2 + n],
                    halo_recv.at[base + 2 + n],
                    device_id=neighbour(0, dj),
                    device_id_type=MESH,
                )
            )
        return cs

    def put_corners(base):
        s = base // 8 * 4
        for n, (side, h) in enumerate(((0, 0), (1, 0), (0, 127), (1, 127))):
            corner_out[s + n] = jnp.broadcast_to(col_f[side, h : h + 1, :], (8, 128))

    def put_columns(base):
        s = base // 8 * 2
        for side in range(2):
            col_b[s + side] = col_f[side].astype(BF16)

    def finish_halo(x, base, copies):
        for c in copies:
            c.wait()
        s2, s4 = base // 8 * 2, base // 8 * 4
        left_ok = jnp.where(j > 0, 1.0, 0.0)
        right_ok = jnp.where(j < 3, 1.0, 0.0)
        up_ok = jnp.where(i > 0, 1.0, 0.0)
        down_ok = jnp.where(i < 7, 1.0, 0.0)
        halo_f[0, 8:136, :] = halo_b[s2 + 1].astype(F32) * left_ok
        halo_f[1, 8:136, :] = halo_b[s2 + 0].astype(F32) * right_ok
        halo_f[0, 0:8, :] = corner_in[s4 + 3] * (left_ok * up_ok)
        halo_f[1, 0:8, :] = corner_in[s4 + 2] * (right_ok * up_ok)
        halo_f[0, 136:144, :] = corner_in[s4 + 1] * (left_ok * down_ok)
        halo_f[1, 136:144, :] = corner_in[s4 + 0] * (right_ok * down_ok)

        @pl.when(i == 0)
        def _():
            x[0, 1:9] = jnp.zeros((8, 16, 128), BF16)

        @pl.when(i == 7)
        def _():
            x[129, 1:9] = jnp.zeros((8, 16, 128), BF16)

        sub = lax.broadcasted_iota(jnp.int32, (16, 128), 0)

        def edge(n, c):
            last = pltpu.roll(x[n, 8].astype(F32), 1, 0)
            x[n, 0] = jnp.where(sub == 0, halo_f[0, pl.ds(n + 7, 1), :], last).astype(BF16)
            first = pltpu.roll(x[n, 1].astype(F32), 15, 0)
            x[n, 9] = jnp.where(sub == 15, halo_f[1, pl.ds(n + 7, 1), :], first).astype(BF16)
            return c

        lax.fori_loop(0, 130, edge, 0, unroll=5)

    mix_pair(0)
    mix_pair(63)
    halo1 = row_copies(x1, 0) + corner_copies(0)
    put_corners(0)
    for c in halo1:
        c.start()

    def mix_loop(p, c):
        mix_pair(p)
        return c

    lax.fori_loop(1, 63, mix_loop, 0, unroll=2)
    put_columns(0)
    cols1 = col_copies(0)
    for c in cols1:
        c.start()
    finish_halo(x1, 0, halo1 + cols1)

    def convolve(x, wb):
        def step(t, carry):
            total, square = carry
            y = t * (2 * PAIRS)
            lhs = []
            for q in range(PAIRS):
                parts = [
                    x[y + 2 * q + a, b : b + 8].reshape(128, 128) for a in range(4) for b in range(3)
                ]
                lhs.append(jnp.concatenate(parts, axis=1))
            got = jnp.dot(jnp.concatenate(lhs, axis=0), wb[...], preferred_element_type=F32)
            for q in range(PAIRS):
                for e in range(2):
                    v = got[q * 128 : (q + 1) * 128, e * 128 : (e + 1) * 128]
                    field[y + 2 * q + e] = v
                    v3 = v.reshape(16, 8, 128)
                    total = total + jnp.sum(v3, axis=0)
                    square = square + jnp.sum(v3 * v3, axis=0)
            return total, square

        zero = jnp.zeros((8, 128), F32)
        return lax.fori_loop(0, 64 // PAIRS, step, (zero, zero))

    group_ones = jnp.where(r_iota // 4 == l_iota // 4, 1.0, 0.0)
    number = float(TILE * TILE * 32 * (C // GROUPS))

    def norm_terms(n, sums, gain, shift):
        total, square = (jnp.sum(s, axis=0, keepdims=True) for s in sums)
        sub8 = lax.broadcasted_iota(jnp.int32, (8, 128), 0)
        mine = jnp.where(sub8 == 0, total, jnp.where(sub8 == 1, square, 0.0))
        st_out[n] = mine
        st_in[n, 0] = mine
        base = g * 32
        home = i * 4 + j

        def send(k, c):
            pltpu.make_async_remote_copy(
                st_out.at[n],
                st_in.at[n, k],
                st_sem.at[n, 0],
                st_sem.at[n, 1],
                device_id=dev(base + (home + k) % 32),
                device_id_type=MESH,
            ).start()
            return c

        lax.fori_loop(1, 32, send, 0)
        whole(st_in.at[n, pl.ds(1, 31)], st_sem.at[n, 1]).wait()
        both = jnp.sum(st_in[n], axis=0)
        both = jnp.dot(
            both, group_ones, precision=lax.Precision.HIGHEST, preferred_element_type=F32
        )
        mean = both[0:1] / number
        spread = both[1:2] / number - mean * mean
        scale = lax.rsqrt(spread + 1e-05) * gain
        whole(st_in.at[n, pl.ds(1, 31)], st_sem.at[n, 0]).wait()
        return scale, shift - mean * scale

    sums = convolve(x1, wb1)
    scale, offset = norm_terms(0, sums, g1_ref[...], s1_ref[...])

    def hide(h, lo, hi):
        v = field[h, lo * 16 : hi * 16, :]
        m = silu(v * scale + offset).astype(BF16)
        x2[h + 1, 1 + lo : 1 + hi] = m.reshape(hi - lo, 16, 128)
        return m.astype(F32)

    def hide_ends(h, c):
        a = hide(h, 0, 1)
        b = hide(h, 7, 8)
        col_f[0, pl.ds(h, 1), :] = a[0:1]
        col_f[1, pl.ds(h, 1), :] = b[15:16]
        return c

    def hide_rest(h, c):
        hide(h, 1, 7)
        return c

    for h in (0, 127):
        hide_ends(h, 0)
        hide_rest(h, 0)
    halo2 = row_copies(x2, 8) + corner_copies(8)
    put_corners(8)
    for c in halo2:
        c.start()
    lax.fori_loop(1, 127, hide_ends, 0, unroll=6)
    put_columns(8)
    cols2 = col_copies(8)
    for c in cols2:
        c.start()
    lax.fori_loop(1, 127, hide_rest, 0, unroll=2)
    finish_halo(x2, 8, halo2 + cols2)

    sums = convolve(x2, wb2)
    scale2, offset2 = norm_terms(1, sums, g2_ref[...], s2_ref[...])

    def finish(p, c):
        both = []
        for e in range(2):
            h = 2 * p + e
            v = silu(field[h] * scale2 + offset2)
            both.append((x1[h + 1, 1:9].reshape(128, 128).astype(F32) + v).astype(BF16))
        res = jnp.dot(unperm[...], jnp.concatenate(both, axis=1), preferred_element_type=F32).astype(BF16)
        out[2 * p] = res[:, 0:128]
        out[2 * p + 1] = res[:, 128:256]
        return c

    parts = 8
    for n in range(parts):
        lax.fori_loop(n * 64 // parts, (n + 1) * 64 // parts, finish, 0, unroll=2)
        rows = pl.ds(n * 128 // parts, 128 // parts)
        pltpu.make_async_copy(out.at[rows], out_hbm.at[rows], out_sem).start()
    whole(rows_in.at[pl.ds(8, 1016)], row_sem.at[0]).wait()
    pltpu.make_async_copy(out, out_hbm, out_sem).wait()


def body(
    noisy_field,
    coarse_cells,
    coarse_proj,
    kernel_first,
    kernel_second,
    gain_first,
    shift_first,
    gain_second,
    shift_second,
    request_ids,
    patch_slots,
    tile_offsets,
):
    hbm = pl.BlockSpec(memory_space=pl.ANY)
    vmem = pl.BlockSpec(memory_space=pltpu.VMEM)
    smem = pl.BlockSpec(memory_space=pltpu.SMEM)
    row = lambda v: v.reshape(1, C)
    got = pl.pallas_call(
        kernel,
        out_shape=jax.ShapeDtypeStruct((TILE, TILE, C), BF16),
        in_specs=[hbm] * 5 + [vmem] * 6 + [smem],
        out_specs=hbm,
        scratch_shapes=[
            pltpu.VMEM((TILE, TILE, C), BF16),
            pltpu.VMEM((HELD, CC), F32),
            pltpu.VMEM((CC, C), F32),
            pltpu.VMEM((3, 3, C, C), BF16),
            pltpu.VMEM((3, 3, C, C), BF16),
            pltpu.VMEM((12 * C, 2 * C), BF16),
            pltpu.VMEM((12 * C, 2 * C), BF16),
            pltpu.VMEM((128, 1, 128), jnp.int32),
            pltpu.VMEM((128, 1, 128), jnp.int32),
            pltpu.VMEM((HELD, 3 * C), BF16),
            pltpu.VMEM((1024, C), F32),
            pltpu.VMEM((1024, C), F32),
            pltpu.VMEM((8, 256), jnp.int32),
            pltpu.VMEM((256, 1024), BF16),
            pltpu.VMEM((256, C), F32),
            pltpu.VMEM((TILE * 16, C), F32),
            pltpu.VMEM((128, 256), BF16),
            pltpu.VMEM((128, 128), BF16),
            pltpu.VMEM((TILE + 2, 10, 16, C), BF16),
            pltpu.VMEM((TILE + 2, 10, 16, C), BF16),
            pltpu.VMEM((TILE, TILE, C), F32),
            pltpu.VMEM((TILE, TILE, C), BF16),
            pltpu.VMEM((2, TILE, C), F32),
            pltpu.VMEM((4, TILE, C), BF16),
            pltpu.VMEM((4, TILE, C), BF16),
            pltpu.VMEM((2, 144, C), F32),
            pltpu.VMEM((8, 8, C), F32),
            pltpu.VMEM((8, 8, C), F32),
            pltpu.VMEM((2, 8, C), F32),
            pltpu.VMEM((2, 32, 8, C), F32),
            pltpu.SemaphoreType.DMA((5,)),
            pltpu.SemaphoreType.DMA((2,)),
            pltpu.SemaphoreType.DMA((2,)),
            pltpu.SemaphoreType.DMA((2, 2)),
            pltpu.SemaphoreType.DMA((16,)),
            pltpu.SemaphoreType.DMA((16,)),
            pltpu.SemaphoreType.DMA,
        ],
        compiler_params=pltpu.CompilerParams(
            collective_id=0, has_side_effects=True, vmem_limit_bytes=60 << 20
        ),
        name="block",
    )(
        noisy_field.reshape(TILE, TILE, C),
        coarse_cells,
        coarse_proj,
        kernel_first,
        kernel_second,
        row(gain_first),
        row(shift_first),
        row(gain_second),
        row(shift_second),
        request_ids.reshape(128, MOST),
        patch_slots.reshape(1, PATCH * PATCH),
        tile_offsets.reshape(1, 2),
    )
    return got[None]


def solution(mesh):
    return jax.shard_map(
        body,
        mesh=mesh,
        in_specs=(
            P("region", "row", "col", None),
            P(("region", "row", "col"), None),
            P(),
            P(),
            P(),
            P(),
            P(),
            P(),
            P(),
            P("region", "row", "col", None, None),
            P("region", "row", "col", None),
            P("region", "row", "col", None),
        ),
        out_specs=P("region", "row", "col", None),
        check_vma=False,
    )
```

```python
import functools

import jax
import jax.numpy as jnp
from jax import lax
from jax.experimental import pallas as pl
from jax.experimental.pallas import tpu as pltpu
from jax.sharding import PartitionSpec as P

GROUPS = 32
STEP = 9
PATCH = 13
MOST = 6
TILE = 128
C = 128
CC = 640
HELD = 256
AXES = ("region", "row", "col")
MESH = pl.DeviceIdType.MESH
FLAT = pl.DeviceIdType.LOGICAL
F32 = jnp.float32
BF16 = jnp.bfloat16
PAIRS = 16


def split3(x):
    hi = x.astype(BF16)
    rest = x - hi.astype(F32)
    mid = rest.astype(BF16)
    lo = (rest - mid.astype(F32)).astype(BF16)
    return hi, mid, lo


def cubic(distance):
    near_part = (1.5 * distance - 2.5) * distance * distance + 1.0
    far_part = ((-0.5 * distance + 2.5) * distance - 4.0) * distance + 2.0
    return jnp.where(distance < 1.0, near_part, jnp.where(distance < 2.0, far_part, 0.0))


def weight_terms(point, lane, offset):
    position = (offset.astype(F32) + point.astype(F32) * STEP) / 128.0 + 1.0
    cell = lane % 16
    group = lane // 16
    weight = cubic(jnp.abs(position - cell.astype(F32)))
    weight = jnp.where(cell < PATCH, weight, 0.0)
    hi, mid, lo = (t.astype(F32) for t in split3(weight))
    return jnp.where(group < 3, hi, jnp.where(group < 5, mid, jnp.where(group < 6, lo, 0.0)))


def silu(v):
    return v * jax.nn.sigmoid(v)


def far_first(n):
    return (~n & 0b1010100) | ((n ^ (n >> 1)) & 0b0101010) | (~n & 1)


def kernel(
    noisy_hbm,
    cells_hbm,
    proj_hbm,
    k1_hbm,
    k2_hbm,
    g1_ref,
    s1_ref,
    g2_ref,
    s2_ref,
    ids_ref,
    slots_ref,
    off_ref,
    out,
    noisy,
    cells,
    proj,
    k1,
    k2,
    wb1,
    wb2,
    id_rows,
    id_buf,
    id_recv,
    pcat,
    rows_out,
    rows_in,
    slot_row,
    sel,
    patch,
    partial,
    lhs_col,
    x1,
    x2,
    field,
    swap,
    col_f,
    col_b,
    halo_b,
    halo_f,
    corner_out,
    corner_in,
    st_out,
    st_in,
    ld_sem,
    id_sem,
    row_sem,
    st_sem,
    halo_send,
    halo_recv,
):
    g, i, j = (lax.axis_index(a) for a in AXES)
    me = g * 32 + i * 4 + j

    loads = [
        pltpu.make_async_copy(a, b, ld_sem.at[n])
        for n, (a, b) in enumerate(
            [(cells_hbm, cells), (proj_hbm, proj), (k1_hbm, k1), (k2_hbm, k2), (noisy_hbm, noisy)]
        )
    ]
    for c in loads:
        c.start()
    barrier = pltpu.get_barrier_semaphore()

    def greet(n, c):
        pl.semaphore_signal(barrier, inc=1, device_id=me ^ far_first(n), device_id_type=FLAT)
        return c

    lax.fori_loop(0, 127, greet, 0)

    id_rows[...] = jnp.zeros_like(id_rows)
    id_rows[0:MOST, :] = ids_ref[...].astype(F32)
    id_buf[:, 0, :] = jnp.transpose(id_rows[...])
    id_recv[0] = id_buf[me]
    pl.semaphore_wait(barrier, 127)

    def send_ids(n, c):
        k = far_first(n)
        pltpu.make_async_remote_copy(
            id_buf.at[me ^ k], id_recv.at[k], id_sem.at[0], id_sem.at[1], device_id=me ^ k, device_id_type=FLAT
        ).start()
        return c

    lax.fori_loop(0, 127, send_ids, 0)

    loads[0].wait()
    loads[1].wait()
    projected = jnp.dot(
        cells[...], proj[...], precision=lax.Precision.HIGHEST, preferred_element_type=F32
    )
    for n, term in enumerate(split3(projected)):
        pcat[:, n * 128 : (n + 1) * 128] = term
    partial[...] = jnp.zeros_like(partial)

    slot_row[...] = jnp.full_like(slot_row, -1)
    slot_row[0:1, 0 : PATCH * PATCH] = slots_ref[...]
    slot = slot_row[0:1, :]
    owner = (slot * 10923) >> 16
    place = slot - owner * MOST
    index = place * 128 + (owner ^ me)
    index = jnp.where(slot < 0, -1, index).astype(F32)
    index = jnp.transpose(jnp.broadcast_to(index, (128, 256)))
    lane = lax.broadcasted_iota(jnp.int32, (256, 128), 1).astype(F32)
    for n in range(MOST):
        sel[:, n * 128 : (n + 1) * 128] = jnp.where(index == lane + 128.0 * n, 1.0, 0.0).astype(BF16)

    r_iota = lax.broadcasted_iota(jnp.int32, (128, 128), 0)
    l_iota = lax.broadcasted_iota(jnp.int32, (128, 128), 1)
    column = (r_iota % 16) * 8 + r_iota // 16
    lhs_col[:, 0:128] = weight_terms(column, l_iota, off_ref[0, 1]).astype(BF16)
    lhs_col[:, 128:256] = jnp.where(column == l_iota, 1.0, 0.0).astype(BF16)
    lhs_row = weight_terms(r_iota, l_iota, off_ref[0, 0]).astype(BF16)

    loads[2].wait()
    loads[3].wait()
    zero_block = jnp.zeros((128, 128), BF16)
    for w, wb in ((k1, wb1), (k2, wb2)):
        for a in range(4):
            for b in range(3):
                for e in range(2):
                    block = w[a - e, b] if 0 <= a - e <= 2 else zero_block
                    wb[(a * 3 + b) * 128 : (a * 3 + b + 1) * 128, e * 128 : (e + 1) * 128] = block

    def whole(ref, sem):
        return pltpu.make_async_copy(ref, ref, sem)

    whole(id_recv.at[pl.ds(1, 127)], id_sem.at[1]).wait()
    asked = id_recv[:, 0, :] - (me * HELD).astype(F32)
    row_iota = lax.broadcasted_iota(jnp.int32, (128, HELD), 1).astype(F32)
    for m in range(MOST):
        hot = jnp.where(asked[:, m : m + 1] == row_iota, 1.0, 0.0).astype(BF16)
        found = jnp.dot(hot, pcat[...], preferred_element_type=F32)
        found = found[:, 0:128] + found[:, 128:256] + found[:, 256:384]
        rows_out[:, m, :] = found
    rows_in[0] = rows_out[0]

    def send_rows(n, c):
        k = far_first(n)
        pltpu.make_async_remote_copy(
            rows_out.at[k],
            rows_in.at[k],
            row_sem.at[0],
            row_sem.at[1],
            device_id=me ^ k,
            device_id_type=FLAT,
        ).start()
        return c

    lax.fori_loop(0, 127, send_rows, 0)
    whole(id_buf.at[pl.ds(1, 127)], id_sem.at[0]).wait()
    loads[4].wait()
    whole(rows_in.at[pl.ds(1, 127)], row_sem.at[1]).wait()

    terms = [jnp.concatenate(split3(rows_in[:, m, :]), axis=1) for m in range(MOST)]
    cell = jnp.dot(sel[...], jnp.concatenate(terms, axis=0), preferred_element_type=F32)
    patch[...] = cell[:, 0:128] + cell[:, 128:256] + cell[:, 256:384]
    zero_tile = jnp.zeros((32, 128), BF16)

    def stack_terms(x):
        hi, mid, lo = split3(x)
        return jnp.concatenate([hi, mid, lo, hi, mid, hi, zero_tile], axis=0)

    for b in range(PATCH):
        rhs = stack_terms(patch[pl.ds(b, 16, stride=PATCH), :])
        partial[pl.ds(b, 128, stride=16), :] = jnp.dot(lhs_row, rhs, preferred_element_type=F32)

    def mix_rows(first, count):
        rhs = []
        for q in range(count):
            h = first + q
            t = stack_terms(partial[pl.ds(pl.multiple_of(h * 16, 16), 16), :])
            rhs.append(jnp.concatenate([t, noisy[h]], axis=0))
        mixed = jnp.dot(
            lhs_col[...], jnp.concatenate(rhs, axis=1), preferred_element_type=F32
        ).astype(BF16)
        for q in range(count):
            h = first + q
            m = mixed[:, q * 128 : (q + 1) * 128]
            x1[h + 1, 1:9] = m.reshape(8, 16, 128)
            col_f[0, pl.ds(h, 1), :] = m[0:16].astype(F32)[0:1]
            col_f[1, pl.ds(h, 1), :] = m[112:128].astype(F32)[15:16]

    def neighbour(di, dj):
        return (g, (i + di + 8) % 8, (j + dj + 4) % 4)

    def row_copies(x, base):
        cs = []
        for n, (src, dst, di) in enumerate(((1, 129, -1), (128, 0, 1))):
            cs.append(
                pltpu.make_async_remote_copy(
                    x.at[src, pl.ds(1, 8)],
                    x.at[dst, pl.ds(1, 8)],
                    halo_send.at[base + n],
                    halo_recv.at[base + n],
                    device_id=neighbour(di, 0),
                    device_id_type=MESH,
                )
            )
        return cs

    def corner_copies(base):
        cs = []
        for n, (di, dj) in enumerate(((-1, -1), (-1, 1), (1, -1), (1, 1))):
            slot_n = base // 8 * 4 + n
            cs.append(
                pltpu.make_async_remote_copy(
                    corner_out.at[slot_n],
                    corner_in.at[slot_n],
                    halo_send.at[base + 4 + n],
                    halo_recv.at[base + 4 + n],
                    device_id=neighbour(di, dj),
                    device_id_type=MESH,
                )
            )
        return cs

    def col_copies(base):
        cs = []
        for n, dj in enumerate((-1, 1)):
            slot_n = base // 8 * 2 + n
            cs.append(
                pltpu.make_async_remote_copy(
                    col_b.at[slot_n],
                    halo_b.at[slot_n],
                    halo_send.at[base + 2 + n],
                    halo_recv.at[base + 2 + n],
                    device_id=neighbour(0, dj),
                    device_id_type=MESH,
                )
            )
        return cs

    def put_corners(base):
        s = base // 8 * 4
        for n, (side, h) in enumerate(((0, 0), (1, 0), (0, 127), (1, 127))):
            corner_out[s + n] = jnp.broadcast_to(col_f[side, h : h + 1, :], (8, 128))

    def put_columns(base):
        s = base // 8 * 2
        for side in range(2):
            col_b[s + side] = col_f[side].astype(BF16)

    left_ok = jnp.where(j > 0, 1.0, 0.0)
    right_ok = jnp.where(j < 3, 1.0, 0.0)
    up_ok = jnp.where(i > 0, 1.0, 0.0)
    down_ok = jnp.where(i < 7, 1.0, 0.0)
    sub = lax.broadcasted_iota(jnp.int32, (16, 128), 0)

    def edge(x, n):
        last = pltpu.roll(x[n, 8].astype(F32), 1, 0)
        x[n, 0] = jnp.where(sub == 0, halo_f[0, pl.ds(n + 7, 1), :], last).astype(BF16)
        first = pltpu.roll(x[n, 1].astype(F32), 15, 0)
        x[n, 9] = jnp.where(sub == 15, halo_f[1, pl.ds(n + 7, 1), :], first).astype(BF16)

    def finish_columns(x, base, copies):
        for c in copies:
            c.wait()
        s2 = base // 8 * 2
        halo_f[0, 8:136, :] = halo_b[s2 + 1].astype(F32) * left_ok
        halo_f[1, 8:136, :] = halo_b[s2 + 0].astype(F32) * right_ok

        def step(n, c):
            edge(x, n)
            return c

        lax.fori_loop(1, 129, step, 0, unroll=8)

    def finish_rows(x, base, copies):
        for c in copies:
            c.wait()
        s4 = base // 8 * 4
        halo_f[0, 0:8, :] = corner_in[s4 + 3] * (left_ok * up_ok)
        halo_f[1, 0:8, :] = corner_in[s4 + 2] * (right_ok * up_ok)
        halo_f[0, 136:144, :] = corner_in[s4 + 1] * (left_ok * down_ok)
        halo_f[1, 136:144, :] = corner_in[s4 + 0] * (right_ok * down_ok)

        @pl.when(i == 0)
        def _():
            x[0, 1:9] = jnp.zeros((8, 16, 128), BF16)

        @pl.when(i == 7)
        def _():
            x[129, 1:9] = jnp.zeros((8, 16, 128), BF16)

        edge(x, 0)
        edge(x, 129)

    mix_rows(0, 2)
    mix_rows(126, 2)
    halo1 = row_copies(x1, 0) + corner_copies(0)
    put_corners(0)
    for c in halo1:
        c.start()

    def mix_loop(n, c):
        mix_rows(2 + n * 32, 32)
        return c

    lax.fori_loop(0, 3, mix_loop, 0)
    mix_rows(98, 28)
    put_columns(0)
    cols1 = col_copies(0)
    for c in cols1:
        c.start()

    def convolve(x, wb, base, columns, rows):
        def step(t, carry):
            total, square = carry
            y = t * (2 * PAIRS)
            lhs = []
            for q in range(PAIRS):
                parts = [
                    x[y + 2 * q + a, b : b + 8].reshape(128, 128) for a in range(4) for b in range(3)
                ]
                lhs.append(jnp.concatenate(parts, axis=1))
            got = jnp.dot(jnp.concatenate(lhs, axis=0), wb[...], preferred_element_type=F32)
            for q in range(PAIRS):
                for e in range(2):
                    v = got[q * 128 : (q + 1) * 128, e * 128 : (e + 1) * 128]
                    field[y + 2 * q + e] = v
                    v3 = v.reshape(16, 8, 128)
                    total = total + jnp.sum(v3, axis=0)
                    square = square + jnp.sum(v3 * v3, axis=0)
            return total, square

        blocks = 64 // PAIRS
        zero = jnp.zeros((8, 128), F32)
        finish_columns(x, base, columns)
        sums = lax.fori_loop(1, blocks - 1, step, (zero, zero))
        finish_rows(x, base, rows)
        return lax.fori_loop(0, 2, lambda n, c: step(n * (blocks - 1), c), sums)

    group_ones = jnp.where(r_iota // 4 == l_iota // 4, 1.0, 0.0)
    number = float(TILE * TILE * 32 * (C // GROUPS))

    def norm_terms(n, sums, gain, shift):
        total, square = (jnp.sum(s, axis=0, keepdims=True) for s in sums)
        sub8 = lax.broadcasted_iota(jnp.int32, (8, 128), 0)
        mine = jnp.where(sub8 == 0, total, jnp.where(sub8 == 1, square, 0.0))
        st_out[n] = mine
        st_in[n, 0] = mine
        def send(t, c):
            k = far_first(t)
            pltpu.make_async_remote_copy(
                st_out.at[n],
                st_in.at[n, k],
                st_sem.at[n, 0],
                st_sem.at[n, 1],
                device_id=me ^ k,
                device_id_type=FLAT,
            ).start()
            return c

        lax.fori_loop(96, 127, send, 0)
        whole(st_in.at[n, pl.ds(1, 31)], st_sem.at[n, 1]).wait()
        both = jnp.sum(st_in[n], axis=0)
        both = jnp.dot(
            both, group_ones, precision=lax.Precision.HIGHEST, preferred_element_type=F32
        )
        mean = both[0:1] / number
        spread = both[1:2] / number - mean * mean
        scale = lax.rsqrt(spread + 1e-05) * gain
        whole(st_in.at[n, pl.ds(1, 31)], st_sem.at[n, 0]).wait()
        return scale, shift - mean * scale

    sums = convolve(x1, wb1, 0, cols1, halo1)
    scale, offset = norm_terms(0, sums, g1_ref[...], s1_ref[...])

    def hide(h, lo, hi):
        v = field[h, lo * 16 : hi * 16, :]
        m = silu(v * scale + offset).astype(BF16)
        x2[h + 1, 1 + lo : 1 + hi] = m.reshape(hi - lo, 16, 128)
        return m.astype(F32)

    def hide_ends(h, c):
        a = hide(h, 0, 1)
        b = hide(h, 7, 8)
        col_f[0, pl.ds(h, 1), :] = a[0:1]
        col_f[1, pl.ds(h, 1), :] = b[15:16]
        return c

    def hide_rest(h, c):
        hide(h, 1, 7)
        return c

    lax.fori_loop(0, 128, hide_ends, 0, unroll=8)
    put_columns(8)
    cols2 = col_copies(8)
    for c in cols2:
        c.start()
    hide_rest(0, 0)
    hide_rest(127, 0)
    halo2 = row_copies(x2, 8) + corner_copies(8)
    put_corners(8)
    for c in halo2:
        c.start()
    lax.fori_loop(1, 127, hide_rest, 0, unroll=7)

    sums = convolve(x2, wb2, 8, cols2, halo2)
    scale2, offset2 = norm_terms(1, sums, g2_ref[...], s2_ref[...])

    def finish(n, c):
        for q in range(8):
            h = n * 8 + q
            v = silu(field[h] * scale2 + offset2)
            v = x1[h + 1, 1:9].reshape(128, 128).astype(F32) + v
            for s in range(8):
                swap[q, pl.ds(s, 16, stride=8), :] = v[s * 16 : (s + 1) * 16]
        for q in range(8):
            out[n * 8 + q] = swap[q].astype(BF16)
        return c

    lax.fori_loop(0, 16, finish, 0)
    whole(rows_in.at[pl.ds(1, 127)], row_sem.at[0]).wait()


def body(
    noisy_field,
    coarse_cells,
    coarse_proj,
    kernel_first,
    kernel_second,
    gain_first,
    shift_first,
    gain_second,
    shift_second,
    request_ids,
    patch_slots,
    tile_offsets,
):
    hbm = pl.BlockSpec(memory_space=pl.ANY)
    vmem = pl.BlockSpec(memory_space=pltpu.VMEM)
    smem = pl.BlockSpec(memory_space=pltpu.SMEM)
    row = lambda v: v.reshape(1, C)
    got = pl.pallas_call(
        kernel,
        out_shape=pltpu.VMEM((TILE, TILE, C), BF16),
        in_specs=[hbm] * 5 + [vmem] * 6 + [smem],
        out_specs=vmem,
        scratch_shapes=[
            pltpu.VMEM((TILE, TILE, C), BF16),
            pltpu.VMEM((HELD, CC), F32),
            pltpu.VMEM((CC, C), F32),
            pltpu.VMEM((3, 3, C, C), BF16),
            pltpu.VMEM((3, 3, C, C), BF16),
            pltpu.VMEM((12 * C, 2 * C), BF16),
            pltpu.VMEM((12 * C, 2 * C), BF16),
            pltpu.VMEM((128, 128), F32),
            pltpu.VMEM((128, 1, 128), F32),
            pltpu.VMEM((128, 1, 128), F32),
            pltpu.VMEM((HELD, 3 * C), BF16),
            pltpu.VMEM((128, MOST, C), F32),
            pltpu.VMEM((128, MOST, C), F32),
            pltpu.VMEM((8, 256), jnp.int32),
            pltpu.VMEM((256, MOST * 128), BF16),
            pltpu.VMEM((256, C), F32),
            pltpu.VMEM((TILE * 16, C), F32),
            pltpu.VMEM((128, 256), BF16),
            pltpu.VMEM((TILE + 2, 10, 16, C), BF16),
            pltpu.VMEM((TILE + 2, 10, 16, C), BF16),
            pltpu.VMEM((TILE, TILE, C), F32),
            pltpu.VMEM((8, TILE, C), F32),
            pltpu.VMEM((2, TILE, C), F32),
            pltpu.VMEM((4, TILE, C), BF16),
            pltpu.VMEM((4, TILE, C), BF16),
            pltpu.VMEM((2, 144, C), F32),
            pltpu.VMEM((8, 8, C), F32),
            pltpu.VMEM((8, 8, C), F32),
            pltpu.VMEM((2, 8, C), F32),
            pltpu.VMEM((2, 32, 8, C), F32),
            pltpu.SemaphoreType.DMA((5,)),
            pltpu.SemaphoreType.DMA((2,)),
            pltpu.SemaphoreType.DMA((2,)),
            pltpu.SemaphoreType.DMA((2, 2)),
            pltpu.SemaphoreType.DMA((16,)),
            pltpu.SemaphoreType.DMA((16,)),
        ],
        compiler_params=pltpu.CompilerParams(
            collective_id=0, has_side_effects=True, vmem_limit_bytes=59 << 20
        ),
        name="block",
    )(
        noisy_field.reshape(TILE, TILE, C),
        coarse_cells,
        coarse_proj,
        kernel_first,
        kernel_second,
        row(gain_first),
        row(shift_first),
        row(gain_second),
        row(shift_second),
        request_ids.reshape(128, MOST).T,
        patch_slots.reshape(1, PATCH * PATCH),
        tile_offsets.reshape(1, 2),
    )
    return got[None]


def solution(mesh):
    return jax.shard_map(
        body,
        mesh=mesh,
        in_specs=(
            P("region", "row", "col", None),
            P(("region", "row", "col"), None),
            P(),
            P(),
            P(),
            P(),
            P(),
            P(),
            P(),
            P("region", "row", "col", None, None),
            P("region", "row", "col", None),
            P("region", "row", "col", None),
        ),
        out_specs=P("region", "row", "col", None),
        check_vma=False,
    )
```

```python
import functools

import jax
import jax.numpy as jnp
from jax import lax
from jax.experimental import pallas as pl
from jax.experimental.pallas import tpu as pltpu
from jax.sharding import PartitionSpec as P

GROUPS = 32
STEP = 9
PATCH = 13
MOST = 6
TILE = 128
C = 128
CC = 640
HELD = 256
AXES = ("region", "row", "col")
MESH = pl.DeviceIdType.MESH
FLAT = pl.DeviceIdType.LOGICAL
F32 = jnp.float32
BF16 = jnp.bfloat16
PAIRS = 16


def split3(x):
    hi = x.astype(BF16)
    rest = x - hi.astype(F32)
    mid = rest.astype(BF16)
    lo = (rest - mid.astype(F32)).astype(BF16)
    return hi, mid, lo


def cubic(distance):
    near_part = (1.5 * distance - 2.5) * distance * distance + 1.0
    far_part = ((-0.5 * distance + 2.5) * distance - 4.0) * distance + 2.0
    return jnp.where(distance < 1.0, near_part, jnp.where(distance < 2.0, far_part, 0.0))


def weight_terms(point, lane, offset):
    position = (offset.astype(F32) + point.astype(F32) * STEP) / 128.0 + 1.0
    cell = lane % 16
    group = lane // 16
    weight = cubic(jnp.abs(position - cell.astype(F32)))
    weight = jnp.where(cell < PATCH, weight, 0.0)
    hi, mid, lo = (t.astype(F32) for t in split3(weight))
    return jnp.where(group < 3, hi, jnp.where(group < 5, mid, jnp.where(group < 6, lo, 0.0)))


def tap_terms(point, lane, offset):
    group = (lane * 1366) >> 16
    rest = lane - group * 48
    point = point + (rest >> 4) - 1
    cell = rest & 15
    position = (offset.astype(F32) + point.astype(F32) * STEP) / 128.0 + 1.0
    weight = cubic(jnp.abs(position - cell.astype(F32)))
    weight = jnp.where((cell < PATCH) & (point >= 0) & (point < TILE), weight, 0.0)
    hi, mid, _ = (t.astype(F32) for t in split3(weight))
    return jnp.where(group < 2, hi, jnp.where(group < 3, mid, 0.0))


def silu(v):
    return v * jax.nn.sigmoid(v)


def far_first(n):
    return (~n & 0b1010100) | ((n ^ (n >> 1)) & 0b0101010) | (~n & 1)


def kernel(
    noisy_hbm,
    cells_hbm,
    proj_hbm,
    k1_hbm,
    k2_hbm,
    g1_ref,
    s1_ref,
    g2_ref,
    s2_ref,
    ids_ref,
    slots_ref,
    off_ref,
    out,
    noisy,
    cells,
    proj,
    k1,
    k2,
    wb1,
    wb2,
    id_rows,
    id_buf,
    id_recv,
    pcat,
    rows_out,
    rows_in,
    slot_row,
    sel,
    patch,
    partial,
    row_out,
    taps,
    lhs_col,
    lhs_tap_row,
    lhs_tap_col,
    edge_sel,
    noisy_col,
    wtap,
    rows_halo,
    mixed,
    x2,
    field,
    swap,
    col_f,
    col_b,
    halo_b,
    halo_f,
    corner_out,
    corner_in,
    st_out,
    st_in,
    ld_sem,
    id_sem,
    row_sem,
    st_sem,
    halo_send,
    halo_recv,
):
    g, i, j = (lax.axis_index(a) for a in AXES)
    me = g * 32 + i * 4 + j

    loads = [
        pltpu.make_async_copy(a, b, ld_sem.at[n])
        for n, (a, b) in enumerate(
            [(cells_hbm, cells), (proj_hbm, proj), (k1_hbm, k1), (k2_hbm, k2), (noisy_hbm, noisy)]
        )
    ]
    for c in loads:
        c.start()
    barrier = pltpu.get_barrier_semaphore()

    def greet(n, c):
        pl.semaphore_signal(barrier, inc=1, device_id=me ^ far_first(n), device_id_type=FLAT)
        return c

    lax.fori_loop(0, 127, greet, 0)

    id_rows[...] = jnp.zeros_like(id_rows)
    id_rows[0:MOST, :] = ids_ref[:, 0, :].astype(F32)
    id_buf[:, 0, :] = jnp.transpose(id_rows[...])
    id_recv[0] = id_buf[me]
    pl.semaphore_wait(barrier, 127)

    def send_ids(n, c):
        k = far_first(n)
        pltpu.make_async_remote_copy(
            id_buf.at[me ^ k], id_recv.at[k], id_sem.at[0], id_sem.at[1], device_id=me ^ k, device_id_type=FLAT
        ).start()
        return c

    lax.fori_loop(0, 127, send_ids, 0)

    loads[0].wait()
    loads[1].wait()
    projected = jnp.dot(
        cells[...], proj[...], precision=lax.Precision.HIGHEST, preferred_element_type=F32
    )
    for n, term in enumerate(split3(projected)):
        pcat[:, n * 128 : (n + 1) * 128] = term
    partial[...] = jnp.zeros_like(partial)
    taps[...] = jnp.zeros_like(taps)

    slot_row[...] = jnp.full_like(slot_row, -1)
    slot_row[0:1, 0 : PATCH * PATCH] = slots_ref[...]
    slot = slot_row[0:1, :]
    owner = (slot * 10923) >> 16
    place = slot - owner * MOST
    index = place * 128 + (owner ^ me)
    index = jnp.where(slot < 0, -1, index).astype(F32)
    index = jnp.transpose(jnp.broadcast_to(index, (128, 256)))
    lane = lax.broadcasted_iota(jnp.int32, (256, 128), 1).astype(F32)
    for n in range(MOST):
        sel[:, n * 128 : (n + 1) * 128] = jnp.where(index == lane + 128.0 * n, 1.0, 0.0).astype(BF16)

    r_iota = lax.broadcasted_iota(jnp.int32, (128, 128), 0)
    l_iota = lax.broadcasted_iota(jnp.int32, (128, 128), 1)
    column = (r_iota % 16) * 8 + r_iota // 16
    lhs_col[:, 0:128] = weight_terms(column, l_iota, off_ref[0, 1]).astype(BF16)
    lhs_col[:, 128:256] = jnp.where(column == l_iota, 1.0, 0.0).astype(BF16)
    lhs_row = weight_terms(r_iota, l_iota, off_ref[0, 0]).astype(BF16)
    r_tap = lax.broadcasted_iota(jnp.int32, (128, 144), 0)
    l_tap = lax.broadcasted_iota(jnp.int32, (128, 144), 1)
    lhs_tap_row[...] = tap_terms(r_tap, l_tap, off_ref[0, 0]).astype(BF16)
    lhs_tap_col[...] = tap_terms((r_tap % 16) * 8 + r_tap // 16, l_tap, off_ref[0, 1]).astype(BF16)
    e_row = lax.broadcasted_iota(jnp.int32, (64, 256), 0)
    p_cell = lax.broadcasted_iota(jnp.int32, (64, 256), 1)
    p_row = (p_cell * 5042) >> 16
    p_col = p_cell - p_row * PATCH
    on_rows = e_row < 32
    point = jnp.where((e_row & 16) == 0, 0, TILE - 1)
    start = jnp.where(on_rows, off_ref[0, 0], off_ref[0, 1])
    position = (start.astype(F32) + point.astype(F32) * STEP) / 128.0 + 1.0
    weight = cubic(jnp.abs(position - jnp.where(on_rows, p_row, p_col).astype(F32)))
    keep = (jnp.where(on_rows, p_col, p_row) == (e_row & 15)) & (p_cell < PATCH * PATCH)
    edge_sel[...] = jnp.where(keep, weight, 0.0)

    loads[2].wait()
    loads[3].wait()
    zero_block = jnp.zeros((128, 128), BF16)
    for w, wb in ((k1, wb1), (k2, wb2)):
        for a in range(4):
            for b in range(3):
                for e in range(2):
                    block = w[a - e, b] if 0 <= a - e <= 2 else zero_block
                    wb[(a * 3 + b) * 128 : (a * 3 + b + 1) * 128, e * 128 : (e + 1) * 128] = block

    for a in range(3):
        for b in range(3):
            n = a * 3 + b
            wtap[0:128, n * 128 : (n + 1) * 128] = k1[a, b]
            wtap[128:256, n * 128 : (n + 1) * 128] = k1[a, b]

    sub = lax.broadcasted_iota(jnp.int32, (16, 128), 0)
    x2[0] = jnp.zeros((160, 128), BF16)
    x2[TILE + 1] = jnp.zeros((160, 128), BF16)
    loads[4].wait()

    def reorder(n, c):
        h0 = n * 16
        got = jnp.dot(
            lhs_col[:, 128:256],
            jnp.concatenate([noisy[h0 + q] for q in range(16)], axis=1),
            preferred_element_type=F32,
        )
        for q in range(16):
            v = got[:, q * 128 : (q + 1) * 128]
            h = h0 + q
            x2[h + 1, 16:144] = v.astype(BF16)
            x2[h + 1, 0:16] = jnp.where(sub == 0, 0.0, pltpu.roll(v[112:128], 1, 0)).astype(BF16)
            x2[h + 1, 144:160] = jnp.where(sub == 15, 0.0, pltpu.roll(v[0:16], 15, 0)).astype(BF16)
            noisy_col[0, pl.ds(h, 1), :] = v[0:1]
            noisy_col[1, pl.ds(h, 1), :] = v[127:128]
        return c

    lax.fori_loop(0, 8, reorder, 0)

    def conv_block(x, wb, t):
        y = t * (2 * PAIRS)
        lhs = []
        for q in range(PAIRS):
            parts = [
                x[y + 2 * q + a, b * 16 : b * 16 + 128] for a in range(4) for b in range(3)
            ]
            lhs.append(jnp.concatenate(parts, axis=1))
        got = jnp.dot(jnp.concatenate(lhs, axis=0), wb[...], preferred_element_type=F32)
        for q in range(PAIRS):
            for e in range(2):
                yield y + 2 * q + e, got[q * 128 : (q + 1) * 128, e * 128 : (e + 1) * 128]

    def at_row(h):
        return pl.ds(pl.multiple_of(h * 128, 128), 128)

    def conv_noisy(t, c):
        for h, v in conv_block(x2, wb1, t):
            field[at_row(h), :] = v
        return c

    def whole(ref, sem):
        return pltpu.make_async_copy(ref, ref, sem)

    whole(id_recv.at[pl.ds(1, 127)], id_sem.at[1]).wait()
    asked = id_recv[:, 0, :] - (me * HELD).astype(F32)
    row_iota = lax.broadcasted_iota(jnp.int32, (128, HELD), 1).astype(F32)
    for m in range(MOST):
        hot = jnp.where(asked[:, m : m + 1] == row_iota, 1.0, 0.0).astype(BF16)
        found = jnp.dot(hot, pcat[...], preferred_element_type=F32)
        found = found[:, 0:128] + found[:, 128:256] + found[:, 256:384]
        rows_out[:, m, :] = found
    rows_in[0] = rows_out[0]

    def send_rows(n, c):
        k = far_first(n)
        pltpu.make_async_remote_copy(
            rows_out.at[k],
            rows_in.at[k],
            row_sem.at[0],
            row_sem.at[1],
            device_id=me ^ k,
            device_id_type=FLAT,
        ).start()
        return c

    lax.fori_loop(0, 127, send_rows, 0)
    lax.fori_loop(0, 64 // PAIRS, conv_noisy, 0)
    whole(id_buf.at[pl.ds(1, 127)], id_sem.at[0]).wait()
    whole(rows_in.at[pl.ds(1, 127)], row_sem.at[1]).wait()

    terms = [jnp.concatenate(split3(rows_in[:, m, :]), axis=1) for m in range(MOST)]
    cell = jnp.dot(sel[...], jnp.concatenate(terms, axis=0), preferred_element_type=F32)
    cell = cell[:, 0:128] + cell[:, 128:256] + cell[:, 256:384]
    patch[9] = cell
    zero_tile = jnp.zeros((32, 128), BF16)

    def stack_terms(x):
        hi, mid, lo = split3(x)
        return jnp.concatenate([hi, mid, lo, hi, mid, hi, zero_tile], axis=0)

    ends = jnp.dot(
        edge_sel[...], cell, precision=lax.Precision.HIGHEST, preferred_element_type=F32
    )
    for side in range(2):
        h = side * (TILE - 1)
        rhs = jnp.concatenate([stack_terms(ends[side * 16 : side * 16 + 16]), noisy[h]], axis=0)
        row_out[side] = jnp.dot(lhs_col[...], rhs, preferred_element_type=F32).astype(BF16)
        rhs = stack_terms(ends[32 + side * 16 : 48 + side * 16])
        got = noisy_col[side] + jnp.dot(lhs_row, rhs, preferred_element_type=F32)
        col_b[side] = got.astype(BF16)
        col_f[side] = col_b[side].astype(F32)

    def form_mixed():
        for b in range(PATCH):
            rhs = stack_terms(patch[9, pl.ds(b, 16, stride=PATCH), :])
            partial[pl.ds(b, 128, stride=16), :] = jnp.dot(
                lhs_row, rhs, preferred_element_type=F32
            )

        def step(n, c):
            rhs = []
            for q in range(16):
                h = n * 16 + q
                t = stack_terms(partial[pl.ds(pl.multiple_of(h * 16, 16), 16), :])
                rhs.append(jnp.concatenate([t, noisy[h]], axis=0))
            got = jnp.dot(
                lhs_col[...], jnp.concatenate(rhs, axis=1), preferred_element_type=F32
            ).astype(BF16)
            for q in range(16):
                mixed[n * 16 + q] = got[:, q * 128 : (q + 1) * 128]
            return c

        lax.fori_loop(0, 8, step, 0)

    def neighbour(di, dj):
        return (g, (i + di + 8) % 8, (j + dj + 4) % 4)

    def row_copies(pairs, base):
        return [
            pltpu.make_async_remote_copy(
                src,
                dst,
                halo_send.at[base + n],
                halo_recv.at[base + n],
                device_id=neighbour(di, 0),
                device_id_type=MESH,
            )
            for n, ((src, dst), di) in enumerate(zip(pairs, (-1, 1)))
        ]

    def corner_copies(base):
        cs = []
        for n, (di, dj) in enumerate(((-1, -1), (-1, 1), (1, -1), (1, 1))):
            slot_n = base // 8 * 4 + n
            cs.append(
                pltpu.make_async_remote_copy(
                    corner_out.at[slot_n],
                    corner_in.at[slot_n],
                    halo_send.at[base + 4 + n],
                    halo_recv.at[base + 4 + n],
                    device_id=neighbour(di, dj),
                    device_id_type=MESH,
                )
            )
        return cs

    def col_copies(base):
        cs = []
        for n, dj in enumerate((-1, 1)):
            slot_n = base // 8 * 2 + n
            cs.append(
                pltpu.make_async_remote_copy(
                    col_b.at[slot_n],
                    halo_b.at[slot_n],
                    halo_send.at[base + 2 + n],
                    halo_recv.at[base + 2 + n],
                    device_id=neighbour(0, dj),
                    device_id_type=MESH,
                )
            )
        return cs

    def put_corners(base):
        s = base // 8 * 4
        for n, (side, h) in enumerate(((0, 0), (1, 0), (0, 127), (1, 127))):
            corner_out[s + n] = jnp.broadcast_to(col_f[side, h : h + 1, :], (8, 128))

    def put_columns(base):
        s = base // 8 * 2
        for side in range(2):
            col_b[s + side] = col_f[side].astype(BF16)

    left_ok = jnp.where(j > 0, 1.0, 0.0)
    right_ok = jnp.where(j < 3, 1.0, 0.0)
    up_ok = jnp.where(i > 0, 1.0, 0.0)
    down_ok = jnp.where(i < 7, 1.0, 0.0)

    def edge(x, n):
        last = pltpu.roll(x[n, 128:144].astype(F32), 1, 0)
        x[n, 0:16] = jnp.where(sub == 0, halo_f[0, pl.ds(n + 7, 1), :], last).astype(BF16)
        first = pltpu.roll(x[n, 16:32].astype(F32), 15, 0)
        x[n, 144:160] = jnp.where(sub == 15, halo_f[1, pl.ds(n + 7, 1), :], first).astype(BF16)

    def take_columns(base, copies):
        for c in copies:
            c.wait()
        s2 = base // 8 * 2
        halo_f[0, 8:136, :] = halo_b[s2 + 1].astype(F32) * left_ok
        halo_f[1, 8:136, :] = halo_b[s2 + 0].astype(F32) * right_ok

    def take_corners(base):
        s4 = base // 8 * 4
        halo_f[0, 0:8, :] = corner_in[s4 + 3] * (left_ok * up_ok)
        halo_f[1, 0:8, :] = corner_in[s4 + 2] * (right_ok * up_ok)
        halo_f[0, 136:144, :] = corner_in[s4 + 1] * (left_ok * down_ok)
        halo_f[1, 136:144, :] = corner_in[s4 + 0] * (right_ok * down_ok)

    put_corners(0)
    mid = pl.ds(16, 128)
    rows1 = row_copies(
        [(row_out.at[0], rows_halo.at[1, mid]), (row_out.at[1], rows_halo.at[0, mid])], 0
    ) + corner_copies(0)
    cols1 = col_copies(0)
    for c in rows1 + cols1:
        c.start()

    hi, low, _ = split3(cell)
    tapped = jnp.dot(jnp.concatenate([hi, low], axis=1), wtap[...], preferred_element_type=F32)
    for n in range(9):
        patch[n] = tapped[:, n * 128 : (n + 1) * 128]
    for b in range(3):
        rhs = []
        for col in range(PATCH):
            parts = [
                patch[a * 3 + b, pl.ds(col, 16, stride=PATCH), :] for a in range(3)
            ]
            hi, low, _ = split3(jnp.concatenate(parts, axis=0))
            rhs.append(jnp.concatenate([hi, low, hi], axis=0))
        got = jnp.dot(
            lhs_tap_row[...], jnp.concatenate(rhs, axis=1), preferred_element_type=F32
        )
        for col in range(PATCH):
            taps[pl.ds(b * 16 + col, 128, stride=48), :] = got[:, col * 128 : (col + 1) * 128]

    def sum_up(carry, v):
        total, square = carry
        v3 = v.reshape(v.shape[0] // 8, 8, 128)
        return total + jnp.sum(v3, axis=0), square + jnp.sum(v3 * v3, axis=0)

    def add_taps(n, carry):
        rhs = []
        for q in range(16):
            h = n * 16 + q
            hi, low, _ = split3(taps[pl.ds(pl.multiple_of(h * 48, 16), 48), :])
            rhs.append(jnp.concatenate([hi, low, hi], axis=0))
        got = jnp.dot(
            lhs_tap_col[...], jnp.concatenate(rhs, axis=1), preferred_element_type=F32
        )
        for q in range(16):
            h = n * 16 + q
            v = field[at_row(h), :] + got[:, q * 128 : (q + 1) * 128]
            field[at_row(h), :] = v
            carry = sum_up(carry, v)
        return carry

    zero8 = jnp.zeros((8, 128), F32)
    sums = lax.fori_loop(0, 8, add_taps, (zero8, zero8))

    def correct(carry, place, delta):
        old = field[place, :]
        new = old + delta
        field[place, :] = new
        d3 = delta.reshape(16, 8, 128)
        q3 = (new * new - old * old).reshape(16, 8, 128)
        return carry[0] + jnp.sum(d3, axis=0), carry[1] + jnp.sum(q3, axis=0)

    def take_rows1():
        for c in rows1:
            c.wait()
        for side, ok in ((0, up_ok), (1, down_ok)):
            v = rows_halo[side, 16:144].astype(F32) * ok
            rows_halo[side, 16:144] = v.astype(BF16)
            last = pltpu.roll(v[112:128], 1, 0)
            rows_halo[side, 0:16] = jnp.where(sub == 0, 0.0, last).astype(BF16)
            first = pltpu.roll(v[0:16], 15, 0)
            rows_halo[side, 144:160] = jnp.where(sub == 15, 0.0, first).astype(BF16)

    take_columns(0, cols1)
    take_rows1()
    take_corners(0)
    for side in range(2):
        lhs = jnp.concatenate([halo_f[side, 7 + a : 135 + a, :].astype(BF16) for a in range(3)], axis=1)
        rhs = jnp.concatenate([k1[a, 2 * side] for a in range(3)], axis=0)
        delta = jnp.dot(lhs, rhs, preferred_element_type=F32)
        sums = correct(sums, pl.ds(side * 127, 128, stride=128), delta)
    for side in range(2):
        lhs = jnp.concatenate([rows_halo[side, b * 16 : b * 16 + 128] for b in range(3)], axis=1)
        rhs = jnp.concatenate([k1[2 * side, b] for b in range(3)], axis=0)
        delta = jnp.dot(lhs, rhs, preferred_element_type=F32)
        sums = correct(sums, pl.ds(side * 127 * 128, 128), delta)

    def convolve(columns, rows):
        def step(t, carry):
            for h, v in conv_block(x2, wb2, t):
                field[at_row(h), :] = v
                carry = sum_up(carry, v)
            return carry

        def edges(n, c):
            edge(x2, n)
            return c

        blocks = 64 // PAIRS
        take_columns(8, columns)
        lax.fori_loop(1, 129, edges, 0, unroll=8)
        sums = lax.fori_loop(1, blocks - 1, step, (zero8, zero8))
        for c in rows:
            c.wait()
        take_corners(8)

        @pl.when(i == 0)
        def _():
            x2[0, 16:144] = jnp.zeros((128, 128), BF16)

        @pl.when(i == 7)
        def _():
            x2[129, 16:144] = jnp.zeros((128, 128), BF16)

        edge(x2, 0)
        edge(x2, 129)
        return lax.fori_loop(0, 2, lambda n, c: step(n * (blocks - 1), c), sums)

    group_ones = jnp.where(r_iota // 4 == l_iota // 4, 1.0, 0.0)
    number = float(TILE * TILE * 32 * (C // GROUPS))

    def norm_terms(n, sums, gain, shift, meanwhile=None):
        total, square = (jnp.sum(s, axis=0, keepdims=True) for s in sums)
        sub8 = lax.broadcasted_iota(jnp.int32, (8, 128), 0)
        mine = jnp.where(sub8 == 0, total, jnp.where(sub8 == 1, square, 0.0))
        st_out[n] = mine
        st_in[n, 0] = mine
        def send(t, c):
            k = far_first(t)
            pltpu.make_async_remote_copy(
                st_out.at[n],
                st_in.at[n, k],
                st_sem.at[n, 0],
                st_sem.at[n, 1],
                device_id=me ^ k,
                device_id_type=FLAT,
            ).start()
            return c

        lax.fori_loop(96, 127, send, 0)
        if meanwhile is not None:
            meanwhile()
        whole(st_in.at[n, pl.ds(1, 31)], st_sem.at[n, 1]).wait()
        both = jnp.sum(st_in[n], axis=0)
        both = jnp.dot(
            both, group_ones, precision=lax.Precision.HIGHEST, preferred_element_type=F32
        )
        mean = both[0:1] / number
        spread = both[1:2] / number - mean * mean
        scale = lax.rsqrt(spread + 1e-05) * gain
        whole(st_in.at[n, pl.ds(1, 31)], st_sem.at[n, 0]).wait()
        return scale, shift - mean * scale

    scale, offset = norm_terms(0, sums, g1_ref[...], s1_ref[...], form_mixed)

    def hide(h, lo, hi):
        v = field[pl.ds(pl.multiple_of(h * 128 + lo * 16, 16), (hi - lo) * 16), :]
        m = silu(v * scale + offset).astype(BF16)
        x2[h + 1, 16 + lo * 16 : 16 + hi * 16] = m
        return m.astype(F32)

    def hide_ends(h, c):
        a = hide(h, 0, 1)
        b = hide(h, 7, 8)
        col_f[0, pl.ds(h, 1), :] = a[0:1]
        col_f[1, pl.ds(h, 1), :] = b[15:16]
        return c

    def hide_rest(h, c):
        hide(h, 1, 7)
        return c

    lax.fori_loop(0, 128, hide_ends, 0, unroll=8)
    put_columns(8)
    cols2 = col_copies(8)
    for c in cols2:
        c.start()
    hide_rest(0, 0)
    hide_rest(127, 0)
    halo2 = row_copies(
        [(x2.at[1, mid], x2.at[129, mid]), (x2.at[128, mid], x2.at[0, mid])], 8
    ) + corner_copies(8)
    put_corners(8)
    for c in halo2:
        c.start()
    lax.fori_loop(1, 127, hide_rest, 0, unroll=7)

    sums = convolve(cols2, halo2)
    scale2, offset2 = norm_terms(1, sums, g2_ref[...], s2_ref[...])

    def finish(n, c):
        for q in range(8):
            h = n * 8 + q
            v = silu(field[at_row(h), :] * scale2 + offset2)
            v = mixed[h].astype(F32) + v
            for s in range(8):
                swap[q, pl.ds(s, 16, stride=8), :] = v[s * 16 : (s + 1) * 16]
        for q in range(8):
            out[n * 8 + q] = swap[q].astype(BF16)
        return c

    lax.fori_loop(0, 16, finish, 0)
    whole(rows_in.at[pl.ds(1, 127)], row_sem.at[0]).wait()


def body(
    noisy_field,
    coarse_cells,
    coarse_proj,
    kernel_first,
    kernel_second,
    gain_first,
    shift_first,
    gain_second,
    shift_second,
    request_ids,
    patch_slots,
    tile_offsets,
):
    hbm = pl.BlockSpec(memory_space=pl.ANY)
    vmem = pl.BlockSpec(memory_space=pltpu.VMEM)
    smem = pl.BlockSpec(memory_space=pltpu.SMEM)
    row = lambda v: v.reshape(1, C)
    got = pl.pallas_call(
        kernel,
        out_shape=pltpu.VMEM((TILE, TILE, C), BF16),
        in_specs=[hbm] * 5 + [vmem] * 6 + [smem],
        out_specs=vmem,
        scratch_shapes=[
            pltpu.VMEM((TILE, TILE, C), BF16),
            pltpu.VMEM((HELD, CC), F32),
            pltpu.VMEM((CC, C), F32),
            pltpu.VMEM((3, 3, C, C), BF16),
            pltpu.VMEM((3, 3, C, C), BF16),
            pltpu.VMEM((12 * C, 2 * C), BF16),
            pltpu.VMEM((12 * C, 2 * C), BF16),
            pltpu.VMEM((128, 128), F32),
            pltpu.VMEM((128, 1, 128), F32),
            pltpu.VMEM((128, 1, 128), F32),
            pltpu.VMEM((HELD, 3 * C), BF16),
            pltpu.VMEM((128, MOST, C), F32),
            pltpu.VMEM((128, MOST, C), F32),
            pltpu.VMEM((8, 256), jnp.int32),
            pltpu.VMEM((256, MOST * 128), BF16),
            pltpu.VMEM((10, 256, C), F32),
            pltpu.VMEM((TILE * 16, C), F32),
            pltpu.VMEM((2, 128, C), BF16),
            pltpu.VMEM((TILE * 48, C), F32),
            pltpu.VMEM((128, 256), BF16),
            pltpu.VMEM((128, 144), BF16),
            pltpu.VMEM((128, 144), BF16),
            pltpu.VMEM((64, 256), F32),
            pltpu.VMEM((2, 128, C), F32),
            pltpu.VMEM((256, 9 * C), BF16),
            pltpu.VMEM((2, 160, C), BF16),
            pltpu.VMEM((TILE, TILE, C), BF16),
            pltpu.VMEM((TILE + 2, 160, C), BF16),
            pltpu.VMEM((TILE * TILE, C), F32),
            pltpu.VMEM((8, TILE, C), F32),
            pltpu.VMEM((2, TILE, C), F32),
            pltpu.VMEM((4, TILE, C), BF16),
            pltpu.VMEM((4, TILE, C), BF16),
            pltpu.VMEM((2, 144, C), F32),
            pltpu.VMEM((8, 8, C), F32),
            pltpu.VMEM((8, 8, C), F32),
            pltpu.VMEM((2, 8, C), F32),
            pltpu.VMEM((2, 32, 8, C), F32),
            pltpu.SemaphoreType.DMA((5,)),
            pltpu.SemaphoreType.DMA((2,)),
            pltpu.SemaphoreType.DMA((2,)),
            pltpu.SemaphoreType.DMA((2, 2)),
            pltpu.SemaphoreType.DMA((16,)),
            pltpu.SemaphoreType.DMA((16,)),
        ],
        compiler_params=pltpu.CompilerParams(
            collective_id=0, has_side_effects=True, vmem_limit_bytes=59 << 20
        ),
        name="block",
    )(
        noisy_field.reshape(TILE, TILE, C),
        coarse_cells,
        coarse_proj,
        kernel_first,
        kernel_second,
        row(gain_first),
        row(shift_first),
        row(gain_second),
        row(shift_second),
        request_ids.transpose(0, 1, 4, 2, 3).reshape(MOST, 1, 128),
        patch_slots.reshape(1, PATCH * PATCH),
        tile_offsets.reshape(1, 2),
    )
    return got[None]


def solution(mesh):
    return jax.shard_map(
        body,
        mesh=mesh,
        in_specs=(
            P("region", "row", "col", None),
            P(("region", "row", "col"), None),
            P(),
            P(),
            P(),
            P(),
            P(),
            P(),
            P(),
            P("region", "row", "col", None, None),
            P("region", "row", "col", None),
            P("region", "row", "col", None),
        ),
        out_specs=P("region", "row", "col", None),
        check_vma=False,
    )
```

```python
import functools

import jax
import jax.numpy as jnp
from jax import lax
from jax.experimental import pallas as pl
from jax.experimental.pallas import tpu as pltpu
from jax.sharding import PartitionSpec as P

GROUPS = 32
STEP = 9
PATCH = 13
MOST = 6
TILE = 128
C = 128
CC = 640
HELD = 256
AXES = ("region", "row", "col")
MESH = pl.DeviceIdType.MESH
FLAT = pl.DeviceIdType.LOGICAL
F32 = jnp.float32
BF16 = jnp.bfloat16
PAIRS = 16


def split3(x):
    hi = x.astype(BF16)
    rest = x - hi.astype(F32)
    mid = rest.astype(BF16)
    lo = (rest - mid.astype(F32)).astype(BF16)
    return hi, mid, lo


def split2(x):
    hi = x.astype(BF16)
    return hi, (x - hi.astype(F32)).astype(BF16)


def cubic(distance):
    near_part = (1.5 * distance - 2.5) * distance * distance + 1.0
    far_part = ((-0.5 * distance + 2.5) * distance - 4.0) * distance + 2.0
    return jnp.where(distance < 1.0, near_part, jnp.where(distance < 2.0, far_part, 0.0))


def weight_terms(point, lane, offset):
    position = (offset.astype(F32) + point.astype(F32) * STEP) / 128.0 + 1.0
    cell = lane % 16
    group = lane // 16
    weight = cubic(jnp.abs(position - cell.astype(F32)))
    weight = jnp.where(cell < PATCH, weight, 0.0)
    hi, mid, lo = (t.astype(F32) for t in split3(weight))
    return jnp.where(group < 3, hi, jnp.where(group < 5, mid, jnp.where(group < 6, lo, 0.0)))


def tap_terms(point, lane, offset):
    group = (lane * 1366) >> 16
    rest = lane - group * 48
    point = point + (rest >> 4) - 1
    cell = rest & 15
    position = (offset.astype(F32) + point.astype(F32) * STEP) / 128.0 + 1.0
    weight = cubic(jnp.abs(position - cell.astype(F32)))
    weight = jnp.where((cell < PATCH) & (point >= 0) & (point < TILE), weight, 0.0)
    hi, mid, _ = (t.astype(F32) for t in split3(weight))
    return jnp.where(group < 2, hi, jnp.where(group < 3, mid, 0.0))


def silu(v):
    return v * jax.nn.sigmoid(v)


def far_first(n):
    return (~n & 0b1010100) | ((n ^ (n >> 1)) & 0b0101010) | (~n & 1)


def kernel(
    noisy_hbm,
    cells_hbm,
    proj_hbm,
    k1_hbm,
    k2_hbm,
    g1_ref,
    s1_ref,
    g2_ref,
    s2_ref,
    ids_ref,
    slots_ref,
    off_ref,
    out,
    noisy,
    cells,
    proj,
    k1,
    k2,
    wb1,
    wb2,
    id_rows,
    id_buf,
    id_recv,
    pcat,
    rows_out,
    rows_in,
    slot_row,
    sel,
    patch,
    partial,
    row_out,
    taps,
    lhs_col,
    lhs_tap_row,
    lhs_tap_col,
    edge_rows,
    noisy_col,
    wtap,
    rows_halo,
    mixed,
    x2,
    field,
    swap,
    col_f,
    col_b,
    halo_b,
    halo_f,
    corner_out,
    corner_in,
    st_out,
    st_in,
    ld_sem,
    id_sem,
    row_sem,
    st_sem,
    halo_send,
    halo_recv,
):
    g, i, j = (lax.axis_index(a) for a in AXES)
    me = g * 32 + i * 4 + j

    loads = [
        pltpu.make_async_copy(a, b, ld_sem.at[n])
        for n, (a, b) in enumerate(
            [(cells_hbm, cells), (proj_hbm, proj), (k1_hbm, k1), (k2_hbm, k2), (noisy_hbm, noisy)]
        )
    ]
    for c in loads:
        c.start()
    barrier = pltpu.get_barrier_semaphore()

    def greet(n, c):
        pl.semaphore_signal(barrier, inc=1, device_id=me ^ far_first(n), device_id_type=FLAT)
        return c

    lax.fori_loop(0, 127, greet, 0)

    id_rows[...] = jnp.zeros_like(id_rows)
    id_rows[0:MOST, :] = ids_ref[:, 0, :].astype(F32)
    id_buf[:, 0, :] = jnp.transpose(id_rows[...])
    id_recv[0] = id_buf[me]
    pl.semaphore_wait(barrier, 127)

    def send_ids(n, c):
        k = far_first(n)
        pltpu.make_async_remote_copy(
            id_buf.at[me ^ k], id_recv.at[k], id_sem.at[0], id_sem.at[1], device_id=me ^ k, device_id_type=FLAT
        ).start()
        return c

    lax.fori_loop(0, 127, send_ids, 0)

    loads[0].wait()
    loads[1].wait()
    projected = jnp.dot(
        cells[...], proj[...], precision=lax.Precision.HIGHEST, preferred_element_type=F32
    )
    for n, term in enumerate(split2(projected)):
        pcat[:, n * 128 : (n + 1) * 128] = term
    partial[...] = jnp.zeros_like(partial)
    taps[...] = jnp.zeros_like(taps)

    slot_row[...] = jnp.full_like(slot_row, -1)
    slot_row[0:1, 0 : PATCH * PATCH] = slots_ref[...]
    slot = slot_row[0:1, :]
    owner = (slot * 10923) >> 16
    place = slot - owner * MOST
    index = place * 128 + (owner ^ me)
    index = jnp.where(slot < 0, -1, index).astype(F32)
    index = jnp.transpose(jnp.broadcast_to(index, (128, 256)))
    lane = lax.broadcasted_iota(jnp.int32, (256, 128), 1).astype(F32)
    for n in range(MOST):
        sel[:, n * 128 : (n + 1) * 128] = jnp.where(index == lane + 128.0 * n, 1.0, 0.0).astype(BF16)

    r_iota = lax.broadcasted_iota(jnp.int32, (128, 128), 0)
    l_iota = lax.broadcasted_iota(jnp.int32, (128, 128), 1)
    column = (r_iota % 16) * 8 + r_iota // 16
    lhs_col[:, 0:128] = weight_terms(column, l_iota, off_ref[0, 1]).astype(BF16)
    lhs_col[:, 128:256] = jnp.where(column == l_iota, 1.0, 0.0).astype(BF16)
    lhs_row = weight_terms(r_iota, l_iota, off_ref[0, 0]).astype(BF16)
    r_tap = lax.broadcasted_iota(jnp.int32, (128, 144), 0)
    l_tap = lax.broadcasted_iota(jnp.int32, (128, 144), 1)
    lhs_tap_row[...] = tap_terms(r_tap, l_tap, off_ref[0, 0]).astype(BF16)
    lhs_tap_col[...] = tap_terms((r_tap % 16) * 8 + r_tap // 16, l_tap, off_ref[0, 1]).astype(BF16)
    e_row = lax.broadcasted_iota(jnp.int32, (64, 256), 0)
    p_cell = lax.broadcasted_iota(jnp.int32, (64, 256), 1)
    p_row = (p_cell * 5042) >> 16
    p_col = p_cell - p_row * PATCH
    on_rows = e_row < 32
    point = jnp.where((e_row & 16) == 0, 0, TILE - 1)
    start = jnp.where(on_rows, off_ref[0, 0], off_ref[0, 1])
    position = (start.astype(F32) + point.astype(F32) * STEP) / 128.0 + 1.0
    weight = cubic(jnp.abs(position - jnp.where(on_rows, p_row, p_col).astype(F32)))
    keep = (jnp.where(on_rows, p_col, p_row) == (e_row & 15)) & (p_cell < PATCH * PATCH)
    edge_terms = jnp.concatenate(split2(jnp.where(keep, weight, 0.0)), axis=0)
    edge_rows[...] = jnp.dot(edge_terms, sel[...], preferred_element_type=F32).astype(BF16)

    loads[2].wait()
    loads[3].wait()
    zero_block = jnp.zeros((128, 128), BF16)
    for w, wb in ((k1, wb1), (k2, wb2)):
        for a in range(4):
            for b in range(3):
                for e in range(2):
                    block = w[a - e, b] if 0 <= a - e <= 2 else zero_block
                    wb[(a * 3 + b) * 128 : (a * 3 + b + 1) * 128, e * 128 : (e + 1) * 128] = block

    for a in range(3):
        for b in range(3):
            n = a * 3 + b
            wtap[0:128, n * 128 : (n + 1) * 128] = k1[a, b]
            wtap[128:256, n * 128 : (n + 1) * 128] = k1[a, b]

    sub = lax.broadcasted_iota(jnp.int32, (16, 128), 0)
    x2[0] = jnp.zeros((160, 128), BF16)
    x2[TILE + 1] = jnp.zeros((160, 128), BF16)
    loads[4].wait()

    def reorder(n, c):
        h0 = n * 16
        got = jnp.dot(
            lhs_col[:, 128:256],
            jnp.concatenate([noisy[h0 + q] for q in range(16)], axis=1),
            preferred_element_type=F32,
        )
        for q in range(16):
            v = got[:, q * 128 : (q + 1) * 128]
            h = h0 + q
            x2[h + 1, 16:144] = v.astype(BF16)
            x2[h + 1, 0:16] = jnp.where(sub == 0, 0.0, pltpu.roll(v[112:128], 1, 0)).astype(BF16)
            x2[h + 1, 144:160] = jnp.where(sub == 15, 0.0, pltpu.roll(v[0:16], 15, 0)).astype(BF16)
            noisy_col[0, pl.ds(h, 1), :] = v[0:1]
            noisy_col[1, pl.ds(h, 1), :] = v[127:128]
        return c

    lax.fori_loop(0, 8, reorder, 0)

    def conv_block(x, wb, t):
        y = t * (2 * PAIRS)
        lhs = []
        for q in range(PAIRS):
            parts = [
                x[y + 2 * q + a, b * 16 : b * 16 + 128] for a in range(4) for b in range(3)
            ]
            lhs.append(jnp.concatenate(parts, axis=1))
        got = jnp.dot(jnp.concatenate(lhs, axis=0), wb[...], preferred_element_type=F32)
        for q in range(PAIRS):
            for e in range(2):
                yield y + 2 * q + e, got[q * 128 : (q + 1) * 128, e * 128 : (e + 1) * 128]

    def at_row(h):
        return pl.ds(pl.multiple_of(h * 128, 128), 128)

    def conv_noisy(t, c):
        for h, v in conv_block(x2, wb1, t):
            field[at_row(h), :] = v
        return c

    def whole(ref, sem):
        return pltpu.make_async_copy(ref, ref, sem)

    whole(id_recv.at[pl.ds(1, 127)], id_sem.at[1]).wait()
    asked = id_recv[:, 0, :] - (me * HELD).astype(F32)
    row_iota = lax.broadcasted_iota(jnp.int32, (128, HELD), 1).astype(F32)
    hot = [
        jnp.where(asked[:, m : m + 1] == row_iota, 1.0, 0.0).astype(BF16) for m in range(MOST)
    ]
    found = jnp.dot(jnp.concatenate(hot, axis=0), pcat[...], preferred_element_type=F32)
    found = found[:, 0:128] + found[:, 128:256]
    for m in range(MOST):
        rows_out[:, m, :] = found[m * 128 : (m + 1) * 128]
    rows_in[0] = rows_out[0]

    def send_rows(n, c):
        k = far_first(n)
        pltpu.make_async_remote_copy(
            rows_out.at[k],
            rows_in.at[k],
            row_sem.at[0],
            row_sem.at[1],
            device_id=me ^ k,
            device_id_type=FLAT,
        ).start()
        return c

    lax.fori_loop(0, 127, send_rows, 0)
    lax.fori_loop(0, 64 // PAIRS, conv_noisy, 0)
    whole(id_buf.at[pl.ds(1, 127)], id_sem.at[0]).wait()
    whole(rows_in.at[pl.ds(1, 127)], row_sem.at[1]).wait()

    terms = [jnp.concatenate(split2(rows_in[:, m, :]), axis=1) for m in range(MOST)]
    terms = jnp.concatenate(terms, axis=0)
    zero_tile = jnp.zeros((32, 128), BF16)

    def stack_terms(x):
        hi, mid, lo = split3(x)
        return jnp.concatenate([hi, mid, lo, hi, mid, hi, zero_tile], axis=0)

    got = jnp.dot(edge_rows[...], terms, preferred_element_type=F32)
    got = got[:, 0:128] + got[:, 128:256]
    ends = got[0:64] + got[64:128]
    for side in range(2):
        h = side * (TILE - 1)
        rhs = jnp.concatenate([stack_terms(ends[side * 16 : side * 16 + 16]), noisy[h]], axis=0)
        row_out[side] = jnp.dot(lhs_col[...], rhs, preferred_element_type=F32).astype(BF16)
        rhs = stack_terms(ends[32 + side * 16 : 48 + side * 16])
        got = noisy_col[side] + jnp.dot(lhs_row, rhs, preferred_element_type=F32)
        col_b[side] = got.astype(BF16)
        col_f[side] = col_b[side].astype(F32)

    def form_mixed():
        for b in range(PATCH):
            rhs = stack_terms(patch[9, pl.ds(b, 16, stride=PATCH), :])
            partial[pl.ds(b, 128, stride=16), :] = jnp.dot(
                lhs_row, rhs, preferred_element_type=F32
            )

        def step(n, c):
            rhs = []
            for q in range(16):
                h = n * 16 + q
                t = stack_terms(partial[pl.ds(pl.multiple_of(h * 16, 16), 16), :])
                rhs.append(jnp.concatenate([t, noisy[h]], axis=0))
            got = jnp.dot(
                lhs_col[...], jnp.concatenate(rhs, axis=1), preferred_element_type=F32
            ).astype(BF16)
            for q in range(16):
                mixed[n * 16 + q] = got[:, q * 128 : (q + 1) * 128]
            return c

        lax.fori_loop(0, 8, step, 0)

    def neighbour(di, dj):
        return (g, (i + di + 8) % 8, (j + dj + 4) % 4)

    def row_copies(pairs, base):
        return [
            pltpu.make_async_remote_copy(
                src,
                dst,
                halo_send.at[base + n],
                halo_recv.at[base + n],
                device_id=neighbour(di, 0),
                device_id_type=MESH,
            )
            for n, ((src, dst), di) in enumerate(zip(pairs, (-1, 1)))
        ]

    def corner_copies(base):
        cs = []
        for n, (di, dj) in enumerate(((-1, -1), (-1, 1), (1, -1), (1, 1))):
            slot_n = base // 8 * 4 + n
            cs.append(
                pltpu.make_async_remote_copy(
                    corner_out.at[slot_n],
                    corner_in.at[slot_n],
                    halo_send.at[base + 4 + n],
                    halo_recv.at[base + 4 + n],
                    device_id=neighbour(di, dj),
                    device_id_type=MESH,
                )
            )
        return cs

    def col_copies(base):
        cs = []
        for n, dj in enumerate((-1, 1)):
            slot_n = base // 8 * 2 + n
            cs.append(
                pltpu.make_async_remote_copy(
                    col_b.at[slot_n],
                    halo_b.at[slot_n],
                    halo_send.at[base + 2 + n],
                    halo_recv.at[base + 2 + n],
                    device_id=neighbour(0, dj),
                    device_id_type=MESH,
                )
            )
        return cs

    def put_corners(base):
        s = base // 8 * 4
        for n, (side, h) in enumerate(((0, 0), (1, 0), (0, 127), (1, 127))):
            corner_out[s + n] = jnp.broadcast_to(col_f[side, h : h + 1, :], (8, 128))

    def put_columns(base):
        s = base // 8 * 2
        for side in range(2):
            col_b[s + side] = col_f[side].astype(BF16)

    left_ok = jnp.where(j > 0, 1.0, 0.0)
    right_ok = jnp.where(j < 3, 1.0, 0.0)
    up_ok = jnp.where(i > 0, 1.0, 0.0)
    down_ok = jnp.where(i < 7, 1.0, 0.0)

    def take_columns(base, copies):
        for c in copies:
            c.wait()
        s2 = base // 8 * 2
        halo_f[0, 8:136, :] = halo_b[s2 + 1].astype(F32) * left_ok
        halo_f[1, 8:136, :] = halo_b[s2 + 0].astype(F32) * right_ok

    def take_corners(base):
        s4 = base // 8 * 4
        halo_f[0, 0:8, :] = corner_in[s4 + 3] * (left_ok * up_ok)
        halo_f[1, 0:8, :] = corner_in[s4 + 2] * (right_ok * up_ok)
        halo_f[0, 136:144, :] = corner_in[s4 + 1] * (left_ok * down_ok)
        halo_f[1, 136:144, :] = corner_in[s4 + 0] * (right_ok * down_ok)

    put_corners(0)
    mid = pl.ds(16, 128)
    rows1 = row_copies(
        [(row_out.at[0], rows_halo.at[1, mid]), (row_out.at[1], rows_halo.at[0, mid])], 0
    ) + corner_copies(0)
    cols1 = col_copies(0)
    for c in rows1[2:] + rows1[:2] + cols1:
        c.start()

    cell = jnp.dot(sel[...], terms, preferred_element_type=F32)
    cell = cell[:, 0:128] + cell[:, 128:256]
    patch[9] = cell
    hi, low = split2(cell)
    tapped = jnp.dot(jnp.concatenate([hi, low], axis=1), wtap[...], preferred_element_type=F32)
    for n in range(9):
        patch[n] = tapped[:, n * 128 : (n + 1) * 128]
    for b in range(3):
        rhs = []
        for col in range(PATCH):
            parts = [
                patch[a * 3 + b, pl.ds(col, 16, stride=PATCH), :] for a in range(3)
            ]
            hi, low = split2(jnp.concatenate(parts, axis=0))
            rhs.append(jnp.concatenate([hi, low, hi], axis=0))
        got = jnp.dot(
            lhs_tap_row[...], jnp.concatenate(rhs, axis=1), preferred_element_type=F32
        )
        for col in range(PATCH):
            taps[pl.ds(b * 16 + col, 128, stride=48), :] = got[:, col * 128 : (col + 1) * 128]

    def sum_up(carry, v):
        total, square = carry
        v3 = v.reshape(v.shape[0] // 8, 8, 128)
        return total + jnp.sum(v3, axis=0), square + jnp.sum(v3 * v3, axis=0)

    def add_taps(n, carry):
        rhs = []
        for q in range(16):
            h = n * 16 + q
            hi, low = split2(taps[pl.ds(pl.multiple_of(h * 48, 16), 48), :])
            rhs.append(jnp.concatenate([hi, low, hi], axis=0))
        got = jnp.dot(
            lhs_tap_col[...], jnp.concatenate(rhs, axis=1), preferred_element_type=F32
        )
        for q in range(16):
            h = n * 16 + q
            v = field[at_row(h), :] + got[:, q * 128 : (q + 1) * 128]
            field[at_row(h), :] = v
            carry = sum_up(carry, v)
        return carry

    zero8 = jnp.zeros((8, 128), F32)
    sums = lax.fori_loop(0, 8, add_taps, (zero8, zero8))

    def correct(carry, place, delta):
        old = field[place, :]
        new = old + delta
        field[place, :] = new
        d3 = delta.reshape(16, 8, 128)
        q3 = (new * new - old * old).reshape(16, 8, 128)
        return carry[0] + jnp.sum(d3, axis=0), carry[1] + jnp.sum(q3, axis=0)

    def add_borders(base, rows, columns, k, carry):
        n = base // 8 * 2
        take_columns(base, columns)
        for c in rows:
            c.wait()
        take_corners(base)
        for side, ok in ((0, up_ok), (1, down_ok)):
            v = rows_halo[n + side, 16:144].astype(F32) * ok
            rows_halo[n + side, 16:144] = v.astype(BF16)
            last = pltpu.roll(v[112:128], 1, 0)
            rows_halo[n + side, 0:16] = jnp.where(sub == 0, 0.0, last).astype(BF16)
            first = pltpu.roll(v[0:16], 15, 0)
            rows_halo[n + side, 144:160] = jnp.where(sub == 15, 0.0, first).astype(BF16)
        for side in range(2):
            lhs = [halo_f[side, 7 + a : 135 + a, :].astype(BF16) for a in range(3)]
            rhs = jnp.concatenate([k[a, 2 * side] for a in range(3)], axis=0)
            delta = jnp.dot(jnp.concatenate(lhs, axis=1), rhs, preferred_element_type=F32)
            carry = correct(carry, pl.ds(side * 127, 128, stride=128), delta)
        for side in range(2):
            lhs = [rows_halo[n + side, b * 16 : b * 16 + 128] for b in range(3)]
            rhs = jnp.concatenate([k[2 * side, b] for b in range(3)], axis=0)
            delta = jnp.dot(jnp.concatenate(lhs, axis=1), rhs, preferred_element_type=F32)
            carry = correct(carry, pl.ds(side * 127 * 128, 128), delta)
        return carry

    sums = add_borders(0, rows1, cols1, k1, sums)

    group_ones = jnp.where(r_iota // 4 == l_iota // 4, 1.0, 0.0)
    number = float(TILE * TILE * 32 * (C // GROUPS))

    def norm_terms(n, sums, gain, shift, meanwhile=None):
        total, square = (jnp.sum(s, axis=0, keepdims=True) for s in sums)
        sub8 = lax.broadcasted_iota(jnp.int32, (8, 128), 0)
        mine = jnp.where(sub8 == 0, total, jnp.where(sub8 == 1, square, 0.0))
        st_out[n] = mine
        st_in[n, 0] = mine
        def send(t, c):
            k = far_first(t)
            pltpu.make_async_remote_copy(
                st_out.at[n],
                st_in.at[n, k],
                st_sem.at[n, 0],
                st_sem.at[n, 1],
                device_id=me ^ k,
                device_id_type=FLAT,
            ).start()
            return c

        lax.fori_loop(96, 127, send, 0)
        if meanwhile is not None:
            meanwhile()
        whole(st_in.at[n, pl.ds(1, 31)], st_sem.at[n, 1]).wait()
        both = jnp.sum(st_in[n], axis=0)
        both = jnp.dot(
            both, group_ones, precision=lax.Precision.HIGHEST, preferred_element_type=F32
        )
        mean = both[0:1] / number
        spread = both[1:2] / number - mean * mean
        scale = lax.rsqrt(spread + 1e-05) * gain
        whole(st_in.at[n, pl.ds(1, 31)], st_sem.at[n, 0]).wait()
        return scale, shift - mean * scale

    scale, offset = norm_terms(0, sums, g1_ref[...], s1_ref[...], form_mixed)

    def hide(place):
        return silu(field[place, :] * scale + offset)

    for side in range(2):
        col_b[2 + side] = hide(pl.ds(side * 127, 128, stride=128)).astype(BF16)
        col_f[side] = col_b[2 + side].astype(F32)
        row_out[2 + side] = hide(pl.ds(side * 127 * 128, 128)).astype(BF16)
    put_corners(8)
    rows2 = row_copies(
        [(row_out.at[2], rows_halo.at[3, mid]), (row_out.at[3], rows_halo.at[2, mid])], 8
    ) + corner_copies(8)
    cols2 = col_copies(8)
    for c in rows2[2:] + rows2[:2] + cols2:
        c.start()

    def hide_row(h):
        v = hide(pl.ds(h * 128, 128))
        x2[h + 1, 16:144] = v.astype(BF16)
        x2[h + 1, 0:16] = jnp.where(sub == 0, 0.0, pltpu.roll(v[112:128], 1, 0)).astype(BF16)
        x2[h + 1, 144:160] = jnp.where(sub == 15, 0.0, pltpu.roll(v[0:16], 15, 0)).astype(BF16)

    many = 2 * PAIRS
    for h in range(many + 1):
        hide_row(h)
    sums = (zero8, zero8)
    for t in range(TILE // many):
        for h in range((t + 1) * many + 1, min((t + 2) * many + 1, TILE)):
            hide_row(h)
        for h, v in conv_block(x2, wb2, t):
            field[pl.ds(h * 128, 128), :] = v
            sums = sum_up(sums, v)
    sums = add_borders(8, rows2, cols2, k2, sums)
    scale2, offset2 = norm_terms(1, sums, g2_ref[...], s2_ref[...])

    def finish(n, c):
        for q in range(8):
            h = n * 8 + q
            v = silu(field[at_row(h), :] * scale2 + offset2)
            v = mixed[h].astype(F32) + v
            for s in range(8):
                swap[q, pl.ds(s, 16, stride=8), :] = v[s * 16 : (s + 1) * 16]
        for q in range(8):
            out[n * 8 + q] = swap[q].astype(BF16)
        return c

    lax.fori_loop(0, 16, finish, 0)
    whole(rows_in.at[pl.ds(1, 127)], row_sem.at[0]).wait()


def body(
    noisy_field,
    coarse_cells,
    coarse_proj,
    kernel_first,
    kernel_second,
    gain_first,
    shift_first,
    gain_second,
    shift_second,
    request_ids,
    patch_slots,
    tile_offsets,
):
    hbm = pl.BlockSpec(memory_space=pl.ANY)
    vmem = pl.BlockSpec(memory_space=pltpu.VMEM)
    smem = pl.BlockSpec(memory_space=pltpu.SMEM)
    row = lambda v: v.reshape(1, C)
    got = pl.pallas_call(
        kernel,
        out_shape=pltpu.VMEM((TILE, TILE, C), BF16),
        in_specs=[hbm] * 5 + [vmem] * 6 + [smem],
        out_specs=vmem,
        scratch_shapes=[
            pltpu.VMEM((TILE, TILE, C), BF16),
            pltpu.VMEM((HELD, CC), F32),
            pltpu.VMEM((CC, C), F32),
            pltpu.VMEM((3, 3, C, C), BF16),
            pltpu.VMEM((3, 3, C, C), BF16),
            pltpu.VMEM((12 * C, 2 * C), BF16),
            pltpu.VMEM((12 * C, 2 * C), BF16),
            pltpu.VMEM((128, 128), F32),
            pltpu.VMEM((128, 1, 128), F32),
            pltpu.VMEM((128, 1, 128), F32),
            pltpu.VMEM((HELD, 2 * C), BF16),
            pltpu.VMEM((128, MOST, C), F32),
            pltpu.VMEM((128, MOST, C), F32),
            pltpu.VMEM((8, 256), jnp.int32),
            pltpu.VMEM((256, MOST * 128), BF16),
            pltpu.VMEM((10, 256, C), F32),
            pltpu.VMEM((TILE * 16, C), F32),
            pltpu.VMEM((4, 128, C), BF16),
            pltpu.VMEM((TILE * 48, C), F32),
            pltpu.VMEM((128, 256), BF16),
            pltpu.VMEM((128, 144), BF16),
            pltpu.VMEM((128, 144), BF16),
            pltpu.VMEM((128, MOST * 128), BF16),
            pltpu.VMEM((2, 128, C), F32),
            pltpu.VMEM((256, 9 * C), BF16),
            pltpu.VMEM((4, 160, C), BF16),
            pltpu.VMEM((TILE, TILE, C), BF16),
            pltpu.VMEM((TILE + 2, 160, C), BF16),
            pltpu.VMEM((TILE * TILE, C), F32),
            pltpu.VMEM((8, TILE, C), F32),
            pltpu.VMEM((2, TILE, C), F32),
            pltpu.VMEM((4, TILE, C), BF16),
            pltpu.VMEM((4, TILE, C), BF16),
            pltpu.VMEM((2, 144, C), F32),
            pltpu.VMEM((8, 8, C), F32),
            pltpu.VMEM((8, 8, C), F32),
            pltpu.VMEM((2, 8, C), F32),
            pltpu.VMEM((2, 32, 8, C), F32),
            pltpu.SemaphoreType.DMA((5,)),
            pltpu.SemaphoreType.DMA((2,)),
            pltpu.SemaphoreType.DMA((2,)),
            pltpu.SemaphoreType.DMA((2, 2)),
            pltpu.SemaphoreType.DMA((16,)),
            pltpu.SemaphoreType.DMA((16,)),
        ],
        compiler_params=pltpu.CompilerParams(
            collective_id=0, has_side_effects=True, vmem_limit_bytes=59 << 20
        ),
        name="block",
    )(
        noisy_field.reshape(TILE, TILE, C),
        coarse_cells,
        coarse_proj,
        kernel_first,
        kernel_second,
        row(gain_first),
        row(shift_first),
        row(gain_second),
        row(shift_second),
        request_ids.transpose(0, 1, 4, 2, 3).reshape(MOST, 1, 128),
        patch_slots.reshape(1, PATCH * PATCH),
        tile_offsets.reshape(1, 2),
    )
    return got[None]


def solution(mesh):
    return jax.shard_map(
        body,
        mesh=mesh,
        in_specs=(
            P("region", "row", "col", None),
            P(("region", "row", "col"), None),
            P(),
            P(),
            P(),
            P(),
            P(),
            P(),
            P(),
            P("region", "row", "col", None, None),
            P("region", "row", "col", None),
            P("region", "row", "col", None),
        ),
        out_specs=P("region", "row", "col", None),
        check_vma=False,
    )
```

```python
import functools

import jax
import jax.numpy as jnp
from jax import lax
from jax.experimental import pallas as pl
from jax.experimental.pallas import tpu as pltpu
from jax.sharding import PartitionSpec as P

GROUPS = 32
STEP = 9
PATCH = 13
MOST = 6
TILE = 128
C = 128
CC = 640
HELD = 256
AXES = ("region", "row", "col")
MESH = pl.DeviceIdType.MESH
FLAT = pl.DeviceIdType.LOGICAL
F32 = jnp.float32
BF16 = jnp.bfloat16
PAIRS = 16


def split3(x):
    hi = x.astype(BF16)
    rest = x - hi.astype(F32)
    mid = rest.astype(BF16)
    lo = (rest - mid.astype(F32)).astype(BF16)
    return hi, mid, lo


def split2(x):
    hi = x.astype(BF16)
    return hi, (x - hi.astype(F32)).astype(BF16)


def cubic(distance):
    near_part = (1.5 * distance - 2.5) * distance * distance + 1.0
    far_part = ((-0.5 * distance + 2.5) * distance - 4.0) * distance + 2.0
    return jnp.where(distance < 1.0, near_part, jnp.where(distance < 2.0, far_part, 0.0))


def weight_terms(point, lane, offset):
    position = (offset.astype(F32) + point.astype(F32) * STEP) / 128.0 + 1.0
    cell = lane % 16
    group = lane // 16
    weight = cubic(jnp.abs(position - cell.astype(F32)))
    weight = jnp.where(cell < PATCH, weight, 0.0)
    hi, mid, lo = (t.astype(F32) for t in split3(weight))
    return jnp.where(group < 3, hi, jnp.where(group < 5, mid, jnp.where(group < 6, lo, 0.0)))


def tap_terms(point, lane, offset):
    group = (lane * 1366) >> 16
    rest = lane - group * 48
    point = point + (rest >> 4) - 1
    cell = rest & 15
    position = (offset.astype(F32) + point.astype(F32) * STEP) / 128.0 + 1.0
    weight = cubic(jnp.abs(position - cell.astype(F32)))
    weight = jnp.where((cell < PATCH) & (point >= 0) & (point < TILE), weight, 0.0)
    hi, mid, _ = (t.astype(F32) for t in split3(weight))
    return jnp.where(group < 2, hi, jnp.where(group < 3, mid, 0.0))


def silu(v):
    return v * jax.nn.sigmoid(v)


def far_first(n):
    return (~n & 0b1010100) | ((n ^ (n >> 1)) & 0b0101010) | (~n & 1)


def kernel(
    noisy_hbm,
    cells_hbm,
    proj_hbm,
    k1_hbm,
    k2_hbm,
    g1_ref,
    s1_ref,
    g2_ref,
    s2_ref,
    ids_ref,
    slots_ref,
    off_ref,
    field,
    mixed,
    terms_out,
    noisy,
    cells,
    proj,
    k1,
    k2,
    wb1,
    wb2,
    id_rows,
    id_buf,
    id_recv,
    pcat,
    rows_out,
    rows_in,
    slot_row,
    sel,
    patch,
    partial,
    row_out,
    taps,
    lhs_col,
    lhs_tap_row,
    lhs_tap_col,
    edge_rows,
    noisy_col,
    wtap,
    rows_halo,
    x2,
    col_f,
    col_b,
    halo_b,
    halo_f,
    corner_out,
    corner_in,
    st_out,
    st_in,
    ld_sem,
    id_sem,
    row_sem,
    st_sem,
    halo_send,
    halo_recv,
):
    g, i, j = (lax.axis_index(a) for a in AXES)
    me = g * 32 + i * 4 + j

    loads = [
        pltpu.make_async_copy(a, b, ld_sem.at[n])
        for n, (a, b) in enumerate(
            [(cells_hbm, cells), (proj_hbm, proj), (k1_hbm, k1), (k2_hbm, k2), (noisy_hbm, noisy)]
        )
    ]
    for c in loads:
        c.start()
    barrier = pltpu.get_barrier_semaphore()

    def greet(n, c):
        pl.semaphore_signal(barrier, inc=1, device_id=me ^ far_first(n), device_id_type=FLAT)
        return c

    lax.fori_loop(0, 127, greet, 0)

    id_rows[...] = jnp.zeros_like(id_rows)
    id_rows[0:MOST, :] = ids_ref[:, 0, :].astype(F32)
    id_buf[:, 0, :] = jnp.transpose(id_rows[...])
    id_recv[0] = id_buf[me]
    pl.semaphore_wait(barrier, 127)

    def send_ids(n, c):
        k = far_first(n)
        pltpu.make_async_remote_copy(
            id_buf.at[me ^ k], id_recv.at[k], id_sem.at[0], id_sem.at[1], device_id=me ^ k, device_id_type=FLAT
        ).start()
        return c

    lax.fori_loop(0, 127, send_ids, 0)

    loads[0].wait()
    loads[1].wait()
    projected = jnp.dot(
        cells[...], proj[...], precision=lax.Precision.HIGHEST, preferred_element_type=F32
    )
    for n, term in enumerate(split2(projected)):
        pcat[:, n * 128 : (n + 1) * 128] = term
    partial[...] = jnp.zeros_like(partial)
    taps[...] = jnp.zeros_like(taps)

    slot_row[...] = jnp.full_like(slot_row, -1)
    slot_row[0:1, 0 : PATCH * PATCH] = slots_ref[...]
    slot = slot_row[0:1, :]
    owner = (slot * 10923) >> 16
    place = slot - owner * MOST
    index = place * 128 + (owner ^ me)
    index = jnp.where(slot < 0, -1, index).astype(F32)
    index = jnp.transpose(jnp.broadcast_to(index, (128, 256)))
    lane = lax.broadcasted_iota(jnp.int32, (256, 128), 1).astype(F32)
    for n in range(MOST):
        sel[:, n * 128 : (n + 1) * 128] = jnp.where(index == lane + 128.0 * n, 1.0, 0.0).astype(BF16)

    r_iota = lax.broadcasted_iota(jnp.int32, (128, 128), 0)
    l_iota = lax.broadcasted_iota(jnp.int32, (128, 128), 1)
    column = (r_iota % 16) * 8 + r_iota // 16
    lhs_col[:, 0:128] = weight_terms(column, l_iota, off_ref[0, 1]).astype(BF16)
    lhs_col[:, 128:256] = jnp.where(column == l_iota, 1.0, 0.0).astype(BF16)
    lhs_row = weight_terms(r_iota, l_iota, off_ref[0, 0]).astype(BF16)
    r_tap = lax.broadcasted_iota(jnp.int32, (128, 144), 0)
    l_tap = lax.broadcasted_iota(jnp.int32, (128, 144), 1)
    lhs_tap_row[...] = tap_terms(r_tap, l_tap, off_ref[0, 0]).astype(BF16)
    lhs_tap_col[...] = tap_terms((r_tap % 16) * 8 + r_tap // 16, l_tap, off_ref[0, 1]).astype(BF16)
    e_row = lax.broadcasted_iota(jnp.int32, (64, 256), 0)
    p_cell = lax.broadcasted_iota(jnp.int32, (64, 256), 1)
    p_row = (p_cell * 5042) >> 16
    p_col = p_cell - p_row * PATCH
    on_rows = e_row < 32
    point = jnp.where((e_row & 16) == 0, 0, TILE - 1)
    start = jnp.where(on_rows, off_ref[0, 0], off_ref[0, 1])
    position = (start.astype(F32) + point.astype(F32) * STEP) / 128.0 + 1.0
    weight = cubic(jnp.abs(position - jnp.where(on_rows, p_row, p_col).astype(F32)))
    keep = (jnp.where(on_rows, p_col, p_row) == (e_row & 15)) & (p_cell < PATCH * PATCH)
    edge_terms = jnp.concatenate(split2(jnp.where(keep, weight, 0.0)), axis=0)
    edge_rows[...] = jnp.dot(edge_terms, sel[...], preferred_element_type=F32).astype(BF16)

    loads[2].wait()
    loads[3].wait()
    zero_block = jnp.zeros((128, 128), BF16)
    for w, wb in ((k1, wb1), (k2, wb2)):
        for a in range(4):
            for b in range(3):
                for e in range(2):
                    block = w[a - e, b] if 0 <= a - e <= 2 else zero_block
                    wb[(a * 3 + b) * 128 : (a * 3 + b + 1) * 128, e * 128 : (e + 1) * 128] = block

    for a in range(3):
        for b in range(3):
            n = a * 3 + b
            wtap[0:128, n * 128 : (n + 1) * 128] = k1[a, b]
            wtap[128:256, n * 128 : (n + 1) * 128] = k1[a, b]

    sub = lax.broadcasted_iota(jnp.int32, (16, 128), 0)
    x2[0] = jnp.zeros((160, 128), BF16)
    x2[TILE + 1] = jnp.zeros((160, 128), BF16)
    loads[4].wait()

    def reorder(n, c):
        h0 = n * 16
        got = jnp.dot(
            lhs_col[:, 128:256],
            jnp.concatenate([noisy[h0 + q] for q in range(16)], axis=1),
            preferred_element_type=F32,
        )
        for q in range(16):
            v = got[:, q * 128 : (q + 1) * 128]
            h = h0 + q
            x2[h + 1, 16:144] = v.astype(BF16)
            x2[h + 1, 0:16] = jnp.where(sub == 0, 0.0, pltpu.roll(v[112:128], 1, 0)).astype(BF16)
            x2[h + 1, 144:160] = jnp.where(sub == 15, 0.0, pltpu.roll(v[0:16], 15, 0)).astype(BF16)
            noisy_col[0, pl.ds(h, 1), :] = v[0:1]
            noisy_col[1, pl.ds(h, 1), :] = v[127:128]
        return c

    lax.fori_loop(0, 8, reorder, 0)

    def conv_block(x, wb, t):
        y = t * (2 * PAIRS)
        lhs = []
        for q in range(PAIRS):
            parts = [
                x[y + 2 * q + a, b * 16 : b * 16 + 128] for a in range(4) for b in range(3)
            ]
            lhs.append(jnp.concatenate(parts, axis=1))
        got = jnp.dot(jnp.concatenate(lhs, axis=0), wb[...], preferred_element_type=F32)
        for q in range(PAIRS):
            for e in range(2):
                yield y + 2 * q + e, got[q * 128 : (q + 1) * 128, e * 128 : (e + 1) * 128]

    def at_row(h):
        return pl.ds(pl.multiple_of(h * 128, 128), 128)

    def conv_noisy(t, c):
        for h, v in conv_block(x2, wb1, t):
            field[at_row(h), :] = v
        return c

    def whole(ref, sem):
        return pltpu.make_async_copy(ref, ref, sem)

    whole(id_recv.at[pl.ds(1, 127)], id_sem.at[1]).wait()
    asked = id_recv[:, 0, :] - (me * HELD).astype(F32)
    row_iota = lax.broadcasted_iota(jnp.int32, (128, HELD), 1).astype(F32)
    hot = [
        jnp.where(asked[:, m : m + 1] == row_iota, 1.0, 0.0).astype(BF16) for m in range(MOST)
    ]
    found = jnp.dot(jnp.concatenate(hot, axis=0), pcat[...], preferred_element_type=F32)
    found = found[:, 0:128] + found[:, 128:256]
    for m in range(MOST):
        rows_out[:, m, :] = found[m * 128 : (m + 1) * 128]
    rows_in[0] = rows_out[0]

    def send_rows(n, c):
        k = far_first(n)
        pltpu.make_async_remote_copy(
            rows_out.at[k],
            rows_in.at[k],
            row_sem.at[0],
            row_sem.at[1],
            device_id=me ^ k,
            device_id_type=FLAT,
        ).start()
        return c

    lax.fori_loop(0, 127, send_rows, 0)
    lax.fori_loop(0, 64 // PAIRS, conv_noisy, 0)
    whole(id_buf.at[pl.ds(1, 127)], id_sem.at[0]).wait()
    whole(rows_in.at[pl.ds(1, 127)], row_sem.at[1]).wait()

    terms = [jnp.concatenate(split2(rows_in[:, m, :]), axis=1) for m in range(MOST)]
    terms = jnp.concatenate(terms, axis=0)
    zero_tile = jnp.zeros((32, 128), BF16)

    def stack_terms(x):
        hi, mid, lo = split3(x)
        return jnp.concatenate([hi, mid, lo, hi, mid, hi, zero_tile], axis=0)

    got = jnp.dot(edge_rows[...], terms, preferred_element_type=F32)
    got = got[:, 0:128] + got[:, 128:256]
    ends = got[0:64] + got[64:128]
    for side in range(2):
        h = side * (TILE - 1)
        rhs = jnp.concatenate([stack_terms(ends[side * 16 : side * 16 + 16]), noisy[h]], axis=0)
        row_out[side] = jnp.dot(lhs_col[...], rhs, preferred_element_type=F32).astype(BF16)
        rhs = stack_terms(ends[32 + side * 16 : 48 + side * 16])
        got = noisy_col[side] + jnp.dot(lhs_row, rhs, preferred_element_type=F32)
        col_b[side] = got.astype(BF16)
        col_f[side] = col_b[side].astype(F32)

    def form_mixed():
        for b in range(PATCH):
            rhs = stack_terms(patch[9, pl.ds(b, 16, stride=PATCH), :])
            partial[pl.ds(b, 128, stride=16), :] = jnp.dot(
                lhs_row, rhs, preferred_element_type=F32
            )

        def step(n, c):
            rhs = []
            for q in range(16):
                h = n * 16 + q
                t = stack_terms(partial[pl.ds(pl.multiple_of(h * 16, 16), 16), :])
                rhs.append(jnp.concatenate([t, noisy[h]], axis=0))
            got = jnp.dot(
                lhs_col[...], jnp.concatenate(rhs, axis=1), preferred_element_type=F32
            ).astype(BF16)
            for q in range(16):
                mixed[n * 16 + q] = got[:, q * 128 : (q + 1) * 128]
            return c

        lax.fori_loop(0, 8, step, 0)

    def neighbour(di, dj):
        return (g, (i + di + 8) % 8, (j + dj + 4) % 4)

    def row_copies(pairs, base):
        return [
            pltpu.make_async_remote_copy(
                src,
                dst,
                halo_send.at[base + n],
                halo_recv.at[base + n],
                device_id=neighbour(di, 0),
                device_id_type=MESH,
            )
            for n, ((src, dst), di) in enumerate(zip(pairs, (-1, 1)))
        ]

    def corner_copies(base):
        cs = []
        for n, (di, dj) in enumerate(((-1, -1), (-1, 1), (1, -1), (1, 1))):
            slot_n = base // 8 * 4 + n
            cs.append(
                pltpu.make_async_remote_copy(
                    corner_out.at[slot_n],
                    corner_in.at[slot_n],
                    halo_send.at[base + 4 + n],
                    halo_recv.at[base + 4 + n],
                    device_id=neighbour(di, dj),
                    device_id_type=MESH,
                )
            )
        return cs

    def col_copies(base):
        cs = []
        for n, dj in enumerate((-1, 1)):
            slot_n = base // 8 * 2 + n
            cs.append(
                pltpu.make_async_remote_copy(
                    col_b.at[slot_n],
                    halo_b.at[slot_n],
                    halo_send.at[base + 2 + n],
                    halo_recv.at[base + 2 + n],
                    device_id=neighbour(0, dj),
                    device_id_type=MESH,
                )
            )
        return cs

    def put_corners(base):
        s = base // 8 * 4
        for n, (side, h) in enumerate(((0, 0), (1, 0), (0, 127), (1, 127))):
            corner_out[s + n] = jnp.broadcast_to(col_f[side, h : h + 1, :], (8, 128))

    def put_columns(base):
        s = base // 8 * 2
        for side in range(2):
            col_b[s + side] = col_f[side].astype(BF16)

    left_ok = jnp.where(j > 0, 1.0, 0.0)
    right_ok = jnp.where(j < 3, 1.0, 0.0)
    up_ok = jnp.where(i > 0, 1.0, 0.0)
    down_ok = jnp.where(i < 7, 1.0, 0.0)

    def take_columns(base, copies):
        for c in copies:
            c.wait()
        s2 = base // 8 * 2
        halo_f[0, 8:136, :] = halo_b[s2 + 1].astype(F32) * left_ok
        halo_f[1, 8:136, :] = halo_b[s2 + 0].astype(F32) * right_ok

    def take_corners(base):
        s4 = base // 8 * 4
        halo_f[0, 0:8, :] = corner_in[s4 + 3] * (left_ok * up_ok)
        halo_f[1, 0:8, :] = corner_in[s4 + 2] * (right_ok * up_ok)
        halo_f[0, 136:144, :] = corner_in[s4 + 1] * (left_ok * down_ok)
        halo_f[1, 136:144, :] = corner_in[s4 + 0] * (right_ok * down_ok)

    put_corners(0)
    mid = pl.ds(16, 128)
    rows1 = row_copies(
        [(row_out.at[0], rows_halo.at[1, mid]), (row_out.at[1], rows_halo.at[0, mid])], 0
    ) + corner_copies(0)
    cols1 = col_copies(0)
    for c in rows1[2:] + rows1[:2] + cols1:
        c.start()

    cell = jnp.dot(sel[...], terms, preferred_element_type=F32)
    cell = cell[:, 0:128] + cell[:, 128:256]
    patch[9] = cell
    hi, low = split2(cell)
    tapped = jnp.dot(jnp.concatenate([hi, low], axis=1), wtap[...], preferred_element_type=F32)
    for n in range(9):
        patch[n] = tapped[:, n * 128 : (n + 1) * 128]
    for b in range(3):
        rhs = []
        for col in range(PATCH):
            parts = [
                patch[a * 3 + b, pl.ds(col, 16, stride=PATCH), :] for a in range(3)
            ]
            hi, low = split2(jnp.concatenate(parts, axis=0))
            rhs.append(jnp.concatenate([hi, low, hi], axis=0))
        got = jnp.dot(
            lhs_tap_row[...], jnp.concatenate(rhs, axis=1), preferred_element_type=F32
        )
        for col in range(PATCH):
            taps[pl.ds(b * 16 + col, 128, stride=48), :] = got[:, col * 128 : (col + 1) * 128]

    def sum_up(carry, v):
        total, square = carry
        v3 = v.reshape(v.shape[0] // 8, 8, 128)
        return total + jnp.sum(v3, axis=0), square + jnp.sum(v3 * v3, axis=0)

    def add_taps(n, carry):
        rhs = []
        for q in range(16):
            h = n * 16 + q
            hi, low = split2(taps[pl.ds(pl.multiple_of(h * 48, 16), 48), :])
            rhs.append(jnp.concatenate([hi, low, hi], axis=0))
        got = jnp.dot(
            lhs_tap_col[...], jnp.concatenate(rhs, axis=1), preferred_element_type=F32
        )
        for q in range(16):
            h = n * 16 + q
            v = field[at_row(h), :] + got[:, q * 128 : (q + 1) * 128]
            field[at_row(h), :] = v
            carry = sum_up(carry, v)
        return carry

    zero8 = jnp.zeros((8, 128), F32)
    sums = lax.fori_loop(0, 8, add_taps, (zero8, zero8))

    def correct(carry, place, delta):
        old = field[place, :]
        new = old + delta
        field[place, :] = new
        d3 = delta.reshape(16, 8, 128)
        q3 = (new * new - old * old).reshape(16, 8, 128)
        return carry[0] + jnp.sum(d3, axis=0), carry[1] + jnp.sum(q3, axis=0)

    def add_borders(base, rows, columns, k, carry):
        n = base // 8 * 2
        take_columns(base, columns)
        for c in rows:
            c.wait()
        take_corners(base)
        for side, ok in ((0, up_ok), (1, down_ok)):
            v = rows_halo[n + side, 16:144].astype(F32) * ok
            rows_halo[n + side, 16:144] = v.astype(BF16)
            last = pltpu.roll(v[112:128], 1, 0)
            rows_halo[n + side, 0:16] = jnp.where(sub == 0, 0.0, last).astype(BF16)
            first = pltpu.roll(v[0:16], 15, 0)
            rows_halo[n + side, 144:160] = jnp.where(sub == 15, 0.0, first).astype(BF16)
        for side in range(2):
            lhs = [halo_f[side, 7 + a : 135 + a, :].astype(BF16) for a in range(3)]
            rhs = jnp.concatenate([k[a, 2 * side] for a in range(3)], axis=0)
            delta = jnp.dot(jnp.concatenate(lhs, axis=1), rhs, preferred_element_type=F32)
            carry = correct(carry, pl.ds(side * 127, 128, stride=128), delta)
        for side in range(2):
            lhs = [rows_halo[n + side, b * 16 : b * 16 + 128] for b in range(3)]
            rhs = jnp.concatenate([k[2 * side, b] for b in range(3)], axis=0)
            delta = jnp.dot(jnp.concatenate(lhs, axis=1), rhs, preferred_element_type=F32)
            carry = correct(carry, pl.ds(side * 127 * 128, 128), delta)
        return carry

    sums = add_borders(0, rows1, cols1, k1, sums)

    group_ones = jnp.where(r_iota // 4 == l_iota // 4, 1.0, 0.0)
    number = float(TILE * TILE * 32 * (C // GROUPS))

    def norm_terms(n, sums, gain, shift, meanwhile=None):
        total, square = (jnp.sum(s, axis=0, keepdims=True) for s in sums)
        sub8 = lax.broadcasted_iota(jnp.int32, (8, 128), 0)
        mine = jnp.where(sub8 == 0, total, jnp.where(sub8 == 1, square, 0.0))
        st_out[n] = mine
        st_in[n, 0] = mine
        def send(t, c):
            k = far_first(t)
            pltpu.make_async_remote_copy(
                st_out.at[n],
                st_in.at[n, k],
                st_sem.at[n, 0],
                st_sem.at[n, 1],
                device_id=me ^ k,
                device_id_type=FLAT,
            ).start()
            return c

        lax.fori_loop(96, 127, send, 0)
        if meanwhile is not None:
            meanwhile()
        whole(st_in.at[n, pl.ds(1, 31)], st_sem.at[n, 1]).wait()
        both = jnp.sum(st_in[n], axis=0)
        both = jnp.dot(
            both, group_ones, precision=lax.Precision.HIGHEST, preferred_element_type=F32
        )
        mean = both[0:1] / number
        spread = both[1:2] / number - mean * mean
        scale = lax.rsqrt(spread + 1e-05) * gain
        whole(st_in.at[n, pl.ds(1, 31)], st_sem.at[n, 0]).wait()
        return scale, shift - mean * scale

    scale, offset = norm_terms(0, sums, g1_ref[...], s1_ref[...], form_mixed)

    def hide(place):
        return silu(field[place, :] * scale + offset)

    for side in range(2):
        col_b[2 + side] = hide(pl.ds(side * 127, 128, stride=128)).astype(BF16)
        col_f[side] = col_b[2 + side].astype(F32)
        row_out[2 + side] = hide(pl.ds(side * 127 * 128, 128)).astype(BF16)
    put_corners(8)
    rows2 = row_copies(
        [(row_out.at[2], rows_halo.at[3, mid]), (row_out.at[3], rows_halo.at[2, mid])], 8
    ) + corner_copies(8)
    cols2 = col_copies(8)
    for c in rows2[2:] + rows2[:2] + cols2:
        c.start()

    def hide_row(h):
        v = hide(pl.ds(h * 128, 128))
        x2[h + 1, 16:144] = v.astype(BF16)
        x2[h + 1, 0:16] = jnp.where(sub == 0, 0.0, pltpu.roll(v[112:128], 1, 0)).astype(BF16)
        x2[h + 1, 144:160] = jnp.where(sub == 15, 0.0, pltpu.roll(v[0:16], 15, 0)).astype(BF16)

    many = 2 * PAIRS
    for h in range(many + 1):
        hide_row(h)
    sums = (zero8, zero8)
    for t in range(TILE // many):
        for h in range((t + 1) * many + 1, min((t + 2) * many + 1, TILE)):
            hide_row(h)
        for h, v in conv_block(x2, wb2, t):
            field[pl.ds(h * 128, 128), :] = v
            sums = sum_up(sums, v)
    sums = add_borders(8, rows2, cols2, k2, sums)
    scale2, offset2 = norm_terms(1, sums, g2_ref[...], s2_ref[...])

    terms_out[0:1, :] = scale2
    terms_out[1:2, :] = offset2
    whole(rows_in.at[pl.ds(1, 127)], row_sem.at[0]).wait()


def result_kernel(field, mixed, terms, out_hbm, stage, swap, sem):
    scale = terms[0:1, :]
    offset = terms[1:2, :]

    def finish(n, c):
        for q in range(8):
            h = n * 8 + q
            v = silu(field[pl.ds(pl.multiple_of(h * 128, 128), 128), :] * scale + offset)
            v = mixed[h].astype(F32) + v
            for s in range(8):
                swap[q, pl.ds(s, 16, stride=8), :] = v[s * 16 : (s + 1) * 16]
        for q in range(8):
            stage[n * 8 + q] = swap[q].astype(BF16)
        rows = pl.ds(n * 8, 8)
        pltpu.make_async_copy(stage.at[rows], out_hbm.at[rows], sem).start()
        return c

    lax.fori_loop(0, 16, finish, 0)
    pltpu.make_async_copy(stage, out_hbm, sem).wait()


def body(
    noisy_field,
    coarse_cells,
    coarse_proj,
    kernel_first,
    kernel_second,
    gain_first,
    shift_first,
    gain_second,
    shift_second,
    request_ids,
    patch_slots,
    tile_offsets,
):
    hbm = pl.BlockSpec(memory_space=pl.ANY)
    vmem = pl.BlockSpec(memory_space=pltpu.VMEM)
    smem = pl.BlockSpec(memory_space=pltpu.SMEM)
    row = lambda v: v.reshape(1, C)
    second, mixed, terms = pl.pallas_call(
        kernel,
        out_shape=[
            pltpu.VMEM((TILE * TILE, C), F32),
            pltpu.VMEM((TILE, TILE, C), BF16),
            pltpu.VMEM((8, C), F32),
        ],
        in_specs=[hbm] * 5 + [vmem] * 6 + [smem],
        out_specs=[vmem] * 3,
        scratch_shapes=[
            pltpu.VMEM((TILE, TILE, C), BF16),
            pltpu.VMEM((HELD, CC), F32),
            pltpu.VMEM((CC, C), F32),
            pltpu.VMEM((3, 3, C, C), BF16),
            pltpu.VMEM((3, 3, C, C), BF16),
            pltpu.VMEM((12 * C, 2 * C), BF16),
            pltpu.VMEM((12 * C, 2 * C), BF16),
            pltpu.VMEM((128, 128), F32),
            pltpu.VMEM((128, 1, 128), F32),
            pltpu.VMEM((128, 1, 128), F32),
            pltpu.VMEM((HELD, 2 * C), BF16),
            pltpu.VMEM((128, MOST, C), F32),
            pltpu.VMEM((128, MOST, C), F32),
            pltpu.VMEM((8, 256), jnp.int32),
            pltpu.VMEM((256, MOST * 128), BF16),
            pltpu.VMEM((10, 256, C), F32),
            pltpu.VMEM((TILE * 16, C), F32),
            pltpu.VMEM((4, 128, C), BF16),
            pltpu.VMEM((TILE * 48, C), F32),
            pltpu.VMEM((128, 256), BF16),
            pltpu.VMEM((128, 144), BF16),
            pltpu.VMEM((128, 144), BF16),
            pltpu.VMEM((128, MOST * 128), BF16),
            pltpu.VMEM((2, 128, C), F32),
            pltpu.VMEM((256, 9 * C), BF16),
            pltpu.VMEM((4, 160, C), BF16),
            pltpu.VMEM((TILE + 2, 160, C), BF16),
            pltpu.VMEM((2, TILE, C), F32),
            pltpu.VMEM((4, TILE, C), BF16),
            pltpu.VMEM((4, TILE, C), BF16),
            pltpu.VMEM((2, 144, C), F32),
            pltpu.VMEM((8, 8, C), F32),
            pltpu.VMEM((8, 8, C), F32),
            pltpu.VMEM((2, 8, C), F32),
            pltpu.VMEM((2, 32, 8, C), F32),
            pltpu.SemaphoreType.DMA((5,)),
            pltpu.SemaphoreType.DMA((2,)),
            pltpu.SemaphoreType.DMA((2,)),
            pltpu.SemaphoreType.DMA((2, 2)),
            pltpu.SemaphoreType.DMA((16,)),
            pltpu.SemaphoreType.DMA((16,)),
        ],
        compiler_params=pltpu.CompilerParams(
            collective_id=0, has_side_effects=True, vmem_limit_bytes=50 << 20
        ),
        name="block",
    )(
        noisy_field.reshape(TILE, TILE, C),
        coarse_cells,
        coarse_proj,
        kernel_first,
        kernel_second,
        row(gain_first),
        row(shift_first),
        row(gain_second),
        row(shift_second),
        request_ids.transpose(0, 1, 4, 2, 3).reshape(MOST, 1, 128),
        patch_slots.reshape(1, PATCH * PATCH),
        tile_offsets.reshape(1, 2),
    )
    got = pl.pallas_call(
        result_kernel,
        out_shape=jax.ShapeDtypeStruct((TILE, TILE, C), BF16),
        in_specs=[vmem] * 3,
        out_specs=hbm,
        scratch_shapes=[
            pltpu.VMEM((TILE, TILE, C), BF16),
            pltpu.VMEM((8, TILE, C), F32),
            pltpu.SemaphoreType.DMA,
        ],
        compiler_params=pltpu.CompilerParams(vmem_limit_bytes=10 << 20),
        name="result",
    )(second, mixed, terms)
    return got[None]


def solution(mesh):
    return jax.shard_map(
        body,
        mesh=mesh,
        in_specs=(
            P("region", "row", "col", None),
            P(("region", "row", "col"), None),
            P(),
            P(),
            P(),
            P(),
            P(),
            P(),
            P(),
            P("region", "row", "col", None, None),
            P("region", "row", "col", None),
            P("region", "row", "col", None),
        ),
        out_specs=P("region", "row", "col", None),
        check_vma=False,
    )
```

```python
import functools

import jax
import jax.numpy as jnp
from jax import lax
from jax.experimental import pallas as pl
from jax.experimental.pallas import tpu as pltpu
from jax.sharding import PartitionSpec as P

GROUPS = 32
STEP = 9
PATCH = 13
MOST = 6
TILE = 128
C = 128
CC = 640
HELD = 256
AXES = ("region", "row", "col")
MESH = pl.DeviceIdType.MESH
FLAT = pl.DeviceIdType.LOGICAL
F32 = jnp.float32
BF16 = jnp.bfloat16
PAIRS = 16


def split3(x):
    hi = x.astype(BF16)
    rest = x - hi.astype(F32)
    mid = rest.astype(BF16)
    lo = (rest - mid.astype(F32)).astype(BF16)
    return hi, mid, lo


def split2(x):
    hi = x.astype(BF16)
    return hi, (x - hi.astype(F32)).astype(BF16)


def cubic(distance):
    near_part = (1.5 * distance - 2.5) * distance * distance + 1.0
    far_part = ((-0.5 * distance + 2.5) * distance - 4.0) * distance + 2.0
    return jnp.where(distance < 1.0, near_part, jnp.where(distance < 2.0, far_part, 0.0))


def weight_terms(point, lane, offset):
    position = (offset.astype(F32) + point.astype(F32) * STEP) / 128.0 + 1.0
    cell = lane % 16
    group = lane // 16
    weight = cubic(jnp.abs(position - cell.astype(F32)))
    weight = jnp.where(cell < PATCH, weight, 0.0)
    hi, mid, lo = (t.astype(F32) for t in split3(weight))
    return jnp.where(group < 3, hi, jnp.where(group < 5, mid, jnp.where(group < 6, lo, 0.0)))


def tap_terms(point, lane, offset):
    group = (lane * 1366) >> 16
    rest = lane - group * 48
    point = point + (rest >> 4) - 1
    cell = rest & 15
    position = (offset.astype(F32) + point.astype(F32) * STEP) / 128.0 + 1.0
    weight = cubic(jnp.abs(position - cell.astype(F32)))
    weight = jnp.where((cell < PATCH) & (point >= 0) & (point < TILE), weight, 0.0)
    hi, mid, _ = (t.astype(F32) for t in split3(weight))
    return jnp.where(group < 2, hi, jnp.where(group < 3, mid, 0.0))


def silu(v):
    return v * jax.nn.sigmoid(v)


def far_first(n):
    return (~n & 0b1010100) | ((n ^ (n >> 1)) & 0b0101010) | (~n & 1)


def kernel(
    noisy_hbm,
    cells_hbm,
    proj_hbm,
    k1_hbm,
    k2_hbm,
    g1_hbm,
    s1_hbm,
    g2_hbm,
    s2_hbm,
    ids_hbm,
    slots_hbm,
    off_hbm,
    field,
    mixed,
    terms_out,
    vectors,
    ids_ref,
    slots_ref,
    off_ref,
    noisy,
    cells,
    proj,
    k1,
    k2,
    wb1,
    wb2,
    id_rows,
    id_buf,
    id_recv,
    pcat,
    rows_out,
    rows_in,
    slot_row,
    sel,
    patch,
    partial,
    row_out,
    taps,
    lhs_col,
    lhs_tap_row,
    lhs_tap_col,
    edge_rows,
    noisy_col,
    wtap,
    rows_halo,
    x2,
    col_f,
    col_b,
    halo_b,
    halo_f,
    corner_out,
    corner_in,
    st_out,
    st_in,
    ld_sem,
    id_sem,
    row_sem,
    st_sem,
    halo_send,
    halo_recv,
):
    g, i, j = (lax.axis_index(a) for a in AXES)
    me = g * 32 + i * 4 + j

    loads = [
        pltpu.make_async_copy(a, b, ld_sem.at[n])
        for n, (a, b) in enumerate(
            [
                (cells_hbm, cells),
                (proj_hbm, proj),
                (k1_hbm, k1),
                (k2_hbm, k2),
                (noisy_hbm, noisy),
                (ids_hbm, ids_ref),
                (slots_hbm, slots_ref),
                (off_hbm, off_ref),
                (g1_hbm, vectors.at[0]),
                (s1_hbm, vectors.at[1]),
                (g2_hbm, vectors.at[2]),
                (s2_hbm, vectors.at[3]),
            ]
        )
    ]
    loads[5].start()
    barrier = pltpu.get_barrier_semaphore()

    def greet(n, c):
        pl.semaphore_signal(barrier, inc=1, device_id=me ^ far_first(n), device_id_type=FLAT)
        return c

    lax.fori_loop(0, 127, greet, 0)
    for c in loads[:5] + loads[6:]:
        c.start()
    loads[5].wait()

    id_rows[...] = jnp.zeros_like(id_rows)
    id_rows[0:MOST, :] = ids_ref[:, 0, :].astype(F32)
    id_buf[:, 0, :] = jnp.transpose(id_rows[...])
    id_recv[0] = id_buf[me]
    pl.semaphore_wait(barrier, 127)

    def send_ids(n, c):
        k = far_first(n)
        pltpu.make_async_remote_copy(
            id_buf.at[me ^ k], id_recv.at[k], id_sem.at[0], id_sem.at[1], device_id=me ^ k, device_id_type=FLAT
        ).start()
        return c

    lax.fori_loop(0, 127, send_ids, 0)

    for n in (0, 1, 6, 7, 8, 9, 10, 11):
        loads[n].wait()
    projected = jnp.dot(
        cells[...], proj[...], precision=lax.Precision.HIGHEST, preferred_element_type=F32
    )
    for n, term in enumerate(split2(projected)):
        pcat[:, n * 128 : (n + 1) * 128] = term
    for b in range(PATCH, 16):
        for n in range(3):
            taps[pl.ds(n * 16 + b, 128, stride=48), :] = jnp.zeros((128, 128), F32)

    slot_row[...] = jnp.full_like(slot_row, -1)
    slot_row[0:1, 0 : PATCH * PATCH] = slots_ref[...]
    slot = slot_row[0:1, :]
    owner = (slot * 10923) >> 16
    place = slot - owner * MOST
    index = place * 128 + (owner ^ me)
    index = jnp.where(slot < 0, -1, index).astype(F32)
    index = jnp.transpose(jnp.broadcast_to(index, (128, 256)))
    lane = lax.broadcasted_iota(jnp.int32, (256, 128), 1).astype(F32)
    for n in range(MOST):
        sel[:, n * 128 : (n + 1) * 128] = jnp.where(index == lane + 128.0 * n, 1.0, 0.0).astype(BF16)

    r_iota = lax.broadcasted_iota(jnp.int32, (128, 128), 0)
    l_iota = lax.broadcasted_iota(jnp.int32, (128, 128), 1)
    column = (r_iota % 16) * 8 + r_iota // 16
    lhs_col[:, 0:128] = weight_terms(column, l_iota, off_ref[0, 1]).astype(BF16)
    lhs_col[:, 128:256] = jnp.where(column == l_iota, 1.0, 0.0).astype(BF16)
    lhs_row = weight_terms(r_iota, l_iota, off_ref[0, 0]).astype(BF16)
    r_tap = lax.broadcasted_iota(jnp.int32, (128, 144), 0)
    l_tap = lax.broadcasted_iota(jnp.int32, (128, 144), 1)
    lhs_tap_row[...] = tap_terms(r_tap, l_tap, off_ref[0, 0]).astype(BF16)
    lhs_tap_col[...] = tap_terms((r_tap % 16) * 8 + r_tap // 16, l_tap, off_ref[0, 1]).astype(BF16)
    e_row = lax.broadcasted_iota(jnp.int32, (64, 256), 0)
    p_cell = lax.broadcasted_iota(jnp.int32, (64, 256), 1)
    p_row = (p_cell * 5042) >> 16
    p_col = p_cell - p_row * PATCH
    on_rows = e_row < 32
    point = jnp.where((e_row & 16) == 0, 0, TILE - 1)
    start = jnp.where(on_rows, off_ref[0, 0], off_ref[0, 1])
    position = (start.astype(F32) + point.astype(F32) * STEP) / 128.0 + 1.0
    weight = cubic(jnp.abs(position - jnp.where(on_rows, p_row, p_col).astype(F32)))
    keep = (jnp.where(on_rows, p_col, p_row) == (e_row & 15)) & (p_cell < PATCH * PATCH)
    edge_terms = jnp.concatenate(split2(jnp.where(keep, weight, 0.0)), axis=0)
    edge_rows[...] = jnp.dot(edge_terms, sel[...], preferred_element_type=F32).astype(BF16)

    loads[2].wait()
    zero_block = jnp.zeros((128, 128), BF16)

    def two_rows(w, wb):
        for a in range(4):
            for b in range(3):
                for e in range(2):
                    block = w[a - e, b] if 0 <= a - e <= 2 else zero_block
                    wb[(a * 3 + b) * 128 : (a * 3 + b + 1) * 128, e * 128 : (e + 1) * 128] = block

    two_rows(k1, wb1)
    for a in range(3):
        for b in range(3):
            n = a * 3 + b
            wtap[0:128, n * 128 : (n + 1) * 128] = k1[a, b]
            wtap[128:256, n * 128 : (n + 1) * 128] = k1[a, b]

    sub = lax.broadcasted_iota(jnp.int32, (16, 128), 0)
    x2[0] = jnp.zeros((160, 128), BF16)
    x2[TILE + 1] = jnp.zeros((160, 128), BF16)
    loads[4].wait()

    def reorder(n, c):
        h0 = n * 16
        got = jnp.dot(
            lhs_col[:, 128:256],
            jnp.concatenate([noisy[h0 + q] for q in range(16)], axis=1),
            preferred_element_type=F32,
        )
        for q in range(16):
            v = got[:, q * 128 : (q + 1) * 128]
            h = h0 + q
            x2[h + 1, 16:144] = v.astype(BF16)
            x2[h + 1, 0:16] = jnp.where(sub == 0, 0.0, pltpu.roll(v[112:128], 1, 0)).astype(BF16)
            x2[h + 1, 144:160] = jnp.where(sub == 15, 0.0, pltpu.roll(v[0:16], 15, 0)).astype(BF16)
            noisy_col[0, pl.ds(h, 1), :] = v[0:1]
            noisy_col[1, pl.ds(h, 1), :] = v[127:128]
        return c

    lax.fori_loop(0, 8, reorder, 0)

    def conv_block(x, wb, t):
        y = t * (2 * PAIRS)
        lhs = []
        for q in range(PAIRS):
            parts = [
                x[y + 2 * q + a, b * 16 : b * 16 + 128] for a in range(4) for b in range(3)
            ]
            lhs.append(jnp.concatenate(parts, axis=1))
        got = jnp.dot(jnp.concatenate(lhs, axis=0), wb[...], preferred_element_type=F32)
        for q in range(PAIRS):
            for e in range(2):
                yield y + 2 * q + e, got[q * 128 : (q + 1) * 128, e * 128 : (e + 1) * 128]

    def at_row(h):
        return pl.ds(pl.multiple_of(h * 128, 128), 128)

    def conv_noisy(t, c):
        for h, v in conv_block(x2, wb1, t):
            field[at_row(h), :] = v
        return c

    def whole(ref, sem):
        return pltpu.make_async_copy(ref, ref, sem)

    whole(id_recv.at[pl.ds(1, 127)], id_sem.at[1]).wait()
    asked = id_recv[:, 0, :] - (me * HELD).astype(F32)
    row_iota = lax.broadcasted_iota(jnp.int32, (128, HELD), 1).astype(F32)
    hot = [
        jnp.where(asked[:, m : m + 1] == row_iota, 1.0, 0.0).astype(BF16) for m in range(MOST)
    ]
    found = jnp.dot(jnp.concatenate(hot, axis=0), pcat[...], preferred_element_type=F32)
    found = found[:, 0:128] + found[:, 128:256]
    for m in range(MOST):
        rows_out[:, m, :] = found[m * 128 : (m + 1) * 128]
    rows_in[0] = rows_out[0]

    def send_rows(n, c):
        k = far_first(n)
        pltpu.make_async_remote_copy(
            rows_out.at[k],
            rows_in.at[k],
            row_sem.at[0],
            row_sem.at[1],
            device_id=me ^ k,
            device_id_type=FLAT,
        ).start()
        return c

    lax.fori_loop(0, 127, send_rows, 0)
    lax.fori_loop(0, 64 // PAIRS, conv_noisy, 0)
    whole(id_buf.at[pl.ds(1, 127)], id_sem.at[0]).wait()
    whole(rows_in.at[pl.ds(1, 127)], row_sem.at[1]).wait()

    terms = [jnp.concatenate(split2(rows_in[:, m, :]), axis=1) for m in range(MOST)]
    terms = jnp.concatenate(terms, axis=0)
    zero_tile = jnp.zeros((32, 128), BF16)

    def stack_terms(x):
        hi, mid, lo = split3(x)
        return jnp.concatenate([hi, mid, lo, hi, mid, hi, zero_tile], axis=0)

    got = jnp.dot(edge_rows[...], terms, preferred_element_type=F32)
    got = got[:, 0:128] + got[:, 128:256]
    ends = got[0:64] + got[64:128]
    for side in range(2):
        h = side * (TILE - 1)
        rhs = jnp.concatenate([stack_terms(ends[side * 16 : side * 16 + 16]), noisy[h]], axis=0)
        row_out[side] = jnp.dot(lhs_col[...], rhs, preferred_element_type=F32).astype(BF16)
        rhs = stack_terms(ends[32 + side * 16 : 48 + side * 16])
        got = noisy_col[side] + jnp.dot(lhs_row, rhs, preferred_element_type=F32)
        col_b[side] = got.astype(BF16)
        col_f[side] = col_b[side].astype(F32)

    def form_mixed():
        for b in range(PATCH):
            rhs = stack_terms(patch[9, pl.ds(b, 16, stride=PATCH), :])
            partial[pl.ds(b, 128, stride=16), :] = jnp.dot(
                lhs_row, rhs, preferred_element_type=F32
            )

        def step(n, c):
            rhs = []
            for q in range(16):
                h = n * 16 + q
                t = stack_terms(partial[pl.ds(pl.multiple_of(h * 16, 16), 16), :])
                rhs.append(jnp.concatenate([t, noisy[h]], axis=0))
            got = jnp.dot(
                lhs_col[...], jnp.concatenate(rhs, axis=1), preferred_element_type=F32
            ).astype(BF16)
            for q in range(16):
                mixed[n * 16 + q] = got[:, q * 128 : (q + 1) * 128]
            return c

        lax.fori_loop(0, 8, step, 0)

    def neighbour(di, dj):
        return (g, (i + di + 8) % 8, (j + dj + 4) % 4)

    def row_copies(pairs, base):
        return [
            pltpu.make_async_remote_copy(
                src,
                dst,
                halo_send.at[base + n],
                halo_recv.at[base + n],
                device_id=neighbour(di, 0),
                device_id_type=MESH,
            )
            for n, ((src, dst), di) in enumerate(zip(pairs, (-1, 1)))
        ]

    def corner_copies(base):
        cs = []
        for n, (di, dj) in enumerate(((-1, -1), (-1, 1), (1, -1), (1, 1))):
            slot_n = base // 8 * 4 + n
            cs.append(
                pltpu.make_async_remote_copy(
                    corner_out.at[slot_n],
                    corner_in.at[slot_n],
                    halo_send.at[base + 4 + n],
                    halo_recv.at[base + 4 + n],
                    device_id=neighbour(di, dj),
                    device_id_type=MESH,
                )
            )
        return cs

    def col_copies(base):
        cs = []
        for n, dj in enumerate((-1, 1)):
            slot_n = base // 8 * 2 + n
            cs.append(
                pltpu.make_async_remote_copy(
                    col_b.at[slot_n],
                    halo_b.at[slot_n],
                    halo_send.at[base + 2 + n],
                    halo_recv.at[base + 2 + n],
                    device_id=neighbour(0, dj),
                    device_id_type=MESH,
                )
            )
        return cs

    def put_corners(base):
        s = base // 8 * 4
        for n, (side, h) in enumerate(((0, 0), (1, 0), (0, 127), (1, 127))):
            corner_out[s + n] = jnp.broadcast_to(col_f[side, h : h + 1, :], (8, 128))

    def put_columns(base):
        s = base // 8 * 2
        for side in range(2):
            col_b[s + side] = col_f[side].astype(BF16)

    left_ok = jnp.where(j > 0, 1.0, 0.0)
    right_ok = jnp.where(j < 3, 1.0, 0.0)
    up_ok = jnp.where(i > 0, 1.0, 0.0)
    down_ok = jnp.where(i < 7, 1.0, 0.0)

    def take_columns(base, copies):
        for c in copies:
            c.wait()
        s2 = base // 8 * 2
        halo_f[0, 8:136, :] = halo_b[s2 + 1].astype(F32) * left_ok
        halo_f[1, 8:136, :] = halo_b[s2 + 0].astype(F32) * right_ok

    def take_corners(base):
        s4 = base // 8 * 4
        halo_f[0, 0:8, :] = corner_in[s4 + 3] * (left_ok * up_ok)
        halo_f[1, 0:8, :] = corner_in[s4 + 2] * (right_ok * up_ok)
        halo_f[0, 136:144, :] = corner_in[s4 + 1] * (left_ok * down_ok)
        halo_f[1, 136:144, :] = corner_in[s4 + 0] * (right_ok * down_ok)

    put_corners(0)
    mid = pl.ds(16, 128)
    rows1 = row_copies(
        [(row_out.at[0], rows_halo.at[1, mid]), (row_out.at[1], rows_halo.at[0, mid])], 0
    ) + corner_copies(0)
    cols1 = col_copies(0)
    for c in rows1[2:] + rows1[:2] + cols1:
        c.start()

    cell = jnp.dot(sel[...], terms, preferred_element_type=F32)
    cell = cell[:, 0:128] + cell[:, 128:256]
    patch[9] = cell
    hi, low = split2(cell)
    tapped = jnp.dot(jnp.concatenate([hi, low], axis=1), wtap[...], preferred_element_type=F32)
    for n in range(9):
        patch[n] = tapped[:, n * 128 : (n + 1) * 128]
    for b in range(3):
        rhs = []
        for col in range(PATCH):
            parts = [
                patch[a * 3 + b, pl.ds(col, 16, stride=PATCH), :] for a in range(3)
            ]
            hi, low = split2(jnp.concatenate(parts, axis=0))
            rhs.append(jnp.concatenate([hi, low, hi], axis=0))
        got = jnp.dot(
            lhs_tap_row[...], jnp.concatenate(rhs, axis=1), preferred_element_type=F32
        )
        for col in range(PATCH):
            taps[pl.ds(b * 16 + col, 128, stride=48), :] = got[:, col * 128 : (col + 1) * 128]

    def sum_up(carry, v):
        total, square = carry
        v3 = v.reshape(v.shape[0] // 8, 8, 128)
        return total + jnp.sum(v3, axis=0), square + jnp.sum(v3 * v3, axis=0)

    def add_taps(n, carry):
        rhs = []
        for q in range(16):
            h = n * 16 + q
            hi, low = split2(taps[pl.ds(pl.multiple_of(h * 48, 16), 48), :])
            rhs.append(jnp.concatenate([hi, low, hi], axis=0))
        got = jnp.dot(
            lhs_tap_col[...], jnp.concatenate(rhs, axis=1), preferred_element_type=F32
        )
        for q in range(16):
            h = n * 16 + q
            v = field[at_row(h), :] + got[:, q * 128 : (q + 1) * 128]
            field[at_row(h), :] = v
            carry = sum_up(carry, v)
        return carry

    zero8 = jnp.zeros((8, 128), F32)
    sums = lax.fori_loop(0, 8, add_taps, (zero8, zero8))

    def correct(carry, place, delta):
        old = field[place, :]
        new = old + delta
        field[place, :] = new
        d3 = delta.reshape(16, 8, 128)
        q3 = (new * new - old * old).reshape(16, 8, 128)
        return carry[0] + jnp.sum(d3, axis=0), carry[1] + jnp.sum(q3, axis=0)

    def add_borders(base, rows, columns, k, carry):
        n = base // 8 * 2
        take_columns(base, columns)
        for c in rows:
            c.wait()
        take_corners(base)
        for side, ok in ((0, up_ok), (1, down_ok)):
            v = rows_halo[n + side, 16:144].astype(F32) * ok
            rows_halo[n + side, 16:144] = v.astype(BF16)
            last = pltpu.roll(v[112:128], 1, 0)
            rows_halo[n + side, 0:16] = jnp.where(sub == 0, 0.0, last).astype(BF16)
            first = pltpu.roll(v[0:16], 15, 0)
            rows_halo[n + side, 144:160] = jnp.where(sub == 15, 0.0, first).astype(BF16)
        for side in range(2):
            lhs = [halo_f[side, 7 + a : 135 + a, :].astype(BF16) for a in range(3)]
            rhs = jnp.concatenate([k[a, 2 * side] for a in range(3)], axis=0)
            delta = jnp.dot(jnp.concatenate(lhs, axis=1), rhs, preferred_element_type=F32)
            carry = correct(carry, pl.ds(side * 127, 128, stride=128), delta)
        for side in range(2):
            lhs = [rows_halo[n + side, b * 16 : b * 16 + 128] for b in range(3)]
            rhs = jnp.concatenate([k[2 * side, b] for b in range(3)], axis=0)
            delta = jnp.dot(jnp.concatenate(lhs, axis=1), rhs, preferred_element_type=F32)
            carry = correct(carry, pl.ds(side * 127 * 128, 128), delta)
        return carry

    loads[3].wait()
    two_rows(k2, wb2)
    for b in range(PATCH, 16):
        partial[pl.ds(b, 128, stride=16), :] = jnp.zeros((128, 128), F32)
    sums = add_borders(0, rows1, cols1, k1, sums)

    lane8 = lax.broadcasted_iota(jnp.int32, (8, 128), 1)
    odd = (lane8 & 1) == 1
    high = (lane8 & 2) == 2
    number = float(TILE * TILE * 32 * (C // GROUPS))

    def norm_terms(n, sums, gain, shift, meanwhile=None):
        total, square = (jnp.sum(s, axis=0, keepdims=True) for s in sums)
        sub8 = lax.broadcasted_iota(jnp.int32, (8, 128), 0)
        mine = jnp.where(sub8 == 0, total, jnp.where(sub8 == 1, square, 0.0))
        st_out[n] = mine
        st_in[n, 0] = mine
        def send(t, c):
            k = far_first(t)
            pltpu.make_async_remote_copy(
                st_out.at[n],
                st_in.at[n, k],
                st_sem.at[n, 0],
                st_sem.at[n, 1],
                device_id=me ^ k,
                device_id_type=FLAT,
            ).start()
            return c

        lax.fori_loop(96, 127, send, 0)
        if meanwhile is not None:
            meanwhile()
        whole(st_in.at[n, pl.ds(1, 31)], st_sem.at[n, 1]).wait()
        both = jnp.sum(st_in[n], axis=0)
        both = both + jnp.where(odd, pltpu.roll(both, 1, 1), pltpu.roll(both, 127, 1))
        both = both + jnp.where(high, pltpu.roll(both, 2, 1), pltpu.roll(both, 126, 1))
        mean = both[0:1] / number
        spread = both[1:2] / number - mean * mean
        scale = lax.rsqrt(spread + 1e-05) * gain
        whole(st_in.at[n, pl.ds(1, 31)], st_sem.at[n, 0]).wait()
        return scale, shift - mean * scale

    scale, offset = norm_terms(0, sums, vectors[0], vectors[1], form_mixed)

    def hide(place):
        return silu(field[place, :] * scale + offset)

    for side in range(2):
        col_b[2 + side] = hide(pl.ds(side * 127, 128, stride=128)).astype(BF16)
        col_f[side] = col_b[2 + side].astype(F32)
        row_out[2 + side] = hide(pl.ds(side * 127 * 128, 128)).astype(BF16)
    put_corners(8)
    rows2 = row_copies(
        [(row_out.at[2], rows_halo.at[3, mid]), (row_out.at[3], rows_halo.at[2, mid])], 8
    ) + corner_copies(8)
    cols2 = col_copies(8)
    for c in rows2[2:] + rows2[:2] + cols2:
        c.start()

    def hide_row(h):
        v = hide(pl.ds(h * 128, 128))
        x2[h + 1, 16:144] = v.astype(BF16)
        x2[h + 1, 0:16] = jnp.where(sub == 0, 0.0, pltpu.roll(v[112:128], 1, 0)).astype(BF16)
        x2[h + 1, 144:160] = jnp.where(sub == 15, 0.0, pltpu.roll(v[0:16], 15, 0)).astype(BF16)

    many = 2 * PAIRS
    for h in range(many + 1):
        hide_row(h)
    sums = (zero8, zero8)
    for t in range(TILE // many):
        for h in range((t + 1) * many + 1, min((t + 2) * many + 1, TILE)):
            hide_row(h)
        for h, v in conv_block(x2, wb2, t):
            field[pl.ds(h * 128, 128), :] = v
            sums = sum_up(sums, v)
    sums = add_borders(8, rows2, cols2, k2, sums)
    scale2, offset2 = norm_terms(1, sums, vectors[2], vectors[3])

    terms_out[0:1, :] = scale2
    terms_out[1:2, :] = offset2
    whole(rows_in.at[pl.ds(1, 127)], row_sem.at[0]).wait()


def result_kernel(field, mixed, terms, out_hbm, stage, swap, sem):
    scale = terms[0:1, :]
    offset = terms[1:2, :]

    def finish(n, c):
        for q in range(8):
            h = n * 8 + q
            v = silu(field[pl.ds(pl.multiple_of(h * 128, 128), 128), :] * scale + offset)
            v = mixed[h].astype(F32) + v
            for s in range(8):
                swap[q, pl.ds(s, 16, stride=8), :] = v[s * 16 : (s + 1) * 16]
        for q in range(8):
            stage[n * 8 + q] = swap[q].astype(BF16)
        rows = pl.ds(n * 8, 8)
        pltpu.make_async_copy(stage.at[rows], out_hbm.at[rows], sem).start()
        return c

    lax.fori_loop(0, 16, finish, 0)
    pltpu.make_async_copy(stage, out_hbm, sem).wait()


def body(
    noisy_field,
    coarse_cells,
    coarse_proj,
    kernel_first,
    kernel_second,
    gain_first,
    shift_first,
    gain_second,
    shift_second,
    request_ids,
    patch_slots,
    tile_offsets,
):
    hbm = pl.BlockSpec(memory_space=pl.ANY)
    vmem = pl.BlockSpec(memory_space=pltpu.VMEM)
    row = lambda v: v.reshape(1, C)
    second, mixed, terms = pl.pallas_call(
        kernel,
        out_shape=[
            pltpu.VMEM((TILE * TILE, C), F32),
            pltpu.VMEM((TILE, TILE, C), BF16),
            pltpu.VMEM((8, C), F32),
        ],
        in_specs=[hbm] * 12,
        out_specs=[vmem] * 3,
        scratch_shapes=[
            pltpu.VMEM((4, 1, C), F32),
            pltpu.VMEM((MOST, 1, 128), jnp.int32),
            pltpu.VMEM((1, PATCH * PATCH), jnp.int32),
            pltpu.SMEM((1, 2), jnp.int32),
            pltpu.VMEM((TILE, TILE, C), BF16),
            pltpu.VMEM((HELD, CC), F32),
            pltpu.VMEM((CC, C), F32),
            pltpu.VMEM((3, 3, C, C), BF16),
            pltpu.VMEM((3, 3, C, C), BF16),
            pltpu.VMEM((12 * C, 2 * C), BF16),
            pltpu.VMEM((12 * C, 2 * C), BF16),
            pltpu.VMEM((128, 128), F32),
            pltpu.VMEM((128, 1, 128), F32),
            pltpu.VMEM((128, 1, 128), F32),
            pltpu.VMEM((HELD, 2 * C), BF16),
            pltpu.VMEM((128, MOST, C), F32),
            pltpu.VMEM((128, MOST, C), F32),
            pltpu.VMEM((8, 256), jnp.int32),
            pltpu.VMEM((256, MOST * 128), BF16),
            pltpu.VMEM((10, 256, C), F32),
            pltpu.VMEM((TILE * 16, C), F32),
            pltpu.VMEM((4, 128, C), BF16),
            pltpu.VMEM((TILE * 48, C), F32),
            pltpu.VMEM((128, 256), BF16),
            pltpu.VMEM((128, 144), BF16),
            pltpu.VMEM((128, 144), BF16),
            pltpu.VMEM((128, MOST * 128), BF16),
            pltpu.VMEM((2, 128, C), F32),
            pltpu.VMEM((256, 9 * C), BF16),
            pltpu.VMEM((4, 160, C), BF16),
            pltpu.VMEM((TILE + 2, 160, C), BF16),
            pltpu.VMEM((2, TILE, C), F32),
            pltpu.VMEM((4, TILE, C), BF16),
            pltpu.VMEM((4, TILE, C), BF16),
            pltpu.VMEM((2, 144, C), F32),
            pltpu.VMEM((8, 8, C), F32),
            pltpu.VMEM((8, 8, C), F32),
            pltpu.VMEM((2, 8, C), F32),
            pltpu.VMEM((2, 32, 8, C), F32),
            pltpu.SemaphoreType.DMA((12,)),
            pltpu.SemaphoreType.DMA((2,)),
            pltpu.SemaphoreType.DMA((2,)),
            pltpu.SemaphoreType.DMA((2, 2)),
            pltpu.SemaphoreType.DMA((16,)),
            pltpu.SemaphoreType.DMA((16,)),
        ],
        compiler_params=pltpu.CompilerParams(
            collective_id=0, has_side_effects=True, vmem_limit_bytes=50 << 20
        ),
        name="block",
    )(
        noisy_field.reshape(TILE, TILE, C),
        coarse_cells,
        coarse_proj,
        kernel_first,
        kernel_second,
        row(gain_first),
        row(shift_first),
        row(gain_second),
        row(shift_second),
        request_ids.transpose(0, 1, 4, 2, 3).reshape(MOST, 1, 128),
        patch_slots.reshape(1, PATCH * PATCH),
        tile_offsets.reshape(1, 2),
    )
    got = pl.pallas_call(
        result_kernel,
        out_shape=jax.ShapeDtypeStruct((TILE, TILE, C), BF16),
        in_specs=[vmem] * 3,
        out_specs=hbm,
        scratch_shapes=[
            pltpu.VMEM((TILE, TILE, C), BF16),
            pltpu.VMEM((8, TILE, C), F32),
            pltpu.SemaphoreType.DMA,
        ],
        compiler_params=pltpu.CompilerParams(vmem_limit_bytes=10 << 20),
        name="result",
    )(second, mixed, terms)
    return got[None]


def solution(mesh):
    return jax.shard_map(
        body,
        mesh=mesh,
        in_specs=(
            P("region", "row", "col", None),
            P(("region", "row", "col"), None),
            P(),
            P(),
            P(),
            P(),
            P(),
            P(),
            P(),
            P("region", "row", "col", None, None),
            P("region", "row", "col", None),
            P("region", "row", "col", None),
        ),
        out_specs=P("region", "row", "col", None),
        check_vma=False,
    )
```

```python
import functools

import jax
import jax.numpy as jnp
from jax import lax
from jax.experimental import pallas as pl
from jax.experimental.pallas import tpu as pltpu
from jax.sharding import PartitionSpec as P

GROUPS = 32
STEP = 9
PATCH = 13
MOST = 6
TILE = 128
C = 128
CC = 640
HELD = 256
AXES = ("region", "row", "col")
MESH = pl.DeviceIdType.MESH
FLAT = pl.DeviceIdType.LOGICAL
F32 = jnp.float32
BF16 = jnp.bfloat16
PAIRS = 16


def split3(x):
    hi = x.astype(BF16)
    rest = x - hi.astype(F32)
    mid = rest.astype(BF16)
    lo = (rest - mid.astype(F32)).astype(BF16)
    return hi, mid, lo


def split2(x):
    hi = x.astype(BF16)
    return hi, (x - hi.astype(F32)).astype(BF16)


def cubic(distance):
    near_part = (1.5 * distance - 2.5) * distance * distance + 1.0
    far_part = ((-0.5 * distance + 2.5) * distance - 4.0) * distance + 2.0
    return jnp.where(distance < 1.0, near_part, jnp.where(distance < 2.0, far_part, 0.0))


def weight_terms(point, lane, offset):
    position = (offset.astype(F32) + point.astype(F32) * STEP) / 128.0 + 1.0
    cell = lane % 16
    group = lane // 16
    weight = cubic(jnp.abs(position - cell.astype(F32)))
    weight = jnp.where(cell < PATCH, weight, 0.0)
    hi, mid, lo = (t.astype(F32) for t in split3(weight))
    return jnp.where(group < 3, hi, jnp.where(group < 5, mid, jnp.where(group < 6, lo, 0.0)))


def tap_terms(point, lane, offset):
    group = (lane * 1366) >> 16
    rest = lane - group * 48
    point = point + (rest >> 4) - 1
    cell = rest & 15
    position = (offset.astype(F32) + point.astype(F32) * STEP) / 128.0 + 1.0
    weight = cubic(jnp.abs(position - cell.astype(F32)))
    weight = jnp.where((cell < PATCH) & (point >= 0) & (point < TILE), weight, 0.0)
    hi, mid, _ = (t.astype(F32) for t in split3(weight))
    return jnp.where(group < 2, hi, jnp.where(group < 3, mid, 0.0))


def silu(v):
    return v * jax.nn.sigmoid(v)


def far_first(n):
    return (~n & 0b1010100) | ((n ^ (n >> 1)) & 0b0101010) | (~n & 1)


def kernel(
    noisy_hbm,
    cells_hbm,
    proj_hbm,
    k1_hbm,
    k2_hbm,
    g1_hbm,
    s1_hbm,
    g2_hbm,
    s2_hbm,
    ids_hbm,
    slots_hbm,
    off_hbm,
    field,
    mixed,
    terms_out,
    vectors,
    ids_ref,
    slots_ref,
    off_ref,
    noisy,
    cells,
    proj,
    k1,
    k2,
    wb1,
    wb2,
    id_rows,
    id_buf,
    id_recv,
    pcat,
    rows_out,
    rows_in,
    slot_row,
    sel,
    patch,
    partial,
    row_out,
    taps,
    lhs_col,
    lhs_tap_row,
    lhs_tap_col,
    edge_rows,
    noisy_col,
    wtap,
    rows_halo,
    x2,
    col_f,
    col_b,
    halo_b,
    halo_f,
    corner_out,
    corner_in,
    st_out,
    st_in,
    ld_sem,
    id_sem,
    row_sem,
    st_sem,
    halo_send,
    halo_recv,
):
    g, i, j = (lax.axis_index(a) for a in AXES)
    me = g * 32 + i * 4 + j

    loads = [
        pltpu.make_async_copy(a, b, ld_sem.at[n])
        for n, (a, b) in enumerate(
            [
                (cells_hbm, cells),
                (proj_hbm, proj),
                (k1_hbm, k1),
                (k2_hbm, k2),
                (noisy_hbm, noisy),
                (ids_hbm, ids_ref),
                (slots_hbm, slots_ref),
                (off_hbm, off_ref),
                (g1_hbm, vectors.at[0]),
                (s1_hbm, vectors.at[1]),
                (g2_hbm, vectors.at[2]),
                (s2_hbm, vectors.at[3]),
            ]
        )
    ]
    loads[5].start()
    barrier = pltpu.get_barrier_semaphore()

    def greet(n, c):
        pl.semaphore_signal(barrier, inc=1, device_id=me ^ far_first(n), device_id_type=FLAT)
        return c

    lax.fori_loop(0, 126, greet, 0, unroll=6)
    greet(126, 0)
    for c in loads[:5] + loads[6:]:
        c.start()
    loads[5].wait()

    id_rows[...] = jnp.zeros_like(id_rows)
    id_rows[0:MOST, :] = ids_ref[:, 0, :].astype(F32)
    id_buf[:, 0, :] = jnp.transpose(id_rows[...])
    id_recv[0] = id_buf[me]
    pl.semaphore_wait(barrier, 127)

    def send_ids(n, c):
        k = far_first(n)
        pltpu.make_async_remote_copy(
            id_buf.at[me ^ k], id_recv.at[k], id_sem.at[0], id_sem.at[1], device_id=me ^ k, device_id_type=FLAT
        ).start()
        return c

    lax.fori_loop(0, 126, send_ids, 0, unroll=6)
    send_ids(126, 0)

    for n in (0, 1, 6, 7, 8, 9, 10, 11):
        loads[n].wait()
    projected = jnp.dot(
        cells[...], proj[...], precision=lax.Precision.HIGHEST, preferred_element_type=F32
    )
    for n, term in enumerate(split2(projected)):
        pcat[:, n * 128 : (n + 1) * 128] = term
    for b in range(PATCH, 16):
        for n in range(3):
            taps[pl.ds(n * 16 + b, 128, stride=48), :] = jnp.zeros((128, 128), F32)

    slot_row[...] = jnp.full_like(slot_row, -1)
    slot_row[0:1, 0 : PATCH * PATCH] = slots_ref[...]
    slot = slot_row[0:1, :]
    owner = (slot * 10923) >> 16
    place = slot - owner * MOST
    index = place * 128 + (owner ^ me)
    index = jnp.where(slot < 0, -1, index).astype(F32)
    index = jnp.transpose(jnp.broadcast_to(index, (128, 256)))
    lane = lax.broadcasted_iota(jnp.int32, (256, 128), 1).astype(F32)
    for n in range(MOST):
        sel[:, n * 128 : (n + 1) * 128] = jnp.where(index == lane + 128.0 * n, 1.0, 0.0).astype(BF16)

    r_iota = lax.broadcasted_iota(jnp.int32, (128, 128), 0)
    l_iota = lax.broadcasted_iota(jnp.int32, (128, 128), 1)
    column = (r_iota % 16) * 8 + r_iota // 16
    lhs_col[:, 0:128] = weight_terms(column, l_iota, off_ref[0, 1]).astype(BF16)
    lhs_col[:, 128:256] = jnp.where(column == l_iota, 1.0, 0.0).astype(BF16)
    lhs_row = weight_terms(r_iota, l_iota, off_ref[0, 0]).astype(BF16)
    r_tap = lax.broadcasted_iota(jnp.int32, (128, 144), 0)
    l_tap = lax.broadcasted_iota(jnp.int32, (128, 144), 1)
    lhs_tap_row[...] = tap_terms(r_tap, l_tap, off_ref[0, 0]).astype(BF16)
    lhs_tap_col[...] = tap_terms((r_tap % 16) * 8 + r_tap // 16, l_tap, off_ref[0, 1]).astype(BF16)
    e_row = lax.broadcasted_iota(jnp.int32, (64, 256), 0)
    p_cell = lax.broadcasted_iota(jnp.int32, (64, 256), 1)
    p_row = (p_cell * 5042) >> 16
    p_col = p_cell - p_row * PATCH
    on_rows = e_row < 32
    point = jnp.where((e_row & 16) == 0, 0, TILE - 1)
    start = jnp.where(on_rows, off_ref[0, 0], off_ref[0, 1])
    position = (start.astype(F32) + point.astype(F32) * STEP) / 128.0 + 1.0
    weight = cubic(jnp.abs(position - jnp.where(on_rows, p_row, p_col).astype(F32)))
    keep = (jnp.where(on_rows, p_col, p_row) == (e_row & 15)) & (p_cell < PATCH * PATCH)
    edge_terms = jnp.concatenate(split2(jnp.where(keep, weight, 0.0)), axis=0)
    edge_rows[...] = jnp.dot(edge_terms, sel[...], preferred_element_type=F32).astype(BF16)

    loads[2].wait()
    zero_block = jnp.zeros((128, 128), BF16)

    def two_rows(w, wb):
        for a in range(4):
            for b in range(3):
                for e in range(2):
                    block = w[a - e, b] if 0 <= a - e <= 2 else zero_block
                    wb[(a * 3 + b) * 128 : (a * 3 + b + 1) * 128, e * 128 : (e + 1) * 128] = block

    two_rows(k1, wb1)
    for a in range(3):
        for b in range(3):
            n = a * 3 + b
            wtap[0:128, n * 128 : (n + 1) * 128] = k1[a, b]
            wtap[128:256, n * 128 : (n + 1) * 128] = k1[a, b]

    sub = lax.broadcasted_iota(jnp.int32, (16, 128), 0)
    x2[0] = jnp.zeros((160, 128), BF16)
    x2[TILE + 1] = jnp.zeros((160, 128), BF16)
    loads[4].wait()

    def reorder(n, c):
        h0 = n * 16
        got = jnp.dot(
            lhs_col[:, 128:256],
            jnp.concatenate([noisy[h0 + q] for q in range(16)], axis=1),
            preferred_element_type=F32,
        )
        for q in range(16):
            v = got[:, q * 128 : (q + 1) * 128]
            h = h0 + q
            x2[h + 1, 16:144] = v.astype(BF16)
            x2[h + 1, 0:16] = jnp.where(sub == 0, 0.0, pltpu.roll(v[112:128], 1, 0)).astype(BF16)
            x2[h + 1, 144:160] = jnp.where(sub == 15, 0.0, pltpu.roll(v[0:16], 15, 0)).astype(BF16)
            noisy_col[0, pl.ds(h, 1), :] = v[0:1]
            noisy_col[1, pl.ds(h, 1), :] = v[127:128]
        return c

    lax.fori_loop(0, 8, reorder, 0)

    def conv_block(x, wb, t, pairs=PAIRS):
        y = t * (2 * pairs)
        lhs = []
        for q in range(pairs):
            parts = [
                x[y + 2 * q + a, b * 16 : b * 16 + 128] for a in range(4) for b in range(3)
            ]
            lhs.append(jnp.concatenate(parts, axis=1))
        got = jnp.dot(jnp.concatenate(lhs, axis=0), wb[...], preferred_element_type=F32)
        for q in range(pairs):
            for e in range(2):
                yield y + 2 * q + e, got[q * 128 : (q + 1) * 128, e * 128 : (e + 1) * 128]

    def at_row(h):
        return pl.ds(pl.multiple_of(h * 128, 128), 128)

    def conv_noisy(t, c):
        for h, v in conv_block(x2, wb1, t, 32):
            field[at_row(h), :] = v
        return c

    def whole(ref, sem):
        return pltpu.make_async_copy(ref, ref, sem)

    whole(id_recv.at[pl.ds(1, 127)], id_sem.at[1]).wait()
    asked = id_recv[:, 0, :] - (me * HELD).astype(F32)
    row_iota = lax.broadcasted_iota(jnp.int32, (128, HELD), 1).astype(F32)
    hot = [
        jnp.where(asked[:, m : m + 1] == row_iota, 1.0, 0.0).astype(BF16) for m in range(MOST)
    ]
    found = jnp.dot(jnp.concatenate(hot, axis=0), pcat[...], preferred_element_type=F32)
    found = found[:, 0:128] + found[:, 128:256]
    for m in range(MOST):
        rows_out[:, m, :] = found[m * 128 : (m + 1) * 128]
    rows_in[0] = rows_out[0]

    def send_rows(n, c):
        k = far_first(n)
        pltpu.make_async_remote_copy(
            rows_out.at[k],
            rows_in.at[k],
            row_sem.at[0],
            row_sem.at[1],
            device_id=me ^ k,
            device_id_type=FLAT,
        ).start()
        return c

    lax.fori_loop(0, 126, send_rows, 0, unroll=6)
    send_rows(126, 0)
    lax.fori_loop(0, 2, conv_noisy, 0)
    whole(id_buf.at[pl.ds(1, 127)], id_sem.at[0]).wait()
    whole(rows_in.at[pl.ds(1, 127)], row_sem.at[1]).wait()

    terms = [jnp.concatenate(split2(rows_in[:, m, :]), axis=1) for m in range(MOST)]
    terms = jnp.concatenate(terms, axis=0)
    zero_tile = jnp.zeros((32, 128), BF16)

    def stack_terms(x):
        hi, mid, lo = split3(x)
        return jnp.concatenate([hi, mid, lo, hi, mid, hi, zero_tile], axis=0)

    got = jnp.dot(edge_rows[...], terms, preferred_element_type=F32)
    got = got[:, 0:128] + got[:, 128:256]
    ends = got[0:64] + got[64:128]
    for side in range(2):
        h = side * (TILE - 1)
        rhs = jnp.concatenate([stack_terms(ends[side * 16 : side * 16 + 16]), noisy[h]], axis=0)
        row_out[side] = jnp.dot(lhs_col[...], rhs, preferred_element_type=F32).astype(BF16)
        rhs = stack_terms(ends[32 + side * 16 : 48 + side * 16])
        got = noisy_col[side] + jnp.dot(lhs_row, rhs, preferred_element_type=F32)
        col_b[side] = got.astype(BF16)
        col_f[side] = col_b[side].astype(F32)

    def form_mixed():
        for b in range(PATCH):
            rhs = stack_terms(patch[9, pl.ds(b, 16, stride=PATCH), :])
            partial[pl.ds(b, 128, stride=16), :] = jnp.dot(
                lhs_row, rhs, preferred_element_type=F32
            )

        def step(n, c):
            rhs = []
            for q in range(16):
                h = n * 16 + q
                t = stack_terms(partial[pl.ds(pl.multiple_of(h * 16, 16), 16), :])
                rhs.append(jnp.concatenate([t, noisy[h]], axis=0))
            got = jnp.dot(
                lhs_col[...], jnp.concatenate(rhs, axis=1), preferred_element_type=F32
            ).astype(BF16)
            for q in range(16):
                mixed[n * 16 + q] = got[:, q * 128 : (q + 1) * 128]
            return c

        lax.fori_loop(0, 8, step, 0)

    def neighbour(di, dj):
        return (g, (i + di + 8) % 8, (j + dj + 4) % 4)

    def row_copies(pairs, base):
        return [
            pltpu.make_async_remote_copy(
                src,
                dst,
                halo_send.at[base + n],
                halo_recv.at[base + n],
                device_id=neighbour(di, 0),
                device_id_type=MESH,
            )
            for n, ((src, dst), di) in enumerate(zip(pairs, (-1, 1)))
        ]

    def corner_copies(base):
        cs = []
        for n, (di, dj) in enumerate(((-1, -1), (-1, 1), (1, -1), (1, 1))):
            slot_n = base // 8 * 4 + n
            cs.append(
                pltpu.make_async_remote_copy(
                    corner_out.at[slot_n],
                    corner_in.at[slot_n],
                    halo_send.at[base + 4 + n],
                    halo_recv.at[base + 4 + n],
                    device_id=neighbour(di, dj),
                    device_id_type=MESH,
                )
            )
        return cs

    def col_copies(base):
        cs = []
        for n, dj in enumerate((-1, 1)):
            slot_n = base // 8 * 2 + n
            cs.append(
                pltpu.make_async_remote_copy(
                    col_b.at[slot_n],
                    halo_b.at[slot_n],
                    halo_send.at[base + 2 + n],
                    halo_recv.at[base + 2 + n],
                    device_id=neighbour(0, dj),
                    device_id_type=MESH,
                )
            )
        return cs

    def put_corners(base):
        s = base // 8 * 4
        for n, (side, h) in enumerate(((0, 0), (1, 0), (0, 127), (1, 127))):
            corner_out[s + n] = jnp.broadcast_to(col_f[side, h : h + 1, :], (8, 128))

    def put_columns(base):
        s = base // 8 * 2
        for side in range(2):
            col_b[s + side] = col_f[side].astype(BF16)

    left_ok = jnp.where(j > 0, 1.0, 0.0)
    right_ok = jnp.where(j < 3, 1.0, 0.0)
    up_ok = jnp.where(i > 0, 1.0, 0.0)
    down_ok = jnp.where(i < 7, 1.0, 0.0)

    def take_columns(base, copies):
        for c in copies:
            c.wait()
        s2 = base // 8 * 2
        halo_f[0, 8:136, :] = halo_b[s2 + 1].astype(F32) * left_ok
        halo_f[1, 8:136, :] = halo_b[s2 + 0].astype(F32) * right_ok

    def take_corners(base):
        s4 = base // 8 * 4
        halo_f[0, 0:8, :] = corner_in[s4 + 3] * (left_ok * up_ok)
        halo_f[1, 0:8, :] = corner_in[s4 + 2] * (right_ok * up_ok)
        halo_f[0, 136:144, :] = corner_in[s4 + 1] * (left_ok * down_ok)
        halo_f[1, 136:144, :] = corner_in[s4 + 0] * (right_ok * down_ok)

    put_corners(0)
    mid = pl.ds(16, 128)
    rows1 = row_copies(
        [(row_out.at[0], rows_halo.at[1, mid]), (row_out.at[1], rows_halo.at[0, mid])], 0
    ) + corner_copies(0)
    cols1 = col_copies(0)
    for c in rows1[2:] + rows1[:2] + cols1:
        c.start()

    cell = jnp.dot(sel[...], terms, preferred_element_type=F32)
    cell = cell[:, 0:128] + cell[:, 128:256]
    patch[9] = cell
    hi, low = split2(cell)
    tapped = jnp.dot(jnp.concatenate([hi, low], axis=1), wtap[...], preferred_element_type=F32)
    for n in range(9):
        patch[n] = tapped[:, n * 128 : (n + 1) * 128]
    for b in range(3):
        rhs = []
        for col in range(PATCH):
            parts = [
                patch[a * 3 + b, pl.ds(col, 16, stride=PATCH), :] for a in range(3)
            ]
            hi, low = split2(jnp.concatenate(parts, axis=0))
            rhs.append(jnp.concatenate([hi, low, hi], axis=0))
        got = jnp.dot(
            lhs_tap_row[...], jnp.concatenate(rhs, axis=1), preferred_element_type=F32
        )
        for col in range(PATCH):
            taps[pl.ds(b * 16 + col, 128, stride=48), :] = got[:, col * 128 : (col + 1) * 128]

    def sum_up(carry, v):
        total, square = carry
        v3 = v.reshape(v.shape[0] // 8, 8, 128)
        return total + jnp.sum(v3, axis=0), square + jnp.sum(v3 * v3, axis=0)

    def add_taps(n, carry):
        rhs = []
        for q in range(16):
            h = n * 16 + q
            hi, low = split2(taps[pl.ds(pl.multiple_of(h * 48, 16), 48), :])
            rhs.append(jnp.concatenate([hi, low, hi], axis=0))
        got = jnp.dot(
            lhs_tap_col[...], jnp.concatenate(rhs, axis=1), preferred_element_type=F32
        )
        for q in range(16):
            h = n * 16 + q
            v = field[at_row(h), :] + got[:, q * 128 : (q + 1) * 128]
            field[at_row(h), :] = v
            carry = sum_up(carry, v)
        return carry

    zero8 = jnp.zeros((8, 128), F32)
    sums = lax.fori_loop(0, 8, add_taps, (zero8, zero8))

    def correct(carry, place, delta):
        old = field[place, :]
        new = old + delta
        field[place, :] = new
        d3 = delta.reshape(16, 8, 128)
        q3 = (new * new - old * old).reshape(16, 8, 128)
        return carry[0] + jnp.sum(d3, axis=0), carry[1] + jnp.sum(q3, axis=0)

    def add_borders(base, rows, columns, k, carry):
        n = base // 8 * 2
        take_columns(base, columns)
        for c in rows:
            c.wait()
        take_corners(base)
        for side, ok in ((0, up_ok), (1, down_ok)):
            v = rows_halo[n + side, 16:144].astype(F32) * ok
            rows_halo[n + side, 16:144] = v.astype(BF16)
            last = pltpu.roll(v[112:128], 1, 0)
            rows_halo[n + side, 0:16] = jnp.where(sub == 0, 0.0, last).astype(BF16)
            first = pltpu.roll(v[0:16], 15, 0)
            rows_halo[n + side, 144:160] = jnp.where(sub == 15, 0.0, first).astype(BF16)
        for side in range(2):
            lhs = [halo_f[side, 7 + a : 135 + a, :].astype(BF16) for a in range(3)]
            rhs = jnp.concatenate([k[a, 2 * side] for a in range(3)], axis=0)
            delta = jnp.dot(jnp.concatenate(lhs, axis=1), rhs, preferred_element_type=F32)
            carry = correct(carry, pl.ds(side * 127, 128, stride=128), delta)
        for side in range(2):
            lhs = [rows_halo[n + side, b * 16 : b * 16 + 128] for b in range(3)]
            rhs = jnp.concatenate([k[2 * side, b] for b in range(3)], axis=0)
            delta = jnp.dot(jnp.concatenate(lhs, axis=1), rhs, preferred_element_type=F32)
            carry = correct(carry, pl.ds(side * 127 * 128, 128), delta)
        return carry

    loads[3].wait()
    two_rows(k2, wb2)
    for b in range(PATCH, 16):
        partial[pl.ds(b, 128, stride=16), :] = jnp.zeros((128, 128), F32)
    sums = add_borders(0, rows1, cols1, k1, sums)

    lane8 = lax.broadcasted_iota(jnp.int32, (8, 128), 1)
    odd = (lane8 & 1) == 1
    high = (lane8 & 2) == 2
    number = float(TILE * TILE * 32 * (C // GROUPS))

    def norm_terms(n, sums, gain, shift, meanwhile=None):
        total, square = (jnp.sum(s, axis=0, keepdims=True) for s in sums)
        sub8 = lax.broadcasted_iota(jnp.int32, (8, 128), 0)
        mine = jnp.where(sub8 == 0, total, jnp.where(sub8 == 1, square, 0.0))
        st_out[n] = mine
        st_in[n, 0] = mine
        def send(t, c):
            k = far_first(t)
            pltpu.make_async_remote_copy(
                st_out.at[n],
                st_in.at[n, k],
                st_sem.at[n, 0],
                st_sem.at[n, 1],
                device_id=me ^ k,
                device_id_type=FLAT,
            ).start()
            return c

        for t in range(96, 127):
            send(t, 0)
        if meanwhile is not None:
            meanwhile()
        whole(st_in.at[n, pl.ds(1, 31)], st_sem.at[n, 1]).wait()
        both = jnp.sum(st_in[n], axis=0)
        both = both + jnp.where(odd, pltpu.roll(both, 1, 1), pltpu.roll(both, 127, 1))
        both = both + jnp.where(high, pltpu.roll(both, 2, 1), pltpu.roll(both, 126, 1))
        mean = both[0:1] / number
        spread = both[1:2] / number - mean * mean
        scale = lax.rsqrt(spread + 1e-05) * gain
        whole(st_in.at[n, pl.ds(1, 31)], st_sem.at[n, 0]).wait()
        return scale, shift - mean * scale

    scale, offset = norm_terms(0, sums, vectors[0], vectors[1], form_mixed)

    def hide(place):
        return silu(field[place, :] * scale + offset)

    for side in range(2):
        col_b[2 + side] = hide(pl.ds(side * 127, 128, stride=128)).astype(BF16)
        col_f[side] = col_b[2 + side].astype(F32)
        row_out[2 + side] = hide(pl.ds(side * 127 * 128, 128)).astype(BF16)
    put_corners(8)
    rows2 = row_copies(
        [(row_out.at[2], rows_halo.at[3, mid]), (row_out.at[3], rows_halo.at[2, mid])], 8
    ) + corner_copies(8)
    cols2 = col_copies(8)
    for c in rows2[2:] + rows2[:2] + cols2:
        c.start()

    def hide_row(h):
        v = hide(pl.ds(h * 128, 128))
        x2[h + 1, 16:144] = v.astype(BF16)
        x2[h + 1, 0:16] = jnp.where(sub == 0, 0.0, pltpu.roll(v[112:128], 1, 0)).astype(BF16)
        x2[h + 1, 144:160] = jnp.where(sub == 15, 0.0, pltpu.roll(v[0:16], 15, 0)).astype(BF16)

    many = 2 * PAIRS
    for h in range(many + 1):
        hide_row(h)
    sums = (zero8, zero8)
    for t in range(TILE // many):
        for h in range((t + 1) * many + 1, min((t + 2) * many + 1, TILE)):
            hide_row(h)
        for h, v in conv_block(x2, wb2, t):
            field[pl.ds(h * 128, 128), :] = v
            sums = sum_up(sums, v)
    sums = add_borders(8, rows2, cols2, k2, sums)
    scale2, offset2 = norm_terms(1, sums, vectors[2], vectors[3])

    terms_out[0:1, :] = scale2
    terms_out[1:2, :] = offset2
    whole(rows_in.at[pl.ds(1, 127)], row_sem.at[0]).wait()


def result_kernel(field, mixed, terms, out_hbm, stage, swap, sem):
    scale = terms[0:1, :]
    offset = terms[1:2, :]

    def finish(n, c):
        for q in range(8):
            h = n * 8 + q
            v = silu(field[pl.ds(pl.multiple_of(h * 128, 128), 128), :] * scale + offset)
            v = mixed[h].astype(F32) + v
            for s in range(8):
                swap[q, pl.ds(s, 16, stride=8), :] = v[s * 16 : (s + 1) * 16]
        for q in range(8):
            stage[n * 8 + q] = swap[q].astype(BF16)
        rows = pl.ds(n * 8, 8)
        pltpu.make_async_copy(stage.at[rows], out_hbm.at[rows], sem).start()
        return c

    lax.fori_loop(0, 16, finish, 0)
    pltpu.make_async_copy(stage, out_hbm, sem).wait()


def body(
    noisy_field,
    coarse_cells,
    coarse_proj,
    kernel_first,
    kernel_second,
    gain_first,
    shift_first,
    gain_second,
    shift_second,
    request_ids,
    patch_slots,
    tile_offsets,
):
    hbm = pl.BlockSpec(memory_space=pl.ANY)
    vmem = pl.BlockSpec(memory_space=pltpu.VMEM)
    row = lambda v: v.reshape(1, C)
    second, mixed, terms = pl.pallas_call(
        kernel,
        out_shape=[
            pltpu.VMEM((TILE * TILE, C), F32),
            pltpu.VMEM((TILE, TILE, C), BF16),
            pltpu.VMEM((8, C), F32),
        ],
        in_specs=[hbm] * 12,
        out_specs=[vmem] * 3,
        scratch_shapes=[
            pltpu.VMEM((4, 1, C), F32),
            pltpu.VMEM((MOST, 1, 128), jnp.int32),
            pltpu.VMEM((1, PATCH * PATCH), jnp.int32),
            pltpu.SMEM((1, 2), jnp.int32),
            pltpu.VMEM((TILE, TILE, C), BF16),
            pltpu.VMEM((HELD, CC), F32),
            pltpu.VMEM((CC, C), F32),
            pltpu.VMEM((3, 3, C, C), BF16),
            pltpu.VMEM((3, 3, C, C), BF16),
            pltpu.VMEM((12 * C, 2 * C), BF16),
            pltpu.VMEM((12 * C, 2 * C), BF16),
            pltpu.VMEM((128, 128), F32),
            pltpu.VMEM((128, 1, 128), F32),
            pltpu.VMEM((128, 1, 128), F32),
            pltpu.VMEM((HELD, 2 * C), BF16),
            pltpu.VMEM((128, MOST, C), F32),
            pltpu.VMEM((128, MOST, C), F32),
            pltpu.VMEM((8, 256), jnp.int32),
            pltpu.VMEM((256, MOST * 128), BF16),
            pltpu.VMEM((10, 256, C), F32),
            pltpu.VMEM((TILE * 16, C), F32),
            pltpu.VMEM((4, 128, C), BF16),
            pltpu.VMEM((TILE * 48, C), F32),
            pltpu.VMEM((128, 256), BF16),
            pltpu.VMEM((128, 144), BF16),
            pltpu.VMEM((128, 144), BF16),
            pltpu.VMEM((128, MOST * 128), BF16),
            pltpu.VMEM((2, 128, C), F32),
            pltpu.VMEM((256, 9 * C), BF16),
            pltpu.VMEM((4, 160, C), BF16),
            pltpu.VMEM((TILE + 2, 160, C), BF16),
            pltpu.VMEM((2, TILE, C), F32),
            pltpu.VMEM((4, TILE, C), BF16),
            pltpu.VMEM((4, TILE, C), BF16),
            pltpu.VMEM((2, 144, C), F32),
            pltpu.VMEM((8, 8, C), F32),
            pltpu.VMEM((8, 8, C), F32),
            pltpu.VMEM((2, 8, C), F32),
            pltpu.VMEM((2, 32, 8, C), F32),
            pltpu.SemaphoreType.DMA((12,)),
            pltpu.SemaphoreType.DMA((2,)),
            pltpu.SemaphoreType.DMA((2,)),
            pltpu.SemaphoreType.DMA((2, 2)),
            pltpu.SemaphoreType.DMA((16,)),
            pltpu.SemaphoreType.DMA((16,)),
        ],
        compiler_params=pltpu.CompilerParams(
            collective_id=0, has_side_effects=True, vmem_limit_bytes=50 << 20
        ),
        name="block",
    )(
        noisy_field.reshape(TILE, TILE, C),
        coarse_cells,
        coarse_proj,
        kernel_first,
        kernel_second,
        row(gain_first),
        row(shift_first),
        row(gain_second),
        row(shift_second),
        request_ids.transpose(0, 1, 4, 2, 3).reshape(MOST, 1, 128),
        patch_slots.reshape(1, PATCH * PATCH),
        tile_offsets.reshape(1, 2),
    )
    got = pl.pallas_call(
        result_kernel,
        out_shape=jax.ShapeDtypeStruct((TILE, TILE, C), BF16),
        in_specs=[vmem] * 3,
        out_specs=hbm,
        scratch_shapes=[
            pltpu.VMEM((TILE, TILE, C), BF16),
            pltpu.VMEM((8, TILE, C), F32),
            pltpu.SemaphoreType.DMA,
        ],
        compiler_params=pltpu.CompilerParams(vmem_limit_bytes=10 << 20),
        name="result",
    )(second, mixed, terms)
    return got[None]


def solution(mesh):
    return jax.shard_map(
        body,
        mesh=mesh,
        in_specs=(
            P("region", "row", "col", None),
            P(("region", "row", "col"), None),
            P(),
            P(),
            P(),
            P(),
            P(),
            P(),
            P(),
            P("region", "row", "col", None, None),
            P("region", "row", "col", None),
            P("region", "row", "col", None),
        ),
        out_specs=P("region", "row", "col", None),
        check_vma=False,
    )
```

```python
import functools

import jax
import jax.numpy as jnp
from jax import lax
from jax.experimental import pallas as pl
from jax.experimental.pallas import tpu as pltpu
from jax.sharding import PartitionSpec as P

GROUPS = 32
STEP = 9
PATCH = 13
MOST = 6
TILE = 128
C = 128
CC = 640
HELD = 256
AXES = ("region", "row", "col")
MESH = pl.DeviceIdType.MESH
FLAT = pl.DeviceIdType.LOGICAL
F32 = jnp.float32
BF16 = jnp.bfloat16
PAIRS = 16


def split3(x):
    hi = x.astype(BF16)
    rest = x - hi.astype(F32)
    mid = rest.astype(BF16)
    lo = (rest - mid.astype(F32)).astype(BF16)
    return hi, mid, lo


def split2(x):
    hi = x.astype(BF16)
    return hi, (x - hi.astype(F32)).astype(BF16)


def cubic(distance):
    near_part = (1.5 * distance - 2.5) * distance * distance + 1.0
    far_part = ((-0.5 * distance + 2.5) * distance - 4.0) * distance + 2.0
    return jnp.where(distance < 1.0, near_part, jnp.where(distance < 2.0, far_part, 0.0))


def weight_terms(point, lane, offset):
    position = (offset.astype(F32) + point.astype(F32) * STEP) / 128.0 + 1.0
    cell = lane % 16
    group = lane // 16
    weight = cubic(jnp.abs(position - cell.astype(F32)))
    weight = jnp.where(cell < PATCH, weight, 0.0)
    hi, mid, lo = (t.astype(F32) for t in split3(weight))
    return jnp.where(group < 3, hi, jnp.where(group < 5, mid, jnp.where(group < 6, lo, 0.0)))


def tap_terms(point, lane, offset):
    group = (lane * 1366) >> 16
    rest = lane - group * 48
    point = point + (rest >> 4) - 1
    cell = rest & 15
    position = (offset.astype(F32) + point.astype(F32) * STEP) / 128.0 + 1.0
    weight = cubic(jnp.abs(position - cell.astype(F32)))
    weight = jnp.where((cell < PATCH) & (point >= 0) & (point < TILE), weight, 0.0)
    hi, mid, _ = (t.astype(F32) for t in split3(weight))
    return jnp.where(group < 2, hi, jnp.where(group < 3, mid, 0.0))


def silu(v):
    return v * jax.nn.sigmoid(v)


def far_first(n):
    return (~n & 0b1010100) | ((n ^ (n >> 1)) & 0b0101010) | (~n & 1)


def kernel(
    noisy_hbm,
    cells_hbm,
    proj_hbm,
    k1_hbm,
    k2_hbm,
    g1_hbm,
    s1_hbm,
    g2_hbm,
    s2_hbm,
    ids_hbm,
    slots_hbm,
    off_hbm,
    field,
    mixed,
    terms_out,
    vectors,
    ids_ref,
    slots_ref,
    off_ref,
    noisy,
    cells,
    proj,
    k1,
    k2,
    wb1,
    wb2,
    id_rows,
    id_buf,
    id_recv,
    pcat,
    rows_out,
    rows_in,
    slot_row,
    sel,
    patch,
    partial,
    row_out,
    taps,
    lhs_col,
    lhs_tap_row,
    lhs_tap_col,
    edge_rows,
    noisy_col,
    wtap,
    rows_halo,
    x2,
    col_f,
    col_b,
    halo_b,
    halo_f,
    corner_out,
    corner_in,
    st_out,
    st_in,
    ld_sem,
    id_sem,
    row_sem,
    st_sem,
    halo_send,
    halo_recv,
):
    g, i, j = (lax.axis_index(a) for a in AXES)
    me = g * 32 + i * 4 + j

    loads = [
        pltpu.make_async_copy(a, b, ld_sem.at[n])
        for n, (a, b) in enumerate(
            [
                (cells_hbm, cells),
                (proj_hbm, proj),
                (k1_hbm, k1),
                (k2_hbm, k2),
                (noisy_hbm, noisy),
                (ids_hbm, ids_ref),
                (slots_hbm, slots_ref),
                (off_hbm, off_ref),
                (g1_hbm, vectors.at[0]),
                (s1_hbm, vectors.at[1]),
                (g2_hbm, vectors.at[2]),
                (s2_hbm, vectors.at[3]),
            ]
        )
    ]
    loads[5].start()
    barrier = pltpu.get_barrier_semaphore()

    def greet(n, c):
        pl.semaphore_signal(barrier, inc=1, device_id=me ^ far_first(n), device_id_type=FLAT)
        return c

    lax.fori_loop(0, 126, greet, 0, unroll=18)
    greet(126, 0)
    for c in loads[:5] + loads[6:]:
        c.start()
    loads[5].wait()

    id_rows[...] = jnp.zeros_like(id_rows)
    id_rows[0:MOST, :] = ids_ref[:, 0, :].astype(F32)
    id_buf[:, 0, :] = jnp.transpose(id_rows[...])
    id_recv[0] = id_buf[me]
    pl.semaphore_wait(barrier, 127)

    def send_ids(n, c):
        k = far_first(n)
        pltpu.make_async_remote_copy(
            id_buf.at[me ^ k], id_recv.at[k], id_sem.at[0], id_sem.at[1], device_id=me ^ k, device_id_type=FLAT
        ).start()
        return c

    lax.fori_loop(0, 126, send_ids, 0, unroll=18)
    send_ids(126, 0)

    for n in (0, 1, 6, 7, 8, 9, 10, 11):
        loads[n].wait()
    projected = jnp.dot(
        cells[...], proj[...], precision=lax.Precision.HIGHEST, preferred_element_type=F32
    )
    for n, term in enumerate(split2(projected)):
        pcat[:, n * 128 : (n + 1) * 128] = term
    for b in range(PATCH, 16):
        for n in range(3):
            taps[pl.ds(n * 16 + b, 128, stride=48), :] = jnp.zeros((128, 128), F32)

    slot_row[...] = jnp.full_like(slot_row, -1)
    slot_row[0:1, 0 : PATCH * PATCH] = slots_ref[...]
    slot = slot_row[0:1, :]
    owner = (slot * 10923) >> 16
    place = slot - owner * MOST
    index = place * 128 + (owner ^ me)
    index = jnp.where(slot < 0, -1, index).astype(F32)
    index = jnp.transpose(jnp.broadcast_to(index, (128, 256)))
    lane = lax.broadcasted_iota(jnp.int32, (256, 128), 1).astype(F32)
    for n in range(MOST):
        sel[:, n * 128 : (n + 1) * 128] = jnp.where(index == lane + 128.0 * n, 1.0, 0.0).astype(BF16)

    r_iota = lax.broadcasted_iota(jnp.int32, (128, 128), 0)
    l_iota = lax.broadcasted_iota(jnp.int32, (128, 128), 1)
    column = (r_iota % 16) * 8 + r_iota // 16
    lhs_col[:, 0:128] = weight_terms(column, l_iota, off_ref[0, 1]).astype(BF16)
    lhs_col[:, 128:256] = jnp.where(column == l_iota, 1.0, 0.0).astype(BF16)
    lhs_row = weight_terms(r_iota, l_iota, off_ref[0, 0]).astype(BF16)
    r_tap = lax.broadcasted_iota(jnp.int32, (128, 144), 0)
    l_tap = lax.broadcasted_iota(jnp.int32, (128, 144), 1)
    lhs_tap_row[...] = tap_terms(r_tap, l_tap, off_ref[0, 0]).astype(BF16)
    lhs_tap_col[...] = tap_terms((r_tap % 16) * 8 + r_tap // 16, l_tap, off_ref[0, 1]).astype(BF16)
    e_row = lax.broadcasted_iota(jnp.int32, (64, 256), 0)
    p_cell = lax.broadcasted_iota(jnp.int32, (64, 256), 1)
    p_row = (p_cell * 5042) >> 16
    p_col = p_cell - p_row * PATCH
    on_rows = e_row < 32
    point = jnp.where((e_row & 16) == 0, 0, TILE - 1)
    start = jnp.where(on_rows, off_ref[0, 0], off_ref[0, 1])
    position = (start.astype(F32) + point.astype(F32) * STEP) / 128.0 + 1.0
    weight = cubic(jnp.abs(position - jnp.where(on_rows, p_row, p_col).astype(F32)))
    keep = (jnp.where(on_rows, p_col, p_row) == (e_row & 15)) & (p_cell < PATCH * PATCH)
    edge_terms = jnp.concatenate(split2(jnp.where(keep, weight, 0.0)), axis=0)
    edge_rows[...] = jnp.dot(edge_terms, sel[...], preferred_element_type=F32).astype(BF16)

    loads[2].wait()
    zero_block = jnp.zeros((128, 128), BF16)

    def two_rows(w, wb):
        for a in range(4):
            for b in range(3):
                for e in range(2):
                    block = w[a - e, b] if 0 <= a - e <= 2 else zero_block
                    wb[(a * 3 + b) * 128 : (a * 3 + b + 1) * 128, e * 128 : (e + 1) * 128] = block

    two_rows(k1, wb1)
    for a in range(3):
        for b in range(3):
            n = a * 3 + b
            wtap[0:128, n * 128 : (n + 1) * 128] = k1[a, b]
            wtap[128:256, n * 128 : (n + 1) * 128] = k1[a, b]

    sub = lax.broadcasted_iota(jnp.int32, (16, 128), 0)
    x2[0] = jnp.zeros((160, 128), BF16)
    x2[TILE + 1] = jnp.zeros((160, 128), BF16)
    loads[4].wait()

    def reorder(n, c):
        h0 = n * 16
        got = jnp.dot(
            lhs_col[:, 128:256],
            jnp.concatenate([noisy[h0 + q] for q in range(16)], axis=1),
            preferred_element_type=F32,
        )
        for q in range(16):
            v = got[:, q * 128 : (q + 1) * 128]
            h = h0 + q
            x2[h + 1, 16:144] = v.astype(BF16)
            x2[h + 1, 0:16] = jnp.where(sub == 0, 0.0, pltpu.roll(v[112:128], 1, 0)).astype(BF16)
            x2[h + 1, 144:160] = jnp.where(sub == 15, 0.0, pltpu.roll(v[0:16], 15, 0)).astype(BF16)
            noisy_col[0, pl.ds(h, 1), :] = v[0:1]
            noisy_col[1, pl.ds(h, 1), :] = v[127:128]
        return c

    lax.fori_loop(0, 8, reorder, 0)

    def conv_block(x, wb, t, pairs=PAIRS):
        y = t * (2 * pairs)
        lhs = []
        for q in range(pairs):
            parts = [
                x[y + 2 * q + a, b * 16 : b * 16 + 128] for a in range(4) for b in range(3)
            ]
            lhs.append(jnp.concatenate(parts, axis=1))
        got = jnp.dot(jnp.concatenate(lhs, axis=0), wb[...], preferred_element_type=F32)
        for q in range(pairs):
            for e in range(2):
                yield y + 2 * q + e, got[q * 128 : (q + 1) * 128, e * 128 : (e + 1) * 128]

    def at_row(h):
        return pl.ds(pl.multiple_of(h * 128, 128), 128)

    def conv_noisy(t, c):
        for h, v in conv_block(x2, wb1, t, 32):
            field[at_row(h), :] = v
        return c

    def whole(ref, sem):
        return pltpu.make_async_copy(ref, ref, sem)

    whole(id_recv.at[pl.ds(1, 127)], id_sem.at[1]).wait()
    asked = id_recv[:, 0, :] - (me * HELD).astype(F32)
    row_iota = lax.broadcasted_iota(jnp.int32, (128, HELD), 1).astype(F32)
    hot = [
        jnp.where(asked[:, m : m + 1] == row_iota, 1.0, 0.0).astype(BF16) for m in range(MOST)
    ]
    found = jnp.dot(jnp.concatenate(hot, axis=0), pcat[...], preferred_element_type=F32)
    found = found[:, 0:128] + found[:, 128:256]
    for m in range(MOST):
        rows_out[:, m, :] = found[m * 128 : (m + 1) * 128]
    rows_in[0] = rows_out[0]

    def send_rows(n, c):
        k = far_first(n)
        pltpu.make_async_remote_copy(
            rows_out.at[k],
            rows_in.at[k],
            row_sem.at[0],
            row_sem.at[1],
            device_id=me ^ k,
            device_id_type=FLAT,
        ).start()
        return c

    lax.fori_loop(0, 126, send_rows, 0, unroll=18)
    send_rows(126, 0)
    lax.fori_loop(0, 2, conv_noisy, 0)
    whole(id_buf.at[pl.ds(1, 127)], id_sem.at[0]).wait()
    whole(rows_in.at[pl.ds(1, 127)], row_sem.at[1]).wait()

    terms = [jnp.concatenate(split2(rows_in[:, m, :]), axis=1) for m in range(MOST)]
    terms = jnp.concatenate(terms, axis=0)
    zero_tile = jnp.zeros((32, 128), BF16)

    def stack_terms(x):
        hi, mid, lo = split3(x)
        return jnp.concatenate([hi, mid, lo, hi, mid, hi, zero_tile], axis=0)

    got = jnp.dot(edge_rows[...], terms, preferred_element_type=F32)
    got = got[:, 0:128] + got[:, 128:256]
    ends = got[0:64] + got[64:128]
    for side in range(2):
        h = side * (TILE - 1)
        rhs = jnp.concatenate([stack_terms(ends[side * 16 : side * 16 + 16]), noisy[h]], axis=0)
        row_out[side] = jnp.dot(lhs_col[...], rhs, preferred_element_type=F32).astype(BF16)
        rhs = stack_terms(ends[32 + side * 16 : 48 + side * 16])
        got = noisy_col[side] + jnp.dot(lhs_row, rhs, preferred_element_type=F32)
        col_b[side] = got.astype(BF16)
        col_f[side] = col_b[side].astype(F32)

    def form_mixed():
        for b in range(PATCH):
            rhs = stack_terms(patch[9, pl.ds(b, 16, stride=PATCH), :])
            partial[pl.ds(b, 128, stride=16), :] = jnp.dot(
                lhs_row, rhs, preferred_element_type=F32
            )

        def step(n, c):
            rhs = []
            for q in range(16):
                h = n * 16 + q
                t = stack_terms(partial[pl.ds(pl.multiple_of(h * 16, 16), 16), :])
                rhs.append(jnp.concatenate([t, noisy[h]], axis=0))
            got = jnp.dot(
                lhs_col[...], jnp.concatenate(rhs, axis=1), preferred_element_type=F32
            ).astype(BF16)
            for q in range(16):
                mixed[n * 16 + q] = got[:, q * 128 : (q + 1) * 128]
            return c

        lax.fori_loop(0, 8, step, 0)

    def neighbour(di, dj):
        return (g, (i + di + 8) % 8, (j + dj + 4) % 4)

    def row_copies(pairs, base):
        return [
            pltpu.make_async_remote_copy(
                src,
                dst,
                halo_send.at[base + n],
                halo_recv.at[base + n],
                device_id=neighbour(di, 0),
                device_id_type=MESH,
            )
            for n, ((src, dst), di) in enumerate(zip(pairs, (-1, 1)))
        ]

    def corner_copies(base):
        cs = []
        for n, (di, dj) in enumerate(((-1, -1), (-1, 1), (1, -1), (1, 1))):
            slot_n = base // 8 * 4 + n
            cs.append(
                pltpu.make_async_remote_copy(
                    corner_out.at[slot_n],
                    corner_in.at[slot_n],
                    halo_send.at[base + 4 + n],
                    halo_recv.at[base + 4 + n],
                    device_id=neighbour(di, dj),
                    device_id_type=MESH,
                )
            )
        return cs

    def col_copies(base):
        cs = []
        for n, dj in enumerate((-1, 1)):
            slot_n = base // 8 * 2 + n
            cs.append(
                pltpu.make_async_remote_copy(
                    col_b.at[slot_n],
                    halo_b.at[slot_n],
                    halo_send.at[base + 2 + n],
                    halo_recv.at[base + 2 + n],
                    device_id=neighbour(0, dj),
                    device_id_type=MESH,
                )
            )
        return cs

    def put_corners(base):
        s = base // 8 * 4
        for n, (side, h) in enumerate(((0, 0), (1, 0), (0, 127), (1, 127))):
            corner_out[s + n] = jnp.broadcast_to(col_f[side, h : h + 1, :], (8, 128))

    def put_columns(base):
        s = base // 8 * 2
        for side in range(2):
            col_b[s + side] = col_f[side].astype(BF16)

    left_ok = jnp.where(j > 0, 1.0, 0.0)
    right_ok = jnp.where(j < 3, 1.0, 0.0)
    up_ok = jnp.where(i > 0, 1.0, 0.0)
    down_ok = jnp.where(i < 7, 1.0, 0.0)

    def take_columns(base, copies):
        for c in copies:
            c.wait()
        s2 = base // 8 * 2
        halo_f[0, 8:136, :] = halo_b[s2 + 1].astype(F32) * left_ok
        halo_f[1, 8:136, :] = halo_b[s2 + 0].astype(F32) * right_ok

    def take_corners(base):
        s4 = base // 8 * 4
        halo_f[0, 0:8, :] = corner_in[s4 + 3] * (left_ok * up_ok)
        halo_f[1, 0:8, :] = corner_in[s4 + 2] * (right_ok * up_ok)
        halo_f[0, 136:144, :] = corner_in[s4 + 1] * (left_ok * down_ok)
        halo_f[1, 136:144, :] = corner_in[s4 + 0] * (right_ok * down_ok)

    put_corners(0)
    mid = pl.ds(16, 128)
    rows1 = row_copies(
        [(row_out.at[0], rows_halo.at[1, mid]), (row_out.at[1], rows_halo.at[0, mid])], 0
    ) + corner_copies(0)
    cols1 = col_copies(0)
    for c in rows1[2:] + rows1[:2] + cols1:
        c.start()

    cell = jnp.dot(sel[...], terms, preferred_element_type=F32)
    cell = cell[:, 0:128] + cell[:, 128:256]
    patch[9] = cell
    hi, low = split2(cell)
    tapped = jnp.dot(jnp.concatenate([hi, low], axis=1), wtap[...], preferred_element_type=F32)
    for n in range(9):
        patch[n] = tapped[:, n * 128 : (n + 1) * 128]
    for b in range(3):
        rhs = []
        for col in range(PATCH):
            parts = [
                patch[a * 3 + b, pl.ds(col, 16, stride=PATCH), :] for a in range(3)
            ]
            hi, low = split2(jnp.concatenate(parts, axis=0))
            rhs.append(jnp.concatenate([hi, low, hi], axis=0))
        got = jnp.dot(
            lhs_tap_row[...], jnp.concatenate(rhs, axis=1), preferred_element_type=F32
        )
        for col in range(PATCH):
            taps[pl.ds(b * 16 + col, 128, stride=48), :] = got[:, col * 128 : (col + 1) * 128]

    def sum_up(carry, v):
        total, square = carry
        v3 = v.reshape(v.shape[0] // 8, 8, 128)
        return total + jnp.sum(v3, axis=0), square + jnp.sum(v3 * v3, axis=0)

    def add_taps(n, carry):
        rhs = []
        for q in range(16):
            h = n * 16 + q
            hi, low = split2(taps[pl.ds(pl.multiple_of(h * 48, 16), 48), :])
            rhs.append(jnp.concatenate([hi, low, hi], axis=0))
        got = jnp.dot(
            lhs_tap_col[...], jnp.concatenate(rhs, axis=1), preferred_element_type=F32
        )
        for q in range(16):
            h = n * 16 + q
            v = field[at_row(h), :] + got[:, q * 128 : (q + 1) * 128]
            field[at_row(h), :] = v
            carry = sum_up(carry, v)
        return carry

    zero8 = jnp.zeros((8, 128), F32)
    sums = lax.fori_loop(0, 8, add_taps, (zero8, zero8))

    def correct(carry, place, delta):
        old = field[place, :]
        new = old + delta
        field[place, :] = new
        d3 = delta.reshape(16, 8, 128)
        q3 = (new * new - old * old).reshape(16, 8, 128)
        return carry[0] + jnp.sum(d3, axis=0), carry[1] + jnp.sum(q3, axis=0)

    def add_borders(base, rows, columns, k, carry):
        n = base // 8 * 2
        take_columns(base, columns)
        for c in rows:
            c.wait()
        take_corners(base)
        for side, ok in ((0, up_ok), (1, down_ok)):
            v = rows_halo[n + side, 16:144].astype(F32) * ok
            rows_halo[n + side, 16:144] = v.astype(BF16)
            last = pltpu.roll(v[112:128], 1, 0)
            rows_halo[n + side, 0:16] = jnp.where(sub == 0, 0.0, last).astype(BF16)
            first = pltpu.roll(v[0:16], 15, 0)
            rows_halo[n + side, 144:160] = jnp.where(sub == 15, 0.0, first).astype(BF16)
        for side in range(2):
            lhs = [halo_f[side, 7 + a : 135 + a, :].astype(BF16) for a in range(3)]
            rhs = jnp.concatenate([k[a, 2 * side] for a in range(3)], axis=0)
            delta = jnp.dot(jnp.concatenate(lhs, axis=1), rhs, preferred_element_type=F32)
            carry = correct(carry, pl.ds(side * 127, 128, stride=128), delta)
        for side in range(2):
            lhs = [rows_halo[n + side, b * 16 : b * 16 + 128] for b in range(3)]
            rhs = jnp.concatenate([k[2 * side, b] for b in range(3)], axis=0)
            delta = jnp.dot(jnp.concatenate(lhs, axis=1), rhs, preferred_element_type=F32)
            carry = correct(carry, pl.ds(side * 127 * 128, 128), delta)
        return carry

    loads[3].wait()
    two_rows(k2, wb2)
    for b in range(PATCH, 16):
        partial[pl.ds(b, 128, stride=16), :] = jnp.zeros((128, 128), F32)
    sums = add_borders(0, rows1, cols1, k1, sums)

    lane8 = lax.broadcasted_iota(jnp.int32, (8, 128), 1)
    odd = (lane8 & 1) == 1
    high = (lane8 & 2) == 2
    number = float(TILE * TILE * 32 * (C // GROUPS))

    def norm_terms(n, sums, gain, shift, meanwhile=None):
        total, square = (jnp.sum(s, axis=0, keepdims=True) for s in sums)
        sub8 = lax.broadcasted_iota(jnp.int32, (8, 128), 0)
        mine = jnp.where(sub8 == 0, total, jnp.where(sub8 == 1, square, 0.0))
        st_out[n] = mine
        st_in[n, 0] = mine
        def send(t, c):
            k = far_first(t)
            pltpu.make_async_remote_copy(
                st_out.at[n],
                st_in.at[n, k],
                st_sem.at[n, 0],
                st_sem.at[n, 1],
                device_id=me ^ k,
                device_id_type=FLAT,
            ).start()
            return c

        for t in range(96, 127):
            send(t, 0)
        if meanwhile is not None:
            meanwhile()
        whole(st_in.at[n, pl.ds(1, 31)], st_sem.at[n, 1]).wait()
        both = jnp.sum(st_in[n], axis=0)
        both = both + jnp.where(odd, pltpu.roll(both, 1, 1), pltpu.roll(both, 127, 1))
        both = both + jnp.where(high, pltpu.roll(both, 2, 1), pltpu.roll(both, 126, 1))
        mean = both[0:1] / number
        spread = both[1:2] / number - mean * mean
        scale = lax.rsqrt(spread + 1e-05) * gain
        whole(st_in.at[n, pl.ds(1, 31)], st_sem.at[n, 0]).wait()
        return scale, shift - mean * scale

    scale, offset = norm_terms(0, sums, vectors[0], vectors[1], form_mixed)

    def hide(place):
        return silu(field[place, :] * scale + offset)

    for side in range(2):
        col_b[2 + side] = hide(pl.ds(side * 127, 128, stride=128)).astype(BF16)
        col_f[side] = col_b[2 + side].astype(F32)
        row_out[2 + side] = hide(pl.ds(side * 127 * 128, 128)).astype(BF16)
    put_corners(8)
    rows2 = row_copies(
        [(row_out.at[2], rows_halo.at[3, mid]), (row_out.at[3], rows_halo.at[2, mid])], 8
    ) + corner_copies(8)
    cols2 = col_copies(8)
    for c in rows2[2:] + rows2[:2] + cols2:
        c.start()

    def hide_row(h):
        v = hide(pl.ds(h * 128, 128))
        x2[h + 1, 16:144] = v.astype(BF16)
        x2[h + 1, 0:16] = jnp.where(sub == 0, 0.0, pltpu.roll(v[112:128], 1, 0)).astype(BF16)
        x2[h + 1, 144:160] = jnp.where(sub == 15, 0.0, pltpu.roll(v[0:16], 15, 0)).astype(BF16)

    many = 2 * PAIRS
    for h in range(many + 1):
        hide_row(h)
    sums = (zero8, zero8)
    for t in range(TILE // many):
        for h in range((t + 1) * many + 1, min((t + 2) * many + 1, TILE)):
            hide_row(h)
        for h, v in conv_block(x2, wb2, t):
            field[pl.ds(h * 128, 128), :] = v
            sums = sum_up(sums, v)
    sums = add_borders(8, rows2, cols2, k2, sums)
    scale2, offset2 = norm_terms(1, sums, vectors[2], vectors[3])

    terms_out[0:1, :] = scale2
    terms_out[1:2, :] = offset2
    whole(rows_in.at[pl.ds(1, 127)], row_sem.at[0]).wait()


def result_kernel(field, mixed, terms, out_hbm, stage, swap, sem):
    scale = terms[0:1, :]
    offset = terms[1:2, :]

    def finish(n, c):
        for q in range(8):
            h = n * 8 + q
            v = silu(field[pl.ds(pl.multiple_of(h * 128, 128), 128), :] * scale + offset)
            v = mixed[h].astype(F32) + v
            for s in range(8):
                swap[q, pl.ds(s, 16, stride=8), :] = v[s * 16 : (s + 1) * 16]
        for q in range(8):
            stage[n * 8 + q] = swap[q].astype(BF16)
        rows = pl.ds(n * 8, 8)
        pltpu.make_async_copy(stage.at[rows], out_hbm.at[rows], sem).start()
        return c

    lax.fori_loop(0, 16, finish, 0)
    pltpu.make_async_copy(stage, out_hbm, sem).wait()


def body(
    noisy_field,
    coarse_cells,
    coarse_proj,
    kernel_first,
    kernel_second,
    gain_first,
    shift_first,
    gain_second,
    shift_second,
    request_ids,
    patch_slots,
    tile_offsets,
):
    hbm = pl.BlockSpec(memory_space=pl.ANY)
    vmem = pl.BlockSpec(memory_space=pltpu.VMEM)
    row = lambda v: v.reshape(1, C)
    second, mixed, terms = pl.pallas_call(
        kernel,
        out_shape=[
            pltpu.VMEM((TILE * TILE, C), F32),
            pltpu.VMEM((TILE, TILE, C), BF16),
            pltpu.VMEM((8, C), F32),
        ],
        in_specs=[hbm] * 12,
        out_specs=[vmem] * 3,
        scratch_shapes=[
            pltpu.VMEM((4, 1, C), F32),
            pltpu.VMEM((MOST, 1, 128), jnp.int32),
            pltpu.VMEM((1, PATCH * PATCH), jnp.int32),
            pltpu.SMEM((1, 2), jnp.int32),
            pltpu.VMEM((TILE, TILE, C), BF16),
            pltpu.VMEM((HELD, CC), F32),
            pltpu.VMEM((CC, C), F32),
            pltpu.VMEM((3, 3, C, C), BF16),
            pltpu.VMEM((3, 3, C, C), BF16),
            pltpu.VMEM((12 * C, 2 * C), BF16),
            pltpu.VMEM((12 * C, 2 * C), BF16),
            pltpu.VMEM((128, 128), F32),
            pltpu.VMEM((128, 1, 128), F32),
            pltpu.VMEM((128, 1, 128), F32),
            pltpu.VMEM((HELD, 2 * C), BF16),
            pltpu.VMEM((128, MOST, C), F32),
            pltpu.VMEM((128, MOST, C), F32),
            pltpu.VMEM((8, 256), jnp.int32),
            pltpu.VMEM((256, MOST * 128), BF16),
            pltpu.VMEM((10, 256, C), F32),
            pltpu.VMEM((TILE * 16, C), F32),
            pltpu.VMEM((4, 128, C), BF16),
            pltpu.VMEM((TILE * 48, C), F32),
            pltpu.VMEM((128, 256), BF16),
            pltpu.VMEM((128, 144), BF16),
            pltpu.VMEM((128, 144), BF16),
            pltpu.VMEM((128, MOST * 128), BF16),
            pltpu.VMEM((2, 128, C), F32),
            pltpu.VMEM((256, 9 * C), BF16),
            pltpu.VMEM((4, 160, C), BF16),
            pltpu.VMEM((TILE + 2, 160, C), BF16),
            pltpu.VMEM((2, TILE, C), F32),
            pltpu.VMEM((4, TILE, C), BF16),
            pltpu.VMEM((4, TILE, C), BF16),
            pltpu.VMEM((2, 144, C), F32),
            pltpu.VMEM((8, 8, C), F32),
            pltpu.VMEM((8, 8, C), F32),
            pltpu.VMEM((2, 8, C), F32),
            pltpu.VMEM((2, 32, 8, C), F32),
            pltpu.SemaphoreType.DMA((12,)),
            pltpu.SemaphoreType.DMA((2,)),
            pltpu.SemaphoreType.DMA((2,)),
            pltpu.SemaphoreType.DMA((2, 2)),
            pltpu.SemaphoreType.DMA((16,)),
            pltpu.SemaphoreType.DMA((16,)),
        ],
        compiler_params=pltpu.CompilerParams(
            collective_id=0, has_side_effects=True, vmem_limit_bytes=50 << 20
        ),
        name="block",
    )(
        noisy_field.reshape(TILE, TILE, C),
        coarse_cells,
        coarse_proj,
        kernel_first,
        kernel_second,
        row(gain_first),
        row(shift_first),
        row(gain_second),
        row(shift_second),
        request_ids.transpose(0, 1, 4, 2, 3).reshape(MOST, 1, 128),
        patch_slots.reshape(1, PATCH * PATCH),
        tile_offsets.reshape(1, 2),
    )
    got = pl.pallas_call(
        result_kernel,
        out_shape=jax.ShapeDtypeStruct((TILE, TILE, C), BF16),
        in_specs=[vmem] * 3,
        out_specs=hbm,
        scratch_shapes=[
            pltpu.VMEM((TILE, TILE, C), BF16),
            pltpu.VMEM((8, TILE, C), F32),
            pltpu.SemaphoreType.DMA,
        ],
        compiler_params=pltpu.CompilerParams(vmem_limit_bytes=10 << 20),
        name="result",
    )(second, mixed, terms)
    return got[None]


def solution(mesh):
    return jax.shard_map(
        body,
        mesh=mesh,
        in_specs=(
            P("region", "row", "col", None),
            P(("region", "row", "col"), None),
            P(),
            P(),
            P(),
            P(),
            P(),
            P(),
            P(),
            P("region", "row", "col", None, None),
            P("region", "row", "col", None),
            P("region", "row", "col", None),
        ),
        out_specs=P("region", "row", "col", None),
        check_vma=False,
    )
```
